512 devices in a mesh: depth: 64 (over y, x, core), rows: 8 (over z).
Axes of the slice: x: 4, y: 8, z: 8, core: 2. Of those that a mesh axis runs over, the one named last changes fastest.
Arguments:
- substrate: float32 [256, 128, 1024], P('depth', 'rows'), may hold values from 0.2 to 1
- catalyst: float32 [256, 128, 1024], P('depth', 'rows'), may hold values from 0 to 0.5
- feed_rate: float32 [256, 128, 1024], P('depth', 'rows'), may hold values from 0.01 to 0.1
- kill_rate: float32 [256, 128, 1024], P('depth', 'rows'), may hold values from 0.03 to 0.1
- extinction: float32 [256, 128, 1024], P('depth', 'rows'), may hold values from 0.001 to 0.03
- palette: float32 [3, 3], replicated, may hold values from -2 to 2
Outputs:
- new_substrate: float32 [256, 128, 1024], P('depth', 'rows')
- new_catalyst: float32 [256, 128, 1024], P('depth', 'rows')
- image: float32 [4, 128, 1024], P(None, 'rows', 'depth')
The draws below stay inside these ranges and needn't reach their ends.
All inputs are finite; a program needn't handle non-finite values.
Results may differ from the reference program's by a relative error of at most 0.000039.
Values sent between devices are 32-bit elements; how exact they have to be, the bound alone decides.
A program may use at most 64 MiB of HBM per device.

```python
import math
import jax
import jax.numpy as jnp

COLS = 1024
STEPS = 2
DEPTH = 256
ROWS = 128


def level_of(own_key, extent, split, least, largest):
    level = 1.0
    for position, parts in split:
        heights = jax.random.uniform(jax.random.fold_in(jax.random.fold_in(own_key, 6), position), (parts,), jnp.float32, least / len(split), largest / len(split))
        level = level * jnp.repeat(jnp.exp(heights), extent[position] // parts).reshape((-1,) + (1,) * (len(extent) - 1 - position))
    return level


def setup_inputs(seed: int = 0) -> dict:
    seeds = jax.random.split(jax.random.key(seed), 7)
    substrate = jnp.clip(0.2 + 0.8 * jax.random.uniform(seeds[0], (DEPTH, ROWS, COLS), jnp.float32) ** level_of(seeds[0], (DEPTH, ROWS, COLS), ((0, 64), (1, 8)), -0.2, 0.2), 0.2, 1.0)
    catalyst = jnp.clip(0.5 * jax.random.uniform(seeds[1], (DEPTH, ROWS, COLS), jnp.float32) ** level_of(seeds[1], (DEPTH, ROWS, COLS), ((0, 64), (1, 8)), -0.2, 0.2), 0.0, 0.5)
    feed_rate = jnp.clip(jnp.exp(math.log(0.1) - 2.3025851 * jax.random.uniform(seeds[2], (DEPTH, ROWS, COLS), jnp.float32) ** level_of(seeds[2], (DEPTH, ROWS, COLS), ((0, 64), (1, 8)), -0.2, 0.2)), 0.01, 0.1)
    kill_rate = jnp.clip(jnp.exp(math.log(0.1) - 1.2039728 * jax.random.uniform(seeds[3], (DEPTH, ROWS, COLS), jnp.float32) ** level_of(seeds[3], (DEPTH, ROWS, COLS), ((0, 64), (1, 8)), -0.2, 0.2)), 0.03, 0.1)
    extinction = jnp.clip(jnp.exp(math.log(0.03) - 3.4011973 * jax.random.uniform(seeds[4], (DEPTH, ROWS, COLS), jnp.float32) ** level_of(seeds[4], (DEPTH, ROWS, COLS), ((0, 64), (1, 8)), -0.2, 0.2)), 0.001, 0.03)
    palette = jnp.clip(jax.random.uniform(seeds[5], (3, 3), jnp.float32, -2.0, 2.0), -2.0, 2.0)
    return dict(substrate=substrate, catalyst=catalyst, feed_rate=feed_rate, kill_rate=kill_rate, extinction=extinction, palette=palette)


diffusion_fast = 0.08
diffusion_slow = 0.04
time_step = 2.0


def react(padded, feed, kill):
    center = padded[:, 1:-1, 1:-1]
    column_pad = jnp.pad(center, ((0, 0), (0, 0), (0, 0), (1, 1)))
    laplace = padded[:, 2:, 1:-1] + padded[:, :-2, 1:-1] + padded[:, 1:-1, 2:] + padded[:, 1:-1, :-2]
    laplace = laplace + column_pad[..., 2:] + column_pad[..., :-2] - 6.0 * center
    fed = center[0]
    auto = center[1]
    reaction = fed * auto * auto
    fed_change = diffusion_fast * laplace[0] - reaction + feed * (1.0 - fed)
    auto_change = diffusion_slow * laplace[1] + reaction - (feed + kill) * auto
    return jnp.stack([fed + time_step * fed_change, auto + time_step * auto_change])


def shade(fields, extinction, palette):
    fed = fields[0]
    auto = fields[1]
    passing = jnp.exp(-extinction * (0.25 + 4.0 * auto * auto))
    opacity = 1.0 - passing
    colors = jax.nn.sigmoid(8.0 * palette[:, 0, None, None, None] * (fed - 0.65)[None]
                            + 8.0 * palette[:, 1, None, None, None] * (auto - 0.25)[None]
                            + palette[:, 2, None, None, None])
    return passing, opacity, colors


def reference(substrate, catalyst, feed_rate, kill_rate, extinction, palette):
    fields = jnp.stack([substrate, catalyst])
    for iteration in range(STEPS):
        padded = jnp.pad(fields, ((0, 0), (1, 1), (1, 1), (0, 0)))
        fields = react(padded, feed_rate, kill_rate)
    passing, opacity, colors = shade(fields, extinction, palette)
    cumul = jnp.cumprod(passing, axis=0)
    before = jnp.concatenate([jnp.ones_like(passing[:1]), cumul[:-1]], axis=0)
    weights = before * opacity
    image = jnp.stack([jnp.sum(weights * colors[0], axis=0), jnp.sum(weights * colors[1], axis=0),
                       jnp.sum(weights * colors[2], axis=0), jnp.sum(weights, axis=0)])
    return fields[0], fields[1], image
```

```python
import jax
import jax.numpy as jnp
from jax import lax
from jax.experimental import pallas as pl
from jax.experimental.pallas import tpu as pltpu
from jax.sharding import PartitionSpec as P

MESH = pl.DeviceIdType.MESH
X, Y = 4, 8
CHIPS = X * Y
DEPTHS = 2 * CHIPS
ZS = 8
CT = 8
LAYERS = 4
TILE = 32
COEF = (0.16, 0.08)
FIRST = 8


def expand(tile, lane):
    light = jnp.where(lane >= 96, tile, 0.0)
    light = light + pltpu.roll(light, 32, 1)
    return light + pltpu.roll(light, 64, 1)


def regroup(tiles, lane):
    tiles = list(tiles)
    for bit in (1, 2, 4):
        low_half = (lane & (16 * bit)) == 0
        for g in range(8):
            if g & bit:
                continue
            low, high = tiles[g], tiles[g | bit]
            tiles[g] = jnp.where(low_half, low, pltpu.roll(high, 16 * bit, 1))
            tiles[g | bit] = jnp.where(low_half, pltpu.roll(low, 128 - 16 * bit, 1), high)
    return tiles


def kernel(pal, S, C, F, K, E, out_s, out_c, img,
           s0, s1, fv, kv, ev, h0, ph, ps, r0, r1, rs0, rs1, dg, new, mid, t0, cr, x0, xr,
           load_sem, out_sem, h_send, h_recv, p_send, p_recv, r0_send, r0_recv, r1_send, r1_recv,
           g_send, g_recv, c_send, c_recv, x_send, x_recv, chain):
    d = lax.axis_index("depth")
    z = lax.axis_index("rows")
    core = d % 2
    x = (d // 2) % X
    y = d // (2 * X)
    chip = d // 2

    def at(yy, xx, cc):
        return (yy * X + xx) * 2 + cc

    has = {"lo": d > 0, "hi": d < DEPTHS - 1, "zlo": z > 0, "zhi": z < ZS - 1}
    up, down = jnp.minimum(d + 1, DEPTHS - 1), jnp.maximum(d - 1, 0)
    zup, zdown = jnp.minimum(z + 1, ZS - 1), jnp.maximum(z - 1, 0)
    x_ring = (at(y, (x + 1) % X, core), at(y, (x + X - 1) % X, core))
    y_ring = (at((y + 1) % Y, x, core), at((y + Y - 1) % Y, x, core))

    for ct in range(CT):
        for sp, src in ((0, S), (1, C)):
            pltpu.make_async_copy(
                src.at[:, :, pl.ds(ct * 128, 128)],
                s0.at[sp, :, pl.ds((ct + 1) * TILE + FIRST, 16), :],
                load_sem.at[sp],
            ).start()
    f_load = pltpu.make_async_copy(F, fv, load_sem.at[2])
    k_load = pltpu.make_async_copy(K, kv, load_sem.at[3])
    e_load = pltpu.make_async_copy(E, ev, load_sem.at[4])
    f_load.start()
    k_load.start()
    e_load.start()

    barrier = pltpu.get_barrier_semaphore()

    def signal(sem, depth, row):
        pl.semaphore_signal(sem, inc=1, device_id=(depth, row), device_id_type=MESH)

    for flag, depth, row in (("lo", down, z), ("hi", up, z), ("zlo", d, zdown), ("zhi", d, zup)):
        @pl.when(has[flag])
        def _(depth=depth, row=row):
            signal(barrier, depth, row)
    for depth in x_ring + y_ring:
        signal(barrier, depth, z)

    zero = jnp.zeros((8, 128), jnp.float32)
    for sp in range(2):
        for layer in range(LAYERS):
            for buf in (s0, s1):
                for t in (0, CT + 1):
                    for rb in range(2):
                        buf[sp, layer, pl.ds(t * TILE + FIRST + 8 * rb, 8), :] = zero
            for row in (FIRST - 1, FIRST + 16):
                s0[sp, layer, pl.ds(TILE + row, CT, stride=TILE), :] = zero
    for side, flag in ((0, "lo"), (1, "hi")):
        @pl.when(jnp.logical_not(has[flag]))
        def _(side=side):
            for sp in range(2):
                for rowside in range(2):
                    dg[side, rowside, sp] = zero

                def fill(i, carry):
                    h0[side, sp, :, pl.ds(i * 128, 128)] = jnp.zeros((16, 128), jnp.float32)
                    ph[side, sp, pl.ds(i * 16, 16), :] = jnp.zeros((16, 128), jnp.float32)
                    return carry

                lax.fori_loop(0, CT, fill, 0)
    for side, flag in ((0, "zlo"), (1, "zhi")):
        @pl.when(jnp.logical_not(has[flag]))
        def _(side=side):
            for sp in range(2):
                for layer in range(LAYERS):
                    r0[side, sp, layer] = zero
                    r1[side, sp, layer] = zero

    neighbours = 4 + sum(jnp.where(has[flag], 1, 0) for flag in has)
    pl.semaphore_wait(barrier, neighbours)

    def remote(src, dst, send, recv, depth, row):
        return pltpu.make_async_remote_copy(
            src_ref=src, dst_ref=dst, send_sem=send, recv_sem=recv,
            device_id=(depth, row), device_id_type=MESH)

    def depth_copy(kind, side, sp):
        target = up if side == 0 else down
        if kind == "h":
            src = (S, C)[sp].at[LAYERS - 1 if side == 0 else 0]
            return remote(src, h0.at[side, sp], h_send.at[side, sp], h_recv.at[side, sp], target, z)
        if kind == "p":
            return remote(ps.at[side, sp], ph.at[side, sp], p_send.at[side, sp], p_recv.at[side, sp], target, z)
        rowside = int(kind)
        return remote(r0.at[rowside, sp, LAYERS - 1 if side == 0 else 0], dg.at[side, rowside, sp],
                      g_send.at[side, rowside, sp], g_recv.at[side, rowside, sp], target, z)

    def row_copy(kind, side, sp):
        target = zup if side == 0 else zdown
        if kind == "0":
            return remote(rs0.at[side, sp], r0.at[side, sp], r0_send.at[side, sp], r0_recv.at[side, sp], d, target)
        return remote(rs1.at[side, sp], r1.at[side, sp], r1_send.at[side, sp], r1_recv.at[side, sp], d, target)

    to = ("hi", "lo")
    source = ("lo", "hi")
    zto = ("zhi", "zlo")
    zsource = ("zlo", "zhi")

    def each(flag, copies, what):
        @pl.when(has[flag])
        def _():
            for copy in copies:
                getattr(copy, what)()

    for side in range(2):
        each(to[side], [depth_copy("h", side, sp) for sp in range(2)], "start")

    def ring_round(k, ring):
        for depth in ring:
            signal(chain.at[k], depth, z)

    ring_round(0, x_ring)

    for sp in range(2):
        whole = s0.at[sp, :, pl.ds(0, CT * 16), :]
        pltpu.make_async_copy(whole, whole, load_sem.at[sp]).wait()
    for side in range(2):
        row = TILE + FIRST + (15 if side == 0 else 0)
        for sp in range(2):
            for layer in range(LAYERS):
                rs0[side, sp, layer] = s0[sp, layer, pl.ds(row, CT, stride=TILE), :]
        each(zto[side], [row_copy("0", side, sp) for sp in range(2)], "start")

    f_load.wait()
    k_load.wait()

    lane = lax.broadcasted_iota(jnp.int32, (8, 128), 1)

    def start_of(ct, rb):
        return pl.multiple_of((ct + 1) * TILE + FIRST + 8 * rb, 8)

    def centre(buf, sp, layer, ct, rb):
        return buf[sp, layer, pl.ds(start_of(ct, rb), 8), :]

    def around(buf, sp, layer, ct, rb):
        here = centre(buf, sp, layer, ct, rb)
        left = centre(buf, sp, layer, ct - 1, rb)
        right = centre(buf, sp, layer, ct + 1, rb)
        total = pltpu.roll(jnp.where(lane == 127, left, here), 1, 1)
        total += pltpu.roll(jnp.where(lane == 0, right, here), 127, 1)
        base = start_of(ct, rb)
        total += buf[sp, layer, pl.ds(base - 1, 8), :]
        total += buf[sp, layer, pl.ds(base + 1, 8), :]
        return here, total

    def native(ref, layer, ct, rb):
        return ref[layer, pl.ds(8 * rb, 8), pl.ds(pl.multiple_of(ct * 128, 128), 128)]

    def react(s, c, around_s, around_c, layer, ct, rb):
        feed = native(fv, layer, ct, rb)
        kill = native(kv, layer, ct, rb)
        feed = feed + feed
        reaction = s * c * c
        reaction = reaction + reaction
        new_s = COEF[0] * around_s + (feed + s * (0.04 - feed)) - reaction
        new_c = COEF[1] * around_c + c * (0.52 - feed - (kill + kill)) + reaction
        return new_s, new_c

    def first(layers):
        def body(ct, carry):
            for layer in layers:
                for rb in range(2):
                    values = []
                    for sp in range(2):
                        here, total = around(s0, sp, layer, ct, rb)
                        if layer > 0:
                            total += centre(s0, sp, layer - 1, ct, rb)
                        if layer < LAYERS - 1:
                            total += centre(s0, sp, layer + 1, ct, rb)
                        values.append((here, total))
                    result = react(values[0][0], values[1][0], values[0][1], values[1][1], layer, ct, rb)
                    for sp in range(2):
                        s1[sp, layer, pl.ds(start_of(ct, rb), 8), :] = result[sp]
                        if layer == LAYERS - 1:
                            ps[0, sp, pl.ds(pl.multiple_of(ct * 16 + 8 * rb, 8), 8), :] = result[sp]
                        if layer == 0:
                            ps[1, sp, pl.ds(pl.multiple_of(ct * 16 + 8 * rb, 8), 8), :] = result[sp]
            return carry

        lax.fori_loop(0, CT, body, 0)

    first((0, LAYERS - 1))
    for side in range(2):
        each(to[side], [depth_copy("p", side, sp) for sp in range(2)], "start")
    first(range(1, LAYERS - 1))
    for side in range(2):
        row = TILE + FIRST + (15 if side == 0 else 0)
        for sp in range(2):
            for layer in range(LAYERS):
                rs1[side, sp, layer] = s1[sp, layer, pl.ds(row, CT, stride=TILE), :]
        each(zto[side], [row_copy("1", side, sp) for sp in range(2)], "start")

    pl.semaphore_wait(chain.at[0], 2)
    ring_round(1, y_ring)

    for side in range(2):
        each(zsource[side], [row_copy("0", side, sp) for sp in range(2)], "wait_recv")
    for side in range(2):
        each(to[side], [depth_copy(str(rowside), side, sp) for rowside in range(2) for sp in range(2)], "start")

    pl.semaphore_wait(chain.at[1], 2)
    ring_round(2, y_ring)

    scale = {flag: jnp.where(has[flag], 1.0, 0.0).astype(jnp.float32) for flag in has}
    for side in range(2):
        row = TILE + FIRST + (0 if side == 0 else 15)
        for sp in range(2):
            for layer in range(LAYERS):
                where = pl.ds(row, CT, stride=TILE)
                s1[sp, layer, where, :] = s1[sp, layer, where, :] + COEF[sp] * r0[side, sp, layer]
    for side in range(2):
        each(zsource[side], [row_copy("1", side, sp) for sp in range(2)], "wait_recv")
    for side in range(2):
        edge = TILE + FIRST + (0 if side == 0 else 15)
        outside = TILE + FIRST + (-1 if side == 0 else 16)
        for sp in range(2):
            factor = COEF[sp] * scale[zsource[side]]
            for layer in range(LAYERS):
                s1[sp, layer, pl.ds(outside, CT, stride=TILE), :] = (
                    r1[side, sp, layer] + factor * s0[sp, layer, pl.ds(edge, CT, stride=TILE), :])
    pl.semaphore_wait(chain.at[2], 2)
    ring_round(3, y_ring)

    for side in range(2):
        each(source[side], [depth_copy("h", side, sp) for sp in range(2)], "wait_recv")

    def add_layers(ct, carry):
        for side, layer in ((0, 0), (1, LAYERS - 1)):
            for sp in range(2):
                for rb in range(2):
                    where = pl.ds(start_of(ct, rb), 8)
                    halo = h0[side, sp, pl.ds(8 * rb, 8), pl.ds(pl.multiple_of(ct * 128, 128), 128)]
                    s1[sp, layer, where, :] = s1[sp, layer, where, :] + COEF[sp] * halo
        return carry

    lax.fori_loop(0, CT, add_layers, 0)
    pl.semaphore_wait(chain.at[3], 2)
    ring_round(4, y_ring)

    e_load.wait()
    weights = []
    for k in range(3):
        a, b = -8.0 * pal[k, 0], -8.0 * pal[k, 1]
        weights.append((a, b, -pal[k, 2] - 0.65 * a - 0.25 * b))

    def second(layer, ct, rb):
        values = []
        for sp in range(2):
            here, total = around(s1, sp, layer, ct, rb)
            rows = pl.ds(pl.multiple_of(ct * 16 + 8 * rb, 8), 8)
            if layer > 0:
                total += centre(s1, sp, layer - 1, ct, rb)
            else:
                total += ph[0, sp, rows, :] + (COEF[sp] * scale["lo"]) * centre(s0, sp, 0, ct, rb)
            if layer < LAYERS - 1:
                total += centre(s1, sp, layer + 1, ct, rb)
            else:
                total += ph[1, sp, rows, :] + (COEF[sp] * scale["hi"]) * centre(s0, sp, LAYERS - 1, ct, rb)
            values.append((here, total))
        s, c = react(values[0][0], values[1][0], values[0][1], values[1][1], layer, ct, rb)
        columns = pl.ds(pl.multiple_of(ct * 128, 128), 128)
        new[0, layer, pl.ds(8 * rb, 8), columns] = s
        new[1, layer, pl.ds(8 * rb, 8), columns] = c
        passing = jnp.exp(-native(ev, layer, ct, rb) * (0.25 + 4.0 * c * c))
        opacity = 1.0 - passing
        colors = [opacity / (1.0 + jnp.exp(a * s + b * c + e)) for a, b, e in weights]
        return colors, passing

    def middle(ct, carry):
        for rb in range(2):
            rows = pl.ds(pl.multiple_of(ct * 16 + 8 * rb, 8), 8)
            near, light = second(1, ct, rb)
            far, light_far = second(2, ct, rb)
            for k in range(3):
                mid[k, rows, :] = near[k] + light * far[k]
            mid[3, rows, :] = light * light_far
        return carry

    lax.fori_loop(0, CT, middle, 0)
    pl.semaphore_wait(chain.at[4], 2)

    for side in range(2):
        each(source[side], [depth_copy(str(rowside), side, sp) for rowside in range(2) for sp in range(2)], "wait_recv")
    for rowside in range(2):
        outside = TILE + FIRST + (-1 if rowside == 0 else 16)
        for sp in range(2):
            factor = COEF[sp] * scale[zsource[rowside]]
            for side, layer in ((0, 0), (1, LAYERS - 1)):
                where = pl.ds(outside, CT, stride=TILE)
                s1[sp, layer, where, :] = s1[sp, layer, where, :] + factor * dg[side, rowside, sp]
    for side in range(2):
        each(source[side], [depth_copy("p", side, sp) for sp in range(2)], "wait_recv")
    for rowside in range(2):
        for sp in range(2):
            for side in range(2):
                factor = COEF[sp] * scale[source[side]]
                where = pl.ds(0 if rowside == 0 else 15, CT, stride=16)
                ph[side, sp, where, :] = ph[side, sp, where, :] + factor * dg[side, rowside, sp]

    partner = d + 1 - 2 * core

    def core_copy(ct):
        some = pl.ds(ct * X, X)
        return remote(t0.at[1 - core, some], cr.at[some], c_send.at[ct], c_recv.at[ct], partner, z)

    def ends(ct, carry):
        tiles = [None] * 8
        for rb in range(2):
            rows = pl.ds(pl.multiple_of(ct * 16 + 8 * rb, 8), 8)
            near, light = second(0, ct, rb)
            far, light_far = second(LAYERS - 1, ct, rb)
            light_mid = light * mid[3, rows, :]
            for k in range(3):
                tiles[2 * k + rb] = near[k] + light * mid[k, rows, :] + light_mid * far[k]
            tiles[6 + rb] = light_mid * light_far
        for j, tile in enumerate(regroup(tiles, lane)):
            t0[j % 2, ct * X + j // 2] = tile
        core_copy(ct).start()
        return carry

    lax.fori_loop(0, CT, ends, 0)

    out_copies = [pltpu.make_async_copy(new.at[0], out_s, out_sem.at[0]),
                  pltpu.make_async_copy(new.at[1], out_c, out_sem.at[1])]
    for copy in out_copies:
        copy.start()

    def chip_copy(i):
        return remote(x0.at[i], xr.at[chip], x_send, x_recv, 2 * i + core, z)

    def merge(ct, carry):
        core_copy(ct).wait_recv()
        for xx in range(X):
            i = ct * X + xx
            mine, other = t0[core, i], cr[i]
            near = jnp.where(core == 0, mine, other)
            far = jnp.where(core == 0, other, mine)
            both = jnp.where(lane < 96, near, 0.0) + expand(near, lane) * far
            x0[i] = both

            @pl.when(i == chip)
            def _(i=i, both=both):
                xr[i] = both

            @pl.when(i != chip)
            def _(i=i):
                chip_copy(i).start()
        return carry

    lax.fori_loop(0, CT, merge, 0)
    arrived = xr.at[pl.ds(0, CHIPS - 1)]
    pltpu.make_async_copy(arrived, arrived, x_recv).wait()

    def compose(i, carry):
        total, light = carry
        tile = xr[i]
        return total + light * jnp.where(lane < 96, tile, 0.0), light * expand(tile, lane)

    total, light = lax.fori_loop(
        0, CHIPS, compose, (jnp.zeros((8, 128), jnp.float32), jnp.ones((8, 128), jnp.float32)), unroll=8)
    tile = jnp.where(lane < 96, total, 1.0 - light)
    for g in range(8):
        part = tile if g == 0 else pltpu.roll(tile, 128 - 16 * g, 1)
        img[g // 2, pl.ds(8 * (g % 2), 8), :] = part[:, :16]

    for side in range(2):
        each(to[side], [depth_copy(kind, side, sp) for kind in ("h", "p", "0", "1") for sp in range(2)], "wait_send")
        each(zto[side], [row_copy(kind, side, sp) for kind in ("0", "1") for sp in range(2)], "wait_send")
    lax.fori_loop(0, CT, lambda ct, carry: (core_copy(ct).wait_send(), carry)[1], 0)
    pltpu.make_async_copy(arrived, arrived, x_send).wait()
    for copy in out_copies:
        copy.wait()


def body(substrate, catalyst, feed_rate, kill_rate, extinction, palette):
    field = jax.ShapeDtypeStruct(substrate.shape, jnp.float32)
    any_ref = pl.BlockSpec(memory_space=pl.ANY)
    f32 = jnp.float32
    dma = pltpu.SemaphoreType.DMA
    return pl.pallas_call(
        kernel,
        out_shape=(field, field, jax.ShapeDtypeStruct((4, 16, 16), f32)),
        in_specs=[pl.BlockSpec(memory_space=pltpu.SMEM)] + [any_ref] * 5,
        out_specs=(any_ref, any_ref, pl.BlockSpec(memory_space=pltpu.VMEM)),
        scratch_shapes=[
            pltpu.VMEM((2, LAYERS, (CT + 2) * TILE, 128), f32),
            pltpu.VMEM((2, LAYERS, (CT + 2) * TILE, 128), f32),
            pltpu.VMEM((LAYERS, 16, CT * 128), f32),
            pltpu.VMEM((LAYERS, 16, CT * 128), f32),
            pltpu.VMEM((LAYERS, 16, CT * 128), f32),
            pltpu.VMEM((2, 2, 16, CT * 128), f32),
            pltpu.VMEM((2, 2, CT * 16, 128), f32),
            pltpu.VMEM((2, 2, CT * 16, 128), f32),
            pltpu.VMEM((2, 2, LAYERS, CT, 128), f32),
            pltpu.VMEM((2, 2, LAYERS, CT, 128), f32),
            pltpu.VMEM((2, 2, LAYERS, CT, 128), f32),
            pltpu.VMEM((2, 2, LAYERS, CT, 128), f32),
            pltpu.VMEM((2, 2, 2, CT, 128), f32),
            pltpu.VMEM((2, LAYERS, 16, CT * 128), f32),
            pltpu.VMEM((4, CT * 16, 128), f32),
            pltpu.VMEM((2, CHIPS, 8, 128), f32),
            pltpu.VMEM((CHIPS, 8, 128), f32),
            pltpu.VMEM((CHIPS, 8, 128), f32),
            pltpu.VMEM((CHIPS, 8, 128), f32),
            dma((5,)), dma((2,)),
            dma((2, 2)), dma((2, 2)), dma((2, 2)), dma((2, 2)),
            dma((2, 2)), dma((2, 2)), dma((2, 2)), dma((2, 2)),
            dma((2, 2, 2)), dma((2, 2, 2)),
            dma((CT,)), dma((CT,)), dma, dma,
            pltpu.SemaphoreType.REGULAR((5,)),
        ],
        compiler_params=pltpu.CompilerParams(collective_id=0, has_side_effects=True),
    )(palette, substrate, catalyst, feed_rate, kill_rate, extinction)


def solution(mesh):
    split = P("depth", "rows", None)
    return jax.shard_map(
        body,
        mesh=mesh,
        in_specs=(split,) * 5 + (P(),),
        out_specs=(split, split, P(None, "rows", "depth")),
        check_vma=False,
    )
```

```python
import contextlib

import jax
import jax.numpy as jnp
from jax import lax
from jax.experimental import pallas as pl
from jax.experimental.pallas import tpu as pltpu
from jax.sharding import PartitionSpec as P

mark = contextlib.nullcontext
MESH = pl.DeviceIdType.MESH
X, Y = 4, 8
CHIPS = X * Y
DEPTHS = 2 * CHIPS
ZS = 8
CT = 8
LAYERS = 4
TILE = 32
COEF = (0.16, 0.08)
FIRST = 8
GROUP = 4
HALF = GROUP * X


def expand(tile, lane):
    light = jnp.where(lane >= 96, tile, 0.0)
    return light + pltpu.roll(light, 32, 1) + (pltpu.roll(light, 64, 1) + pltpu.roll(light, 96, 1))


def regroup(tiles, lane):
    tiles = list(tiles)
    for bit in (1, 2, 4):
        low_half = (lane & (16 * bit)) == 0
        for g in range(8):
            if g & bit:
                continue
            low, high = tiles[g], tiles[g | bit]
            tiles[g] = jnp.where(low_half, low, pltpu.roll(high, 16 * bit, 1))
            tiles[g | bit] = jnp.where(low_half, pltpu.roll(low, 128 - 16 * bit, 1), high)
    return tiles


def kernel(palette, S, C, F, K, E, new, xr,
           s0, s1, fv, kv, ev, h0, ph, ps, r0, r1, rs0, rs1, dg, mid, flat, t0, cr, x0, pal,
           load_sem, h_send, h_recv, p_send, p_recv, r0_send, r0_recv, r1_send, r1_recv,
           g_send, g_recv, c_send, c_recv, x_send, x_recv, chain):
    d = lax.axis_index("depth")
    z = lax.axis_index("rows")
    core = d & 1
    chip = d >> 1
    x = chip & (X - 1)
    y = chip >> 2

    def at(yy, xx, cc):
        return (yy * X + xx) * 2 + cc

    has = {"lo": d > 0, "hi": d < DEPTHS - 1, "zlo": z > 0, "zhi": z < ZS - 1}
    up, down = jnp.minimum(d + 1, DEPTHS - 1), jnp.maximum(d - 1, 0)
    zup, zdown = jnp.minimum(z + 1, ZS - 1), jnp.maximum(z - 1, 0)
    x_ring = (at(y, (x + 1) & (X - 1), core), at(y, (x + X - 1) & (X - 1), core))
    y_ring = (at((y + 1) & (Y - 1), x, core), at((y + Y - 1) & (Y - 1), x, core))

    barrier = pltpu.get_barrier_semaphore()

    def signal(sem, depth, row):
        pl.semaphore_signal(sem, inc=1, device_id=(depth, row), device_id_type=MESH)

    for flag, depth, row in (("lo", down, z), ("hi", up, z), ("zlo", d, zdown), ("zhi", d, zup)):
        @pl.when(has[flag])
        def _(depth=depth, row=row):
            signal(barrier, depth, row)
    for depth in x_ring + y_ring:
        signal(barrier, depth, z)

    for ct in range(CT):
        for sp, src in ((0, S), (1, C)):
            pltpu.make_async_copy(
                src.at[:, :, pl.ds(ct * 128, 128)],
                s0.at[sp, :, pl.ds((ct + 1) * TILE + FIRST, 16), :],
                load_sem.at[sp],
            ).start()
    pal_load = pltpu.make_async_copy(palette, pal, load_sem.at[5])
    f_load = pltpu.make_async_copy(F, fv, load_sem.at[2])
    k_load = pltpu.make_async_copy(K, kv, load_sem.at[3])
    e_load = pltpu.make_async_copy(E, ev, load_sem.at[4])
    f_load.start()
    k_load.start()
    e_load.start()
    pal_load.start()

    zero = jnp.zeros((8, 128), jnp.float32)
    for sp in range(2):
        for layer in range(LAYERS):
            for buf in (s0, s1):
                for t in (0, CT + 1):
                    for rb in range(2):
                        buf[sp, layer, pl.ds(t * TILE + FIRST + 8 * rb, 8), :] = zero
            for row in (FIRST - 1, FIRST + 16):
                s0[sp, layer, pl.ds(TILE + row, CT, stride=TILE), :] = zero
    for side, flag in ((0, "lo"), (1, "hi")):
        @pl.when(jnp.logical_not(has[flag]))
        def _(side=side):
            for sp in range(2):
                for rowside in range(2):
                    dg[side, rowside, sp] = zero

                def fill(i, carry):
                    h0[side, sp, :, pl.ds(i * 128, 128)] = jnp.zeros((16, 128), jnp.float32)
                    ph[side, sp, pl.ds(i * 16, 16), :] = jnp.zeros((16, 128), jnp.float32)
                    return carry

                lax.fori_loop(0, CT, fill, 0)
    for side, flag in ((0, "zlo"), (1, "zhi")):
        @pl.when(jnp.logical_not(has[flag]))
        def _(side=side):
            for sp in range(2):
                for layer in range(LAYERS):
                    r0[side, sp, layer] = zero
                    r1[side, sp, layer] = zero

    neighbours = 4 + sum(jnp.where(has[flag], 1, 0) for flag in has)
    with mark("w_barrier"):
        pl.semaphore_wait(barrier, neighbours)

    def remote(src, dst, send, recv, depth, row):
        return pltpu.make_async_remote_copy(
            src_ref=src, dst_ref=dst, send_sem=send, recv_sem=recv,
            device_id=(depth, row), device_id_type=MESH)

    def depth_copy(kind, side, sp):
        target = up if side == 0 else down
        if kind == "h":
            src = (S, C)[sp].at[LAYERS - 1 if side == 0 else 0]
            return remote(src, h0.at[side, sp], h_send.at[side, sp], h_recv.at[side, sp], target, z)
        if kind == "p":
            return remote(ps.at[side, sp], ph.at[side, sp], p_send.at[side, sp], p_recv.at[side, sp], target, z)
        rowside = int(kind)
        return remote(r0.at[rowside, sp, LAYERS - 1 if side == 0 else 0], dg.at[side, rowside, sp],
                      g_send.at[side, rowside, sp], g_recv.at[side, rowside, sp], target, z)

    def row_copy(kind, side, sp):
        target = zup if side == 0 else zdown
        if kind == "0":
            return remote(rs0.at[side, sp], r0.at[side, sp], r0_send.at[side, sp], r0_recv.at[side, sp], d, target)
        return remote(rs1.at[side, sp], r1.at[side, sp], r1_send.at[side, sp], r1_recv.at[side, sp], d, target)

    to = ("hi", "lo")
    source = ("lo", "hi")
    zto = ("zhi", "zlo")
    zsource = ("zlo", "zhi")

    def each(flag, copies, what):
        @pl.when(has[flag])
        def _():
            for copy in copies:
                getattr(copy, what)()

    for side in range(2):
        each(to[side], [depth_copy("h", side, sp) for sp in range(2)], "start")

    def ring_round(k, ring):
        for depth in ring:
            signal(chain.at[k], depth, z)

    ring_round(0, x_ring)

    with mark("w_load"):
        for sp in range(2):
            whole = s0.at[sp, :, pl.ds(0, CT * 16), :]
            pltpu.make_async_copy(whole, whole, load_sem.at[sp]).wait()
    for side in range(2):
        row = TILE + FIRST + (15 if side == 0 else 0)
        for sp in range(2):
            for layer in range(LAYERS):
                rs0[side, sp, layer] = s0[sp, layer, pl.ds(row, CT, stride=TILE), :]
        each(zto[side], [row_copy("0", side, sp) for sp in range(2)], "start")

    with mark("w_loadfk"):
        f_load.wait()
        k_load.wait()

    lane = lax.broadcasted_iota(jnp.int32, (8, 128), 1)

    def in_groups(step):
        def group(g, carry):
            for q in range(GROUP):
                step(g * GROUP + q, carry)
            return carry

        lax.fori_loop(0, CT // GROUP, group, 0)

    def start_of(ct, rb):
        return pl.multiple_of((ct + 1) * TILE + FIRST + 8 * rb, 8)

    def centre(buf, sp, layer, ct, rb):
        return buf[sp, layer, pl.ds(start_of(ct, rb), 8), :]

    def around(buf, sp, layer, ct, rb):
        here = centre(buf, sp, layer, ct, rb)
        left = centre(buf, sp, layer, ct - 1, rb)
        right = centre(buf, sp, layer, ct + 1, rb)
        total = pltpu.roll(jnp.where(lane == 127, left, here), 1, 1)
        total += pltpu.roll(jnp.where(lane == 0, right, here), 127, 1)
        base = start_of(ct, rb)
        total += buf[sp, layer, pl.ds(base - 1, 8), :]
        total += buf[sp, layer, pl.ds(base + 1, 8), :]
        return here, total

    def native(ref, layer, ct, rb):
        return ref[layer, pl.ds(8 * rb, 8), pl.ds(pl.multiple_of(ct * 128, 128), 128)]

    def react(s, c, around_s, around_c, layer, ct, rb):
        feed = native(fv, layer, ct, rb)
        kill = native(kv, layer, ct, rb)
        feed = feed + feed
        reaction = s * c * c
        reaction = reaction + reaction
        new_s = COEF[0] * around_s + (feed + s * (0.04 - feed)) - reaction
        new_c = COEF[1] * around_c + c * (0.52 - feed - (kill + kill)) + reaction
        return new_s, new_c

    def first(layers):
        def body(ct, carry):
            for layer in layers:
                for rb in range(2):
                    values = []
                    for sp in range(2):
                        here, total = around(s0, sp, layer, ct, rb)
                        if layer > 0:
                            total += centre(s0, sp, layer - 1, ct, rb)
                        if layer < LAYERS - 1:
                            total += centre(s0, sp, layer + 1, ct, rb)
                        values.append((here, total))
                    result = react(values[0][0], values[1][0], values[0][1], values[1][1], layer, ct, rb)
                    for sp in range(2):
                        s1[sp, layer, pl.ds(start_of(ct, rb), 8), :] = result[sp]
                        if layer == LAYERS - 1:
                            ps[0, sp, pl.ds(pl.multiple_of(ct * 16 + 8 * rb, 8), 8), :] = result[sp]
                        if layer == 0:
                            ps[1, sp, pl.ds(pl.multiple_of(ct * 16 + 8 * rb, 8), 8), :] = result[sp]
            return carry

        in_groups(body)

    with mark("first03"):
        first((0, LAYERS - 1))
    for side in range(2):
        each(to[side], [depth_copy("p", side, sp) for sp in range(2)], "start")
    with mark("w_chain0"):
        pl.semaphore_wait(chain.at[0], 2)
    ring_round(1, y_ring)
    with mark("first12"):
        first(range(1, LAYERS - 1))
    for side in range(2):
        row = TILE + FIRST + (15 if side == 0 else 0)
        for sp in range(2):
            for layer in range(LAYERS):
                rs1[side, sp, layer] = s1[sp, layer, pl.ds(row, CT, stride=TILE), :]
        each(zto[side], [row_copy("1", side, sp) for sp in range(2)], "start")


    with mark("w_chain1"):
        pl.semaphore_wait(chain.at[1], 2)
    ring_round(2, y_ring)
    with mark("w_row0"):
        for side in range(2):
            each(zsource[side], [row_copy("0", side, sp) for sp in range(2)], "wait_recv")
    for side in range(2):
        each(to[side], [depth_copy(str(rowside), side, sp) for rowside in range(2) for sp in range(2)], "start")


    with mark("w_chain2"):
        pl.semaphore_wait(chain.at[2], 2)
    ring_round(3, y_ring)
    scale = {flag: jnp.where(has[flag], 1.0, 0.0).astype(jnp.float32) for flag in has}
    for side in range(2):
        row = TILE + FIRST + (0 if side == 0 else 15)
        for sp in range(2):
            for layer in range(LAYERS):
                where = pl.ds(row, CT, stride=TILE)
                s1[sp, layer, where, :] = s1[sp, layer, where, :] + COEF[sp] * r0[side, sp, layer]
    with mark("w_row1"):
        for side in range(2):
            each(zsource[side], [row_copy("1", side, sp) for sp in range(2)], "wait_recv")
    for side in range(2):
        edge = TILE + FIRST + (0 if side == 0 else 15)
        outside = TILE + FIRST + (-1 if side == 0 else 16)
        for sp in range(2):
            factor = COEF[sp] * scale[zsource[side]]
            for layer in range(LAYERS):
                s1[sp, layer, pl.ds(outside, CT, stride=TILE), :] = (
                    r1[side, sp, layer] + factor * s0[sp, layer, pl.ds(edge, CT, stride=TILE), :])

    with mark("w_h"):
        for side in range(2):
            each(source[side], [depth_copy("h", side, sp) for sp in range(2)], "wait_recv")

    def add_layers(ct, carry):
        for side, layer in ((0, 0), (1, LAYERS - 1)):
            for sp in range(2):
                for rb in range(2):
                    where = pl.ds(start_of(ct, rb), 8)
                    halo = h0[side, sp, pl.ds(8 * rb, 8), pl.ds(pl.multiple_of(ct * 128, 128), 128)]
                    s1[sp, layer, where, :] = s1[sp, layer, where, :] + COEF[sp] * halo
        return carry

    with mark("w_chain3"):
        pl.semaphore_wait(chain.at[3], 2)
    ring_round(4, y_ring)
    with mark("addlayers"):
        in_groups(add_layers)

    e_load.wait()
    pal_load.wait()
    weights = []
    for k in range(3):
        a, b = -8.0 * pal[k, 0], -8.0 * pal[k, 1]
        weights.append((a, b, -pal[k, 2] - 0.65 * a - 0.25 * b))

    def second(layer, ct, rb):
        values = []
        for sp in range(2):
            here, total = around(s1, sp, layer, ct, rb)
            rows = pl.ds(pl.multiple_of(ct * 16 + 8 * rb, 8), 8)
            if layer > 0:
                total += centre(s1, sp, layer - 1, ct, rb)
            else:
                total += ph[0, sp, rows, :] + (COEF[sp] * scale["lo"]) * centre(s0, sp, 0, ct, rb)
            if layer < LAYERS - 1:
                total += centre(s1, sp, layer + 1, ct, rb)
            else:
                total += ph[1, sp, rows, :] + (COEF[sp] * scale["hi"]) * centre(s0, sp, LAYERS - 1, ct, rb)
            values.append((here, total))
        s, c = react(values[0][0], values[1][0], values[0][1], values[1][1], layer, ct, rb)
        columns = pl.ds(pl.multiple_of(ct * 128, 128), 128)
        new[0, layer, pl.ds(8 * rb, 8), columns] = s
        new[1, layer, pl.ds(8 * rb, 8), columns] = c
        passing = jnp.exp(-native(ev, layer, ct, rb) * (0.25 + 4.0 * c * c))
        opacity = 1.0 - passing
        colors = [opacity / (1.0 + jnp.exp(a * s + b * c + e)) for a, b, e in weights]
        return colors, passing

    def middle(ct, carry):
        for rb in range(2):
            rows = pl.ds(pl.multiple_of(ct * 16 + 8 * rb, 8), 8)
            near, light = second(1, ct, rb)
            far, light_far = second(2, ct, rb)
            for k in range(3):
                mid[k, rows, :] = near[k] + light * far[k]
            mid[3, rows, :] = light * light_far
        return carry

    with mark("middle"):
        in_groups(middle)

    with mark("w_diag"):
        for side in range(2):
            each(source[side], [depth_copy(str(rowside), side, sp) for rowside in range(2) for sp in range(2)], "wait_recv")
    for rowside in range(2):
        outside = TILE + FIRST + (-1 if rowside == 0 else 16)
        for sp in range(2):
            factor = COEF[sp] * scale[zsource[rowside]]
            for side, layer in ((0, 0), (1, LAYERS - 1)):
                where = pl.ds(outside, CT, stride=TILE)
                s1[sp, layer, where, :] = s1[sp, layer, where, :] + factor * dg[side, rowside, sp]
    with mark("w_p"):
        for side in range(2):
            each(source[side], [depth_copy("p", side, sp) for sp in range(2)], "wait_recv")
    for rowside in range(2):
        for sp in range(2):
            for side in range(2):
                factor = COEF[sp] * scale[source[side]]
                where = pl.ds(0 if rowside == 0 else 15, CT, stride=16)
                ph[side, sp, where, :] = ph[side, sp, where, :] + factor * dg[side, rowside, sp]

    partner = d + 1 - 2 * core

    def core_copy(g):
        some = pl.ds(g * HALF, HALF)
        return remote(t0.at[1 - core, some], cr.at[some], c_send.at[g], c_recv.at[g], partner, z)

    def ends(g, carry):
        for q in range(GROUP):
            ct = g * GROUP + q
            for rb in range(2):
                rows = pl.ds(pl.multiple_of(ct * 16 + 8 * rb, 8), 8)
                near, light = second(0, ct, rb)
                far, light_far = second(LAYERS - 1, ct, rb)
                light_mid = light * mid[3, rows, :]
                for k in range(3):
                    flat[ct * 8 + 2 * k + rb] = near[k] + light * mid[k, rows, :] + light_mid * far[k]
                flat[ct * 8 + 6 + rb] = light_mid * light_far
        for q in range(GROUP):
            ct = g * GROUP + q
            for j, tile in enumerate(regroup([flat[ct * 8 + i] for i in range(8)], lane)):
                t0[j % 2, ct * X + j // 2] = tile
        core_copy(g).start()
        return carry

    with mark("ends"):
        lax.fori_loop(0, CT // GROUP, ends, 0)

    def chip_copy(i):
        return remote(x0.at[i], xr.at[chip], x_send, x_recv, 2 * i + core, z)

    def merge(g, carry):
        core_copy(g).wait_recv()
        for q in range(HALF):
            i = g * HALF + q
            mine, other = t0[core, i], cr[i]
            near = jnp.where(core == 0, mine, other)
            far = jnp.where(core == 0, other, mine)
            x0[i] = jnp.where(lane < 96, near, 0.0) + expand(near, lane) * far
        for q in range(HALF):
            i = g * HALF + q

            @pl.when(i != chip)
            def _(i=i):
                chip_copy(i).start()
        return carry

    with mark("w_chain4"):
        pl.semaphore_wait(chain.at[4], 2)
    with mark("merge"):
        lax.fori_loop(0, CT // GROUP, merge, 0)
    xr[chip] = x0[chip]
    arrived = xr.at[pl.ds(0, CHIPS - 1)]
    with mark("w_xy"):
        pltpu.make_async_copy(arrived, arrived, x_recv).wait()

    for side in range(2):
        each(to[side], [depth_copy(kind, side, sp) for kind in ("h", "p", "0", "1") for sp in range(2)], "wait_send")
        each(zto[side], [row_copy(kind, side, sp) for kind in ("0", "1") for sp in range(2)], "wait_send")
    for g in range(CT // GROUP):
        core_copy(g).wait_send()
    pltpu.make_async_copy(arrived, arrived, x_send).wait()


def finish(new, xr, out_s, out_c, img, out_sem):
    copies = [pltpu.make_async_copy(new.at[0], out_s, out_sem.at[0]),
              pltpu.make_async_copy(new.at[1], out_c, out_sem.at[1])]
    for copy in copies:
        copy.start()
    lane = lax.broadcasted_iota(jnp.int32, (8, 128), 1)
    total, light = jnp.zeros((8, 128), jnp.float32), jnp.ones((8, 128), jnp.float32)
    for i in range(CHIPS):
        tile = xr[i]
        total += light * jnp.where(lane < 96, tile, 0.0)
        light *= expand(tile, lane)
    tile = jnp.where(lane < 96, total, 1.0 - light)
    for g in range(8):
        part = tile if g == 0 else pltpu.roll(tile, 128 - 16 * g, 1)
        img[g // 2, pl.ds(8 * (g % 2), 8), :] = part[:, :16]
    for copy in copies:
        copy.wait()


def body(substrate, catalyst, feed_rate, kill_rate, extinction, palette):
    field = jax.ShapeDtypeStruct(substrate.shape, jnp.float32)
    any_ref = pl.BlockSpec(memory_space=pl.ANY)
    f32 = jnp.float32
    dma = pltpu.SemaphoreType.DMA
    new, parts = pl.pallas_call(
        kernel,
        out_shape=(pltpu.VMEM((2,) + field.shape, f32), pltpu.VMEM((CHIPS, 8, 128), f32)),
        in_specs=[any_ref] * 6,
        out_specs=(pl.BlockSpec(memory_space=pltpu.VMEM),) * 2,
        scratch_shapes=[
            pltpu.VMEM((2, LAYERS, (CT + 2) * TILE, 128), f32),
            pltpu.VMEM((2, LAYERS, (CT + 2) * TILE, 128), f32),
            pltpu.VMEM((LAYERS, 16, CT * 128), f32),
            pltpu.VMEM((LAYERS, 16, CT * 128), f32),
            pltpu.VMEM((LAYERS, 16, CT * 128), f32),
            pltpu.VMEM((2, 2, 16, CT * 128), f32),
            pltpu.VMEM((2, 2, CT * 16, 128), f32),
            pltpu.VMEM((2, 2, CT * 16, 128), f32),
            pltpu.VMEM((2, 2, LAYERS, CT, 128), f32),
            pltpu.VMEM((2, 2, LAYERS, CT, 128), f32),
            pltpu.VMEM((2, 2, LAYERS, CT, 128), f32),
            pltpu.VMEM((2, 2, LAYERS, CT, 128), f32),
            pltpu.VMEM((2, 2, 2, CT, 128), f32),
            pltpu.VMEM((4, CT * 16, 128), f32),
            pltpu.VMEM((CT * 8, 8, 128), f32),
            pltpu.VMEM((2, CHIPS, 8, 128), f32),
            pltpu.VMEM((CHIPS, 8, 128), f32),
            pltpu.VMEM((CHIPS, 8, 128), f32),
            pltpu.SMEM((3, 3), f32),
            dma((6,)),
            dma((2, 2)), dma((2, 2)), dma((2, 2)), dma((2, 2)),
            dma((2, 2)), dma((2, 2)), dma((2, 2)), dma((2, 2)),
            dma((2, 2, 2)), dma((2, 2, 2)),
            dma((CT // GROUP,)), dma((CT // GROUP,)), dma, dma,
            pltpu.SemaphoreType.REGULAR((5,)),
        ],
        compiler_params=pltpu.CompilerParams(collective_id=0, has_side_effects=True),
    )(palette, substrate, catalyst, feed_rate, kill_rate, extinction)
    return pl.pallas_call(
        finish,
        out_shape=(field, field, jax.ShapeDtypeStruct((4, 16, 16), f32)),
        in_specs=[pl.BlockSpec(memory_space=pltpu.VMEM)] * 2,
        out_specs=(any_ref, any_ref, pl.BlockSpec(memory_space=pltpu.VMEM)),
        scratch_shapes=[dma((2,))],
    )(*(pltpu.with_memory_space_constraint(part, pltpu.VMEM) for part in (new, parts)))


def solution(mesh):
    split = P("depth", "rows", None)
    return jax.shard_map(
        body,
        mesh=mesh,
        in_specs=(split,) * 5 + (P(),),
        out_specs=(split, split, P(None, "rows", "depth")),
        check_vma=False,
    )
```

```python
import contextlib

import jax
import jax.numpy as jnp
from jax import lax
from jax.experimental import pallas as pl
from jax.experimental.pallas import tpu as pltpu
from jax.sharding import PartitionSpec as P

mark = contextlib.nullcontext
MESH = pl.DeviceIdType.MESH
X, Y = 4, 8
CHIPS = X * Y
DEPTHS = 2 * CHIPS
ZS = 8
CT = 8
LAYERS = 4
TILE = 32
COEF = (0.16, 0.08)
FIRST = 8
GROUP = 4
HALF = CT // 2


def expand(tile, lane):
    light = jnp.where(lane >= 96, tile, 0.0)
    return light + pltpu.roll(light, 32, 1) + (pltpu.roll(light, 64, 1) + pltpu.roll(light, 96, 1))


def regroup(tiles, lane):
    tiles = list(tiles)
    for bit in (1, 2, 4):
        low_half = (lane & (16 * bit)) == 0
        for g in range(8):
            if g & bit:
                continue
            low, high = tiles[g], tiles[g | bit]
            tiles[g] = jnp.where(low_half, low, pltpu.roll(high, 16 * bit, 1))
            tiles[g | bit] = jnp.where(low_half, pltpu.roll(low, 128 - 16 * bit, 1), high)
    return tiles


def kernel(palette, S, C, F, K, E, new, xr,
           s0, s1, fv, kv, ev, h0, ph, ps, r0, r1, rs0, rs1, dg, mid, flat, t0, cr, x0, pal,
           load_sem, h_send, h_recv, p_send, p_recv, r0_send, r0_recv, r1_send, r1_recv,
           g_send, g_recv, c_send, c_recv, x_send, x_recv, chain):
    d = lax.axis_index("depth")
    z = lax.axis_index("rows")
    core = d & 1
    chip = d >> 1
    x = chip & (X - 1)
    y = chip >> 2

    def at(yy, xx, cc):
        return (yy * X + xx) * 2 + cc

    has = {"lo": d > 0, "hi": d < DEPTHS - 1, "zlo": z > 0, "zhi": z < ZS - 1}
    up, down = jnp.minimum(d + 1, DEPTHS - 1), jnp.maximum(d - 1, 0)
    zup, zdown = jnp.minimum(z + 1, ZS - 1), jnp.maximum(z - 1, 0)
    x_ring = (at(y, (x + 1) & (X - 1), core), at(y, (x + X - 1) & (X - 1), core))
    y_ring = (at((y + 1) & (Y - 1), x, core), at((y + Y - 1) & (Y - 1), x, core))

    barrier = pltpu.get_barrier_semaphore()

    def signal(sem, depth, row):
        pl.semaphore_signal(sem, inc=1, device_id=(depth, row), device_id_type=MESH)

    for flag, depth, row in (("lo", down, z), ("hi", up, z), ("zlo", d, zdown), ("zhi", d, zup)):
        @pl.when(has[flag])
        def _(depth=depth, row=row):
            signal(barrier, depth, row)
    for depth in x_ring + y_ring:
        signal(barrier, depth, z)

    for ct in range(CT):
        for sp, src in ((0, S), (1, C)):
            pltpu.make_async_copy(
                src.at[:, :, pl.ds(ct * 128, 128)],
                s0.at[sp, :, pl.ds((ct + 1) * TILE + FIRST, 16), :],
                load_sem.at[sp],
            ).start()
    pal_load = pltpu.make_async_copy(palette, pal, load_sem.at[5])
    f_load = pltpu.make_async_copy(F, fv, load_sem.at[2])
    k_load = pltpu.make_async_copy(K, kv, load_sem.at[3])
    e_load = pltpu.make_async_copy(E, ev, load_sem.at[4])
    f_load.start()
    k_load.start()
    e_load.start()
    pal_load.start()

    zero = jnp.zeros((8, 128), jnp.float32)
    for sp in range(2):
        for layer in range(LAYERS):
            for buf in (s0, s1):
                for t in (0, CT + 1):
                    for rb in range(2):
                        buf[sp, layer, pl.ds(t * TILE + FIRST + 8 * rb, 8), :] = zero
            for row in (FIRST - 1, FIRST + 16):
                s0[sp, layer, pl.ds(TILE + row, CT, stride=TILE), :] = zero
    for side, flag in ((0, "lo"), (1, "hi")):
        @pl.when(jnp.logical_not(has[flag]))
        def _(side=side):
            for sp in range(2):
                for rowside in range(2):
                    dg[side, rowside, sp] = zero

                def fill(i, carry):
                    h0[side, sp, :, pl.ds(i * 128, 128)] = jnp.zeros((16, 128), jnp.float32)
                    ph[side, i // HALF, sp, pl.ds((i % HALF) * 16, 16), :] = jnp.zeros((16, 128), jnp.float32)
                    return carry

                lax.fori_loop(0, CT, fill, 0)
    for side, flag in ((0, "zlo"), (1, "zhi")):
        @pl.when(jnp.logical_not(has[flag]))
        def _(side=side):
            for sp in range(2):
                for layer in range(LAYERS):
                    r0[side, sp, layer] = zero
                    r1[side, sp, layer] = zero

    neighbours = 4 + sum(jnp.where(has[flag], 1, 0) for flag in has)
    with mark("w_barrier"):
        pl.semaphore_wait(barrier, neighbours)

    def remote(src, dst, send, recv, depth, row):
        return pltpu.make_async_remote_copy(
            src_ref=src, dst_ref=dst, send_sem=send, recv_sem=recv,
            device_id=(depth, row), device_id_type=MESH)

    def depth_copy(kind, side, sp):
        target = up if side == 0 else down
        if kind == "h":
            src = (S, C)[sp].at[LAYERS - 1 if side == 0 else 0]
            return remote(src, h0.at[side, sp], h_send.at[side, sp], h_recv.at[side, sp], target, z)
        if kind == "p":
            half = sp
            return remote(ps.at[side, half], ph.at[side, half], p_send.at[side, half], p_recv.at[side, half], target, z)
        rowside = int(kind)
        return remote(r0.at[rowside, sp, LAYERS - 1 if side == 0 else 0], dg.at[side, rowside, sp],
                      g_send.at[side, rowside, sp], g_recv.at[side, rowside, sp], target, z)

    def row_copy(kind, side, sp):
        target = zup if side == 0 else zdown
        if kind == "0":
            return remote(rs0.at[side, sp], r0.at[side, sp], r0_send.at[side, sp], r0_recv.at[side, sp], d, target)
        return remote(rs1.at[side, sp], r1.at[side, sp], r1_send.at[side, sp], r1_recv.at[side, sp], d, target)

    to = ("hi", "lo")
    source = ("lo", "hi")
    zto = ("zhi", "zlo")
    zsource = ("zlo", "zhi")

    def each(flag, copies, what):
        @pl.when(has[flag])
        def _():
            for copy in copies:
                getattr(copy, what)()

    for side in range(2):
        each(to[side], [depth_copy("h", side, sp) for sp in range(2)], "start")

    near_by = x_ring + y_ring
    two_off = [at((y + dy) & (Y - 1), (x + dx) & (X - 1), core)
               for dy, dx in ((2, 0), (6, 0), (0, 2), (1, 1), (1, 3), (7, 1), (7, 3))]

    def spread(k, depths):
        for depth in depths:
            signal(chain.at[k], depth, z)

    def heard(k, depths):
        with mark(f"w_chain{k}"):
            pl.semaphore_wait(chain.at[k], len(depths))

    spread(0, near_by)

    with mark("w_load"):
        for sp in range(2):
            whole = s0.at[sp, :, pl.ds(0, CT * 16), :]
            pltpu.make_async_copy(whole, whole, load_sem.at[sp]).wait()
    for side in range(2):
        row = TILE + FIRST + (15 if side == 0 else 0)
        for sp in range(2):
            for layer in range(LAYERS):
                rs0[side, sp, layer] = s0[sp, layer, pl.ds(row, CT, stride=TILE), :]
        each(zto[side], [row_copy("0", side, sp) for sp in range(2)], "start")

    with mark("w_loadfk"):
        f_load.wait()
        k_load.wait()

    lane = lax.broadcasted_iota(jnp.int32, (8, 128), 1)

    def in_groups(step):
        def group(g, carry):
            for q in range(GROUP):
                step(g * GROUP + q, carry)
            return carry

        lax.fori_loop(0, CT // GROUP, group, 0)

    def start_of(ct, rb):
        return pl.multiple_of((ct + 1) * TILE + FIRST + 8 * rb, 8)

    def centre(buf, sp, layer, ct, rb):
        return buf[sp, layer, pl.ds(start_of(ct, rb), 8), :]

    def around(buf, sp, layer, ct, rb):
        here = centre(buf, sp, layer, ct, rb)
        left = centre(buf, sp, layer, ct - 1, rb)
        right = centre(buf, sp, layer, ct + 1, rb)
        total = pltpu.roll(jnp.where(lane == 127, left, here), 1, 1)
        total += pltpu.roll(jnp.where(lane == 0, right, here), 127, 1)
        base = start_of(ct, rb)
        total += buf[sp, layer, pl.ds(base - 1, 8), :]
        total += buf[sp, layer, pl.ds(base + 1, 8), :]
        return here, total

    def native(ref, layer, ct, rb):
        return ref[layer, pl.ds(8 * rb, 8), pl.ds(pl.multiple_of(ct * 128, 128), 128)]

    def react(s, c, around_s, around_c, layer, ct, rb):
        feed = native(fv, layer, ct, rb)
        kill = native(kv, layer, ct, rb)
        feed = feed + feed
        reaction = s * c * c
        reaction = reaction + reaction
        new_s = COEF[0] * around_s + (feed + s * (0.04 - feed)) - reaction
        new_c = COEF[1] * around_c + c * (0.52 - feed - (kill + kill)) + reaction
        return new_s, new_c

    def first(layers):
        def body(ct, carry):
            for layer in layers:
                for rb in range(2):
                    values = []
                    for sp in range(2):
                        here, total = around(s0, sp, layer, ct, rb)
                        if layer > 0:
                            total += centre(s0, sp, layer - 1, ct, rb)
                        if layer < LAYERS - 1:
                            total += centre(s0, sp, layer + 1, ct, rb)
                        values.append((here, total))
                    result = react(values[0][0], values[1][0], values[0][1], values[1][1], layer, ct, rb)
                    for sp in range(2):
                        s1[sp, layer, pl.ds(start_of(ct, rb), 8), :] = result[sp]
                        for side, edge, target in ((0, LAYERS - 1, up), (1, 0, down)):
                            if layer == edge:
                                place = (ct - (target >> 3) + (Y - 2)) & (Y - 1)
                                rows = pl.multiple_of((place & (HALF - 1)) * 16 + 8 * rb, 8)
                                ps[side, place >> 2, sp, pl.ds(rows, 8), :] = result[sp]
            return carry

        in_groups(body)

    with mark("first03"):
        first((0, LAYERS - 1))
    for side in range(2):
        each(to[side], [depth_copy("p", side, 0)], "start")
    with mark("first12"):
        first(range(1, LAYERS - 1))
    for side in range(2):
        row = TILE + FIRST + (15 if side == 0 else 0)
        for sp in range(2):
            for layer in range(LAYERS):
                rs1[side, sp, layer] = s1[sp, layer, pl.ds(row, CT, stride=TILE), :]
        each(zto[side], [row_copy("1", side, sp) for sp in range(2)], "start")


    heard(0, near_by)
    spread(1, two_off)

    with mark("w_row0"):
        for side in range(2):
            each(zsource[side], [row_copy("0", side, sp) for sp in range(2)], "wait_recv")
    for side in range(2):
        each(to[side], [depth_copy(str(rowside), side, sp) for rowside in range(2) for sp in range(2)], "start")
    for side in range(2):
        each(to[side], [depth_copy("p", side, 1)], "start")


    scale = {flag: jnp.where(has[flag], 1.0, 0.0).astype(jnp.float32) for flag in has}
    for side in range(2):
        row = TILE + FIRST + (0 if side == 0 else 15)
        for sp in range(2):
            for layer in range(LAYERS):
                where = pl.ds(row, CT, stride=TILE)
                s1[sp, layer, where, :] = s1[sp, layer, where, :] + COEF[sp] * r0[side, sp, layer]
    with mark("w_row1"):
        for side in range(2):
            each(zsource[side], [row_copy("1", side, sp) for sp in range(2)], "wait_recv")
    for side in range(2):
        edge = TILE + FIRST + (0 if side == 0 else 15)
        outside = TILE + FIRST + (-1 if side == 0 else 16)
        for sp in range(2):
            factor = COEF[sp] * scale[zsource[side]]
            for layer in range(LAYERS):
                s1[sp, layer, pl.ds(outside, CT, stride=TILE), :] = (
                    r1[side, sp, layer] + factor * s0[sp, layer, pl.ds(edge, CT, stride=TILE), :])

    with mark("w_h"):
        for side in range(2):
            each(source[side], [depth_copy("h", side, sp) for sp in range(2)], "wait_recv")

    def add_layers(ct, carry):
        for side, layer in ((0, 0), (1, LAYERS - 1)):
            for sp in range(2):
                for rb in range(2):
                    where = pl.ds(start_of(ct, rb), 8)
                    halo = h0[side, sp, pl.ds(8 * rb, 8), pl.ds(pl.multiple_of(ct * 128, 128), 128)]
                    s1[sp, layer, where, :] = s1[sp, layer, where, :] + COEF[sp] * halo
        return carry

    with mark("addlayers"):
        in_groups(add_layers)

    heard(1, two_off)
    spread(2, two_off)
    e_load.wait()
    pal_load.wait()
    weights = []
    for k in range(3):
        a, b = -8.0 * pal[k, 0], -8.0 * pal[k, 1]
        weights.append((a, b, -pal[k, 2] - 0.65 * a - 0.25 * b))

    def columns_of(ct):
        return pl.ds(pl.multiple_of(ct * 128, 128), 128)

    def second(layer, ct, rb):
        values = []
        for sp in range(2):
            here, total = around(s1, sp, layer, ct, rb)
            if layer > 0:
                total += centre(s1, sp, layer - 1, ct, rb)
            else:
                total += (COEF[sp] * scale["lo"]) * centre(s0, sp, 0, ct, rb)
            if layer < LAYERS - 1:
                total += centre(s1, sp, layer + 1, ct, rb)
            else:
                total += (COEF[sp] * scale["hi"]) * centre(s0, sp, LAYERS - 1, ct, rb)
            values.append((here, total))
        return react(values[0][0], values[1][0], values[0][1], values[1][1], layer, ct, rb)

    def shade(s, c, layer, ct, rb):
        new[0, layer, pl.ds(8 * rb, 8), columns_of(ct)] = s
        new[1, layer, pl.ds(8 * rb, 8), columns_of(ct)] = c
        passing = jnp.exp(-native(ev, layer, ct, rb) * (0.25 + 4.0 * c * c))
        opacity = 1.0 - passing
        colors = [opacity / (1.0 + jnp.exp(a * s + b * c + e)) for a, b, e in weights]
        return colors, passing

    def middle(ct, carry):
        for rb in range(2):
            rows = pl.ds(pl.multiple_of(ct * 16 + 8 * rb, 8), 8)
            near, light = shade(*second(1, ct, rb), 1, ct, rb)
            far, light_far = shade(*second(2, ct, rb), 2, ct, rb)
            for k in range(3):
                mid[k, rows, :] = near[k] + light * far[k]
            mid[3, rows, :] = light * light_far
        return carry

    with mark("middle"):
        in_groups(middle)

    def open_ends(ct, carry):
        for layer in (0, LAYERS - 1):
            for rb in range(2):
                for sp, value in enumerate(second(layer, ct, rb)):
                    new[sp, layer, pl.ds(8 * rb, 8), columns_of(ct)] = value
        return carry

    with mark("open_ends"):
        in_groups(open_ends)

    with mark("w_diag"):
        for side in range(2):
            each(source[side], [depth_copy(str(rowside), side, sp) for rowside in range(2) for sp in range(2)], "wait_recv")
    corner = {}
    for side in range(2):
        for rowside in range(2):
            for sp in range(2):
                corner[side, rowside, sp] = pltpu.roll(dg[side, rowside, sp], (Y - 2 - y) & (Y - 1), 0) * (2.0 * COEF[sp])

    def add_corners(half):
        for (side, rowside, sp), rows in corner.items():
            where = pl.ds(15 * rowside, HALF, stride=16)
            ph[side, half, sp, where, :] = ph[side, half, sp, where, :] + rows[half * HALF:half * HALF + HALF]

    partner = d + 1 - 2 * core

    def core_copy(g):
        some = pl.ds(g * HALF * X, HALF * X)
        return remote(t0.at[1 - core, some], cr.at[some], c_send.at[g], c_recv.at[g], partner, z)

    def ends(g):
        with mark(f"w_p{g}"):
            for side in range(2):
                each(source[side], [depth_copy("p", side, g)], "wait_recv")
        add_corners(g)
        for q in range(HALF):
            place = g * HALF + q
            ct = (y + place + 2) & (Y - 1)
            for rb in range(2):
                parts = []
                for side, layer in ((0, 0), (1, LAYERS - 1)):
                    values = [new[sp, layer, pl.ds(8 * rb, 8), columns_of(ct)]
                              + COEF[sp] * ph[side, g, sp, pl.ds(q * 16 + 8 * rb, 8), :] for sp in range(2)]
                    parts.append(shade(*values, layer, ct, rb))
                (near, light), (far, light_far) = parts
                rows = pl.ds(pl.multiple_of(ct * 16 + 8 * rb, 8), 8)
                light_mid = light * mid[3, rows, :]
                for k in range(3):
                    flat[place * 8 + 2 * k + rb] = near[k] + light * mid[k, rows, :] + light_mid * far[k]
                flat[place * 8 + 6 + rb] = light_mid * light_far
        for place in range(g * HALF, g * HALF + HALF):
            for j, tile in enumerate(regroup([flat[place * 8 + i] for i in range(8)], lane)):
                t0[j % 2, place * X + j // 2] = tile
        core_copy(g).start()

    for g in range(2):
        with mark(f"ends{g}"):
            ends(g)

    def chip_copy(place, away, across):
        xx = (x + across) & (X - 1)
        return remote(x0.at[place * X + xx], xr.at[chip], x_send, x_recv, at((y + away) & (Y - 1), xx, core), z)

    def merge(g):
        core_copy(g).wait_recv()
        for i in range(g * HALF * X, (g + 1) * HALF * X):
            mine, other = t0[core, i], cr[i]
            near = jnp.where(core == 0, mine, other)
            far = jnp.where(core == 0, other, mine)
            x0[i] = jnp.where(lane < 96, near, 0.0) + expand(near, lane) * far
        for away in ((4, 3, 5, 2), (6, 1, 7, 0))[g]:
            for across in (2, 1, 3, 0):
                if away or across:
                    chip_copy((away - 2) % Y, away, across).start()

    heard(2, two_off)
    for g in range(2):
        with mark(f"merge{g}"):
            merge(g)
    for side in range(2):
        each(to[side], [depth_copy(kind, side, sp) for kind in ("h", "p", "0", "1") for sp in range(2)], "wait_send")
        each(zto[side], [row_copy(kind, side, sp) for kind in ("0", "1") for sp in range(2)], "wait_send")
    for g in range(2):
        core_copy(g).wait_send()
    xr[chip] = x0[(Y - 2) * X + x]
    arrived = xr.at[pl.ds(0, CHIPS - 1)]
    with mark("w_xy"):
        pltpu.make_async_copy(arrived, arrived, x_recv).wait()

    pltpu.make_async_copy(arrived, arrived, x_send).wait()


def finish(new, xr, out_s, out_c, out_image, img, out_sem):
    copies = [pltpu.make_async_copy(new.at[0], out_s, out_sem.at[0]),
              pltpu.make_async_copy(new.at[1], out_c, out_sem.at[1])]
    for copy in copies:
        copy.start()
    lane = lax.broadcasted_iota(jnp.int32, (8, 128), 1)
    total, light = jnp.zeros((8, 128), jnp.float32), jnp.ones((8, 128), jnp.float32)
    for i in range(CHIPS):
        tile = xr[i]
        total += light * jnp.where(lane < 96, tile, 0.0)
        light *= expand(tile, lane)
    tile = jnp.where(lane < 96, total, 1.0 - light)
    for g in range(8):
        part = tile if g == 0 else pltpu.roll(tile, 128 - 16 * g, 1)
        img[g // 2, pl.ds(8 * (g % 2), 8), :] = part[:, :16]
    copies.append(pltpu.make_async_copy(img, out_image, out_sem.at[2]))
    copies[2].start()
    for copy in copies:
        copy.wait()


def body(substrate, catalyst, feed_rate, kill_rate, extinction, palette):
    field = jax.ShapeDtypeStruct(substrate.shape, jnp.float32)
    any_ref = pl.BlockSpec(memory_space=pl.ANY)
    f32 = jnp.float32
    dma = pltpu.SemaphoreType.DMA
    new, parts = pl.pallas_call(
        kernel,
        out_shape=(pltpu.VMEM((2,) + field.shape, f32), pltpu.VMEM((CHIPS, 8, 128), f32)),
        in_specs=[any_ref] * 6,
        out_specs=(pl.BlockSpec(memory_space=pltpu.VMEM),) * 2,
        scratch_shapes=[
            pltpu.VMEM((2, LAYERS, (CT + 2) * TILE, 128), f32),
            pltpu.VMEM((2, LAYERS, (CT + 2) * TILE, 128), f32),
            pltpu.VMEM((LAYERS, 16, CT * 128), f32),
            pltpu.VMEM((LAYERS, 16, CT * 128), f32),
            pltpu.VMEM((LAYERS, 16, CT * 128), f32),
            pltpu.VMEM((2, 2, 16, CT * 128), f32),
            pltpu.VMEM((2, 2, 2, HALF * 16, 128), f32),
            pltpu.VMEM((2, 2, 2, HALF * 16, 128), f32),
            pltpu.VMEM((2, 2, LAYERS, CT, 128), f32),
            pltpu.VMEM((2, 2, LAYERS, CT, 128), f32),
            pltpu.VMEM((2, 2, LAYERS, CT, 128), f32),
            pltpu.VMEM((2, 2, LAYERS, CT, 128), f32),
            pltpu.VMEM((2, 2, 2, CT, 128), f32),
            pltpu.VMEM((4, CT * 16, 128), f32),
            pltpu.VMEM((CT * 8, 8, 128), f32),
            pltpu.VMEM((2, CHIPS, 8, 128), f32),
            pltpu.VMEM((CHIPS, 8, 128), f32),
            pltpu.VMEM((CHIPS, 8, 128), f32),
            pltpu.SMEM((3, 3), f32),
            dma((6,)),
            dma((2, 2)), dma((2, 2)), dma((2, 2)), dma((2, 2)),
            dma((2, 2)), dma((2, 2)), dma((2, 2)), dma((2, 2)),
            dma((2, 2, 2)), dma((2, 2, 2)),
            dma((2,)), dma((2,)), dma, dma,
            pltpu.SemaphoreType.REGULAR((3,)),
        ],
        compiler_params=pltpu.CompilerParams(collective_id=0, has_side_effects=True),
    )(palette, substrate, catalyst, feed_rate, kill_rate, extinction)
    return pl.pallas_call(
        finish,
        out_shape=(field, field, jax.ShapeDtypeStruct((4, 16, 16), f32)),
        in_specs=[pl.BlockSpec(memory_space=pltpu.VMEM)] * 2,
        out_specs=(any_ref,) * 3,
        scratch_shapes=[pltpu.VMEM((4, 16, 16), f32), dma((3,))],
    )(*(pltpu.with_memory_space_constraint(part, pltpu.VMEM) for part in (new, parts)))


def solution(mesh):
    split = P("depth", "rows", None)
    return jax.shard_map(
        body,
        mesh=mesh,
        in_specs=(split,) * 5 + (P(),),
        out_specs=(split, split, P(None, "rows", "depth")),
        check_vma=False,
    )
```

```python
import contextlib

import jax
import jax.numpy as jnp
from jax import lax
from jax.experimental import pallas as pl
from jax.experimental.pallas import tpu as pltpu
from jax.sharding import PartitionSpec as P

mark = contextlib.nullcontext
MESH = pl.DeviceIdType.MESH
X, Y = 4, 8
CHIPS = X * Y
DEPTHS = 2 * CHIPS
ZS = 8
CT = 8
LAYERS = 4
TILE = 32
COEF = (0.16, 0.08)
FIRST = 8
GROUP = 4
HALF = CT // 2


def expand(tile, lane):
    light = jnp.where(lane >= 96, tile, 0.0)
    return light + pltpu.roll(light, 32, 1) + (pltpu.roll(light, 64, 1) + pltpu.roll(light, 96, 1))


def regroup(tiles, lane):
    tiles = list(tiles)
    for bit in (1, 2, 4):
        low_half = (lane & (16 * bit)) == 0
        for g in range(8):
            if g & bit:
                continue
            low, high = tiles[g], tiles[g | bit]
            tiles[g] = jnp.where(low_half, low, pltpu.roll(high, 16 * bit, 1))
            tiles[g | bit] = jnp.where(low_half, pltpu.roll(low, 128 - 16 * bit, 1), high)
    return tiles


def kernel(palette, S, C, F, K, E, new, xr,
           s0, s1, fv, kv, ev, h0, ph, ps, r0, r1, rs0, rs1, eg, dg, mid, flat, t0, cr, x0, pal,
           load_sem, h_send, h_recv, p_send, p_recv, r0_send, r0_recv, r1_send, r1_recv,
           e_send, e_recv, g_send, g_recv, c_send, c_recv, x_send, x_recv, everyone, ready):
    d = lax.axis_index("depth")
    z = lax.axis_index("rows")
    core = d & 1
    chip = d >> 1
    x = chip & (X - 1)
    y = chip >> 2

    def at(yy, xx, cc):
        return (yy * X + xx) * 2 + cc

    has = {"lo": d > 0, "hi": d < DEPTHS - 1, "zlo": z > 0, "zhi": z < ZS - 1}
    up, down = jnp.minimum(d + 1, DEPTHS - 1), jnp.maximum(d - 1, 0)
    zup, zdown = jnp.minimum(z + 1, ZS - 1), jnp.maximum(z - 1, 0)

    barrier = pltpu.get_barrier_semaphore()

    def signal(sem, depth, row):
        pl.semaphore_signal(sem, inc=1, device_id=(depth, row), device_id_type=MESH)

    for flag, depth, row in (("lo", down, z), ("hi", up, z), ("zhi", d, zup)):
        @pl.when(has[flag])
        def _(depth=depth, row=row):
            signal(barrier, depth, row)

    collector = at(Y // 2, X // 2, core)
    collects = d == collector

    @pl.when(jnp.logical_not(collects))
    def _():
        signal(barrier, collector, z)

    for ct in range(CT):
        for sp, src in ((0, S), (1, C)):
            pltpu.make_async_copy(
                src.at[:, :, pl.ds(ct * 128, 128)],
                s0.at[sp, :, pl.ds((ct + 1) * TILE + FIRST, 16), :],
                load_sem.at[sp],
            ).start()
    pal_load = pltpu.make_async_copy(palette, pal, load_sem.at[5])
    f_load = pltpu.make_async_copy(F, fv, load_sem.at[2])
    k_load = pltpu.make_async_copy(K, kv, load_sem.at[3])
    e_load = pltpu.make_async_copy(E, ev, load_sem.at[4])
    f_load.start()
    k_load.start()
    e_load.start()
    pal_load.start()

    with mark("w_barrier"):
        pl.semaphore_wait(barrier, sum(jnp.where(has[flag], 1, 0) for flag in ("lo", "hi", "zlo")) + jnp.where(collects, CHIPS - 1, 0))

    @pl.when(has["zlo"])
    def _():
        signal(ready, d, zdown)

    @pl.when(collects)
    def _():
        def tell(i, carry):
            signal(everyone, 2 * ((chip + i) & (CHIPS - 1)) + core, z)
            return carry

        lax.fori_loop(1, CHIPS, tell, 0)

    zero = jnp.zeros((8, 128), jnp.float32)
    for sp in range(2):
        for layer in range(LAYERS):
            for buf in (s0, s1):
                for t in (0, CT + 1):
                    for rb in range(2):
                        buf[sp, layer, pl.ds(t * TILE + FIRST + 8 * rb, 8), :] = zero
            for row in (FIRST - 1, FIRST + 16):
                s0[sp, layer, pl.ds(TILE + row, CT, stride=TILE), :] = zero
    for side, flag in ((0, "lo"), (1, "hi")):
        @pl.when(jnp.logical_not(has[flag]))
        def _(side=side):
            for sp in range(2):
                for rowside in range(2):
                    eg[side, rowside, sp] = zero

                def fill(i, carry):
                    h0[side, sp, :, pl.ds(i * 128, 128)] = jnp.zeros((16, 128), jnp.float32)
                    ph[side, i // HALF, sp, pl.ds((i % HALF) * 16, 16), :] = jnp.zeros((16, 128), jnp.float32)
                    return carry

                lax.fori_loop(0, CT, fill, 0)
    for side, flag in ((0, "zlo"), (1, "zhi")):
        @pl.when(jnp.logical_not(has[flag]))
        def _(side=side):
            for sp in range(2):
                for layer in range(LAYERS):
                    r0[side, sp, layer] = zero
                    r1[side, sp, layer] = zero
                for depthside in range(2):
                    dg[depthside, side, sp] = zero

    def remote(src, dst, send, recv, depth, row):
        return pltpu.make_async_remote_copy(
            src_ref=src, dst_ref=dst, send_sem=send, recv_sem=recv,
            device_id=(depth, row), device_id_type=MESH)

    def depth_copy(kind, side, sp):
        target = up if side == 0 else down
        if kind == "h":
            src = (S, C)[sp].at[LAYERS - 1 if side == 0 else 0]
            return remote(src, h0.at[side, sp], h_send.at[side, sp], h_recv.at[side, sp], target, z)
        if kind == "p":
            half = sp
            return remote(ps.at[side, half], ph.at[side, half], p_send.at[side, half], p_recv.at[side, half], target, z)
        return remote(rs0.at[:, :, LAYERS - 1 if side == 0 else 0], eg.at[side],
                      e_send.at[side], e_recv.at[side], target, z)

    def row_copy(kind, side):
        target = zup if side == 0 else zdown
        if kind == "0":
            return remote(rs0.at[side], r0.at[side], r0_send.at[side], r0_recv.at[side], d, target)
        if kind == "corner":
            return remote(eg.at[:, side], dg.at[:, side], g_send.at[side], g_recv.at[side], d, target)
        return remote(rs1.at[side], r1.at[side], r1_send.at[side], r1_recv.at[side], d, target)

    to = ("hi", "lo")
    source = ("lo", "hi")
    zto = ("zhi", "zlo")
    zsource = ("zlo", "zhi")

    def each(flag, copies, what):
        @pl.when(has[flag])
        def _():
            for copy in copies:
                getattr(copy, what)()

    with mark("w_load"):
        for sp in range(2):
            whole = s0.at[sp, :, pl.ds(0, CT * 16), :]
            pltpu.make_async_copy(whole, whole, load_sem.at[sp]).wait()
    for side in range(2):
        row = TILE + FIRST + (15 if side == 0 else 0)
        for sp in range(2):
            for layer in range(LAYERS):
                rs0[side, sp, layer] = s0[sp, layer, pl.ds(row, CT, stride=TILE), :]
    for side in range(2):
        each(to[side], [depth_copy("edge", side, 0)] + [depth_copy("h", side, sp) for sp in range(2)], "start")
    each("zlo", [row_copy("0", 1)], "start")

    with mark("w_loadfk"):
        f_load.wait()
        k_load.wait()

    lane = lax.broadcasted_iota(jnp.int32, (8, 128), 1)

    def in_groups(step):
        def group(g, carry):
            for q in range(GROUP):
                step(g * GROUP + q, carry)
            return carry

        lax.fori_loop(0, CT // GROUP, group, 0)

    def start_of(ct, rb):
        return pl.multiple_of((ct + 1) * TILE + FIRST + 8 * rb, 8)

    def centre(buf, sp, layer, ct, rb):
        return buf[sp, layer, pl.ds(start_of(ct, rb), 8), :]

    def around(buf, sp, layer, ct, rb):
        here = centre(buf, sp, layer, ct, rb)
        left = centre(buf, sp, layer, ct - 1, rb)
        right = centre(buf, sp, layer, ct + 1, rb)
        total = pltpu.roll(jnp.where(lane == 127, left, here), 1, 1)
        total += pltpu.roll(jnp.where(lane == 0, right, here), 127, 1)
        base = start_of(ct, rb)
        total += buf[sp, layer, pl.ds(base - 1, 8), :]
        total += buf[sp, layer, pl.ds(base + 1, 8), :]
        return here, total

    def native(ref, layer, ct, rb):
        return ref[layer, pl.ds(8 * rb, 8), pl.ds(pl.multiple_of(ct * 128, 128), 128)]

    def react(s, c, around_s, around_c, layer, ct, rb):
        feed = native(fv, layer, ct, rb)
        kill = native(kv, layer, ct, rb)
        feed = feed + feed
        reaction = s * c * c
        reaction = reaction + reaction
        new_s = COEF[0] * around_s + (feed + s * (0.04 - feed)) - reaction
        new_c = COEF[1] * around_c + c * (0.52 - feed - (kill + kill)) + reaction
        return new_s, new_c

    def first(layers):
        def body(ct, carry):
            for layer in layers:
                for rb in range(2):
                    values = []
                    for sp in range(2):
                        here, total = around(s0, sp, layer, ct, rb)
                        if layer > 0:
                            total += centre(s0, sp, layer - 1, ct, rb)
                        if layer < LAYERS - 1:
                            total += centre(s0, sp, layer + 1, ct, rb)
                        values.append((here, total))
                    result = react(values[0][0], values[1][0], values[0][1], values[1][1], layer, ct, rb)
                    for sp in range(2):
                        s1[sp, layer, pl.ds(start_of(ct, rb), 8), :] = result[sp]
                        for side, edge, target in ((0, LAYERS - 1, up), (1, 0, down)):
                            if layer == edge:
                                place = (ct - (target >> 3) + (Y - 2)) & (Y - 1)
                                rows = pl.multiple_of((place & (HALF - 1)) * 16 + 8 * rb, 8)
                                ps[side, place >> 2, sp, pl.ds(rows, 8), :] = result[sp]
            return carry

        in_groups(body)

    with mark("first03"):
        first((0, LAYERS - 1))
    for side in range(2):
        each(to[side], [depth_copy("p", side, half) for half in range(2)], "start")
    with mark("first12"):
        first(range(1, LAYERS - 1))
    for side in range(2):
        row = TILE + FIRST + (15 if side == 0 else 0)
        for sp in range(2):
            for layer in range(LAYERS):
                rs1[side, sp, layer] = s1[sp, layer, pl.ds(row, CT, stride=TILE), :]
    each("zlo", [row_copy("1", 1)], "start")
    with mark("w_readyz"):
        @pl.when(has["zhi"])
        def _():
            pl.semaphore_wait(ready, 1)
            for kind in ("0", "1"):
                row_copy(kind, 0).start()

    with mark("w_edge"):
        for side in range(2):
            each(source[side], [depth_copy("edge", side, 0)], "wait_recv")
    for side in range(2):
        each(zto[side], [row_copy("corner", side)], "start")

    with mark("w_row0"):
        for side in range(2):
            each(zsource[side], [row_copy("0", side)], "wait_recv")

    scale = {flag: jnp.where(has[flag], 1.0, 0.0).astype(jnp.float32) for flag in has}
    for side in range(2):
        row = TILE + FIRST + (0 if side == 0 else 15)
        for sp in range(2):
            for layer in range(LAYERS):
                where = pl.ds(row, CT, stride=TILE)
                s1[sp, layer, where, :] = s1[sp, layer, where, :] + COEF[sp] * r0[side, sp, layer]
    with mark("w_row1"):
        for side in range(2):
            each(zsource[side], [row_copy("1", side)], "wait_recv")
    for side in range(2):
        edge = TILE + FIRST + (0 if side == 0 else 15)
        outside = TILE + FIRST + (-1 if side == 0 else 16)
        for sp in range(2):
            factor = COEF[sp] * scale[zsource[side]]
            for layer in range(LAYERS):
                s1[sp, layer, pl.ds(outside, CT, stride=TILE), :] = (
                    r1[side, sp, layer] + factor * s0[sp, layer, pl.ds(edge, CT, stride=TILE), :])

    with mark("w_h"):
        for side in range(2):
            each(source[side], [depth_copy("h", side, sp) for sp in range(2)], "wait_recv")

    def add_layers(ct, carry):
        for side, layer in ((0, 0), (1, LAYERS - 1)):
            for sp in range(2):
                for rb in range(2):
                    where = pl.ds(start_of(ct, rb), 8)
                    halo = h0[side, sp, pl.ds(8 * rb, 8), pl.ds(pl.multiple_of(ct * 128, 128), 128)]
                    s1[sp, layer, where, :] = s1[sp, layer, where, :] + COEF[sp] * halo
        return carry

    with mark("addlayers"):
        in_groups(add_layers)

    e_load.wait()
    pal_load.wait()
    weights = []
    for k in range(3):
        a, b = -8.0 * pal[k, 0], -8.0 * pal[k, 1]
        weights.append((a, b, -pal[k, 2] - 0.65 * a - 0.25 * b))

    def columns_of(ct):
        return pl.ds(pl.multiple_of(ct * 128, 128), 128)

    def second(layer, ct, rb):
        values = []
        for sp in range(2):
            here, total = around(s1, sp, layer, ct, rb)
            if layer > 0:
                total += centre(s1, sp, layer - 1, ct, rb)
            else:
                total += (COEF[sp] * scale["lo"]) * centre(s0, sp, 0, ct, rb)
            if layer < LAYERS - 1:
                total += centre(s1, sp, layer + 1, ct, rb)
            else:
                total += (COEF[sp] * scale["hi"]) * centre(s0, sp, LAYERS - 1, ct, rb)
            values.append((here, total))
        return react(values[0][0], values[1][0], values[0][1], values[1][1], layer, ct, rb)

    def shade(s, c, layer, ct, rb):
        new[0, layer, pl.ds(8 * rb, 8), columns_of(ct)] = s
        new[1, layer, pl.ds(8 * rb, 8), columns_of(ct)] = c
        passing = jnp.exp(-native(ev, layer, ct, rb) * (0.25 + 4.0 * c * c))
        opacity = 1.0 - passing
        colors = [opacity / (1.0 + jnp.exp(a * s + b * c + e)) for a, b, e in weights]
        return colors, passing

    def middle(ct, carry):
        for rb in range(2):
            rows = pl.ds(pl.multiple_of(ct * 16 + 8 * rb, 8), 8)
            near, light = shade(*second(1, ct, rb), 1, ct, rb)
            far, light_far = shade(*second(2, ct, rb), 2, ct, rb)
            for k in range(3):
                mid[k, rows, :] = near[k] + light * far[k]
            mid[3, rows, :] = light * light_far
        return carry

    with mark("middle"):
        in_groups(middle)

    def open_ends(ct, carry):
        for layer in (0, LAYERS - 1):
            for rb in range(2):
                for sp, value in enumerate(second(layer, ct, rb)):
                    new[sp, layer, pl.ds(8 * rb, 8), columns_of(ct)] = value
        return carry

    with mark("open_ends"):
        in_groups(open_ends)

    with mark("w_diag"):
        for side in range(2):
            each(zsource[side], [row_copy("corner", side)], "wait_recv")
    corner = {}
    for side in range(2):
        for rowside in range(2):
            for sp in range(2):
                corner[side, rowside, sp] = pltpu.roll(dg[side, rowside, sp], (Y - 2 - y) & (Y - 1), 0) * (2.0 * COEF[sp])

    def add_corners(half):
        for (side, rowside, sp), rows in corner.items():
            where = pl.ds(15 * rowside, HALF, stride=16)
            ph[side, half, sp, where, :] = ph[side, half, sp, where, :] + rows[half * HALF:half * HALF + HALF]

    partner = d + 1 - 2 * core

    def core_copy(g):
        some = pl.ds(g * HALF * X, HALF * X)
        return remote(t0.at[1 - core, some], cr.at[some], c_send.at[g], c_recv.at[g], partner, z)

    def ends(g):
        with mark(f"w_p{g}"):
            for side in range(2):
                each(source[side], [depth_copy("p", side, g)], "wait_recv")
        add_corners(g)
        for q in range(HALF):
            place = g * HALF + q
            ct = (y + place + 2) & (Y - 1)
            for rb in range(2):
                parts = []
                for side, layer in ((0, 0), (1, LAYERS - 1)):
                    values = [new[sp, layer, pl.ds(8 * rb, 8), columns_of(ct)]
                              + COEF[sp] * ph[side, g, sp, pl.ds(q * 16 + 8 * rb, 8), :] for sp in range(2)]
                    parts.append(shade(*values, layer, ct, rb))
                (near, light), (far, light_far) = parts
                rows = pl.ds(pl.multiple_of(ct * 16 + 8 * rb, 8), 8)
                light_mid = light * mid[3, rows, :]
                for k in range(3):
                    flat[place * 8 + 2 * k + rb] = near[k] + light * mid[k, rows, :] + light_mid * far[k]
                flat[place * 8 + 6 + rb] = light_mid * light_far
        for place in range(g * HALF, g * HALF + HALF):
            for j, tile in enumerate(regroup([flat[place * 8 + i] for i in range(8)], lane)):
                t0[j % 2, place * X + j // 2] = tile
        core_copy(g).start()

    for g in range(2):
        with mark(f"ends{g}"):
            ends(g)

    def chip_copy(place, away, across):
        xx = (x + across) & (X - 1)
        return remote(x0.at[place * X + xx], xr.at[chip], x_send, x_recv, at((y + away) & (Y - 1), xx, core), z)

    def merge(g):
        core_copy(g).wait_recv()
        for i in range(g * HALF * X, (g + 1) * HALF * X):
            mine, other = t0[core, i], cr[i]
            near = jnp.where(core == 0, mine, other)
            far = jnp.where(core == 0, other, mine)
            x0[i] = jnp.where(lane < 96, near, 0.0) + expand(near, lane) * far
        for away in ((4, 3, 5, 2), (6, 1, 7, 0))[g]:
            for across in (2, 1, 3, 0):
                if away or across:
                    chip_copy((away - 2) % Y, away, across).start()

    with mark("w_everyone"):
        @pl.when(jnp.logical_not(collects))
        def _():
            pl.semaphore_wait(everyone, 1)

    for g in range(2):
        with mark(f"merge{g}"):
            merge(g)
    for side in range(2):
        each(to[side], [depth_copy("edge", side, 0)] + [depth_copy(kind, side, i) for kind in ("h", "p") for i in range(2)], "wait_send")
        each(zto[side], [row_copy(kind, side) for kind in ("0", "1", "corner")], "wait_send")
    for g in range(2):
        core_copy(g).wait_send()
    xr[chip] = x0[(Y - 2) * X + x]
    arrived = xr.at[pl.ds(0, CHIPS - 1)]
    with mark("w_xy"):
        pltpu.make_async_copy(arrived, arrived, x_recv).wait()

    pltpu.make_async_copy(arrived, arrived, x_send).wait()


def finish(new, xr, out_s, out_c, out_image, img, out_sem):
    copies = [pltpu.make_async_copy(new.at[0], out_s, out_sem.at[0]),
              pltpu.make_async_copy(new.at[1], out_c, out_sem.at[1])]
    for copy in copies:
        copy.start()
    lane = lax.broadcasted_iota(jnp.int32, (8, 128), 1)

    def compose(g, carry):
        total, light = carry
        for i in range(HALF * X):
            tile = xr[g * HALF * X + i]
            total += light * jnp.where(lane < 96, tile, 0.0)
            light *= expand(tile, lane)
        return total, light

    total, light = lax.fori_loop(0, 2, compose, (jnp.zeros((8, 128), jnp.float32), jnp.ones((8, 128), jnp.float32)))
    tile = jnp.where(lane < 96, total, 1.0 - light)
    for g in range(8):
        part = tile if g == 0 else pltpu.roll(tile, 128 - 16 * g, 1)
        img[g // 2, pl.ds(8 * (g % 2), 8), :] = part[:, :16]
    copies.append(pltpu.make_async_copy(img, out_image, out_sem.at[2]))
    copies[2].start()
    for copy in copies:
        copy.wait()


def body(substrate, catalyst, feed_rate, kill_rate, extinction, palette):
    field = jax.ShapeDtypeStruct(substrate.shape, jnp.float32)
    any_ref = pl.BlockSpec(memory_space=pl.ANY)
    f32 = jnp.float32
    dma = pltpu.SemaphoreType.DMA
    new, parts = pl.pallas_call(
        kernel,
        out_shape=(pltpu.VMEM((2,) + field.shape, f32), pltpu.VMEM((CHIPS, 8, 128), f32)),
        in_specs=[any_ref] * 6,
        out_specs=(pl.BlockSpec(memory_space=pltpu.VMEM),) * 2,
        scratch_shapes=[
            pltpu.VMEM((2, LAYERS, (CT + 2) * TILE, 128), f32),
            pltpu.VMEM((2, LAYERS, (CT + 2) * TILE, 128), f32),
            pltpu.VMEM((LAYERS, 16, CT * 128), f32),
            pltpu.VMEM((LAYERS, 16, CT * 128), f32),
            pltpu.VMEM((LAYERS, 16, CT * 128), f32),
            pltpu.VMEM((2, 2, 16, CT * 128), f32),
            pltpu.VMEM((2, 2, 2, HALF * 16, 128), f32),
            pltpu.VMEM((2, 2, 2, HALF * 16, 128), f32),
            pltpu.VMEM((2, 2, LAYERS, CT, 128), f32),
            pltpu.VMEM((2, 2, LAYERS, CT, 128), f32),
            pltpu.VMEM((2, 2, LAYERS, CT, 128), f32),
            pltpu.VMEM((2, 2, LAYERS, CT, 128), f32),
            pltpu.VMEM((2, 2, 2, CT, 128), f32),
            pltpu.VMEM((2, 2, 2, CT, 128), f32),
            pltpu.VMEM((4, CT * 16, 128), f32),
            pltpu.VMEM((CT * 8, 8, 128), f32),
            pltpu.VMEM((2, CHIPS, 8, 128), f32),
            pltpu.VMEM((CHIPS, 8, 128), f32),
            pltpu.VMEM((CHIPS, 8, 128), f32),
            pltpu.SMEM((3, 3), f32),
            dma((6,)),
            dma((2, 2)), dma((2, 2)), dma((2, 2)), dma((2, 2)),
            dma((2,)), dma((2,)), dma((2,)), dma((2,)),
            dma((2,)), dma((2,)), dma((2,)), dma((2,)),
            dma((2,)), dma((2,)), dma, dma,
            pltpu.SemaphoreType.REGULAR, pltpu.SemaphoreType.REGULAR,
        ],
        compiler_params=pltpu.CompilerParams(collective_id=0, has_side_effects=True),
    )(palette, substrate, catalyst, feed_rate, kill_rate, extinction)
    return pl.pallas_call(
        finish,
        out_shape=(field, field, jax.ShapeDtypeStruct((4, 16, 16), f32)),
        in_specs=[pl.BlockSpec(memory_space=pltpu.VMEM)] * 2,
        out_specs=(any_ref,) * 3,
        scratch_shapes=[pltpu.VMEM((4, 16, 16), f32), dma((3,))],
    )(*(pltpu.with_memory_space_constraint(part, pltpu.VMEM) for part in (new, parts)))


def solution(mesh):
    split = P("depth", "rows", None)
    return jax.shard_map(
        body,
        mesh=mesh,
        in_specs=(split,) * 5 + (P(),),
        out_specs=(split, split, P(None, "rows", "depth")),
        check_vma=False,
    )
```

```python
import contextlib

import jax
import jax.numpy as jnp
from jax import lax
from jax.experimental import pallas as pl
from jax.experimental.pallas import tpu as pltpu
from jax.sharding import PartitionSpec as P

mark = contextlib.nullcontext
MESH = pl.DeviceIdType.MESH
X, Y = 4, 8
CHIPS = X * Y
DEPTHS = 2 * CHIPS
ZS = 8
CT = 8
LAYERS = 4
TILE = 32
COEF = (0.16, 0.08)
FIRST = 8
GROUP = 4
HALF = CT // 2
COLLECTORS = (1, (Y // 2) * X + X // 2)
DIRECT = ((4, 2), (4, 1), (4, 3), (3, 2), (5, 2), (6, 2))
TILES = CHIPS - 1 + len(DIRECT)


def expand(tile, lane):
    light = jnp.where(lane >= 96, tile, 0.0)
    return light + pltpu.roll(light, 32, 1) + (pltpu.roll(light, 64, 1) + pltpu.roll(light, 96, 1))


def regroup(tiles, lane):
    tiles = list(tiles)
    for bit in (1, 2, 4):
        low_half = (lane & (16 * bit)) == 0
        for g in range(8):
            if g & bit:
                continue
            low, high = tiles[g], tiles[g | bit]
            tiles[g] = jnp.where(low_half, low, pltpu.roll(high, 16 * bit, 1))
            tiles[g | bit] = jnp.where(low_half, pltpu.roll(low, 128 - 16 * bit, 1), high)
    return tiles


def kernel(palette, S, C, F, K, E, new, xr,
           s0, s1, fv, kv, ev, h0, ph, ps, r0, r1, rs0, rs1, eg, dg, mid, flat, t0, cr, x0, pal,
           load_sem, h_send, h_recv, p_send, p_recv, r0_send, r0_recv, r1_send, r1_recv,
           e_send, e_recv, g_send, g_recv, c_send, c_recv, x_send, x_recv, everyone, ready):
    d = lax.axis_index("depth")
    z = lax.axis_index("rows")
    core = d & 1
    chip = d >> 1
    x = chip & (X - 1)
    y = chip >> 2

    def at(yy, xx, cc):
        return (yy * X + xx) * 2 + cc

    has = {"lo": d > 0, "hi": d < DEPTHS - 1, "zlo": z > 0, "zhi": z < ZS - 1}
    up, down = jnp.minimum(d + 1, DEPTHS - 1), jnp.maximum(d - 1, 0)
    zup, zdown = jnp.minimum(z + 1, ZS - 1), jnp.maximum(z - 1, 0)

    barrier = pltpu.get_barrier_semaphore()

    def signal(sem, depth, row):
        pl.semaphore_signal(sem, inc=1, device_id=(depth, row), device_id_type=MESH)

    for flag, depth, row in (("lo", down, z), ("hi", up, z), ("zhi", d, zup)):
        @pl.when(has[flag])
        def _(depth=depth, row=row):
            signal(barrier, depth, row)

    collector = jnp.where(z == 0, COLLECTORS[0], COLLECTORS[1])
    collects = chip == collector
    for c in range(2):
        @pl.when(d != 2 * collector + c)
        def _(c=c):
            signal(barrier, 2 * collector + c, z)

    for ct in range(CT):
        for sp, src in ((0, S), (1, C)):
            pltpu.make_async_copy(
                src.at[:, :, pl.ds(ct * 128, 128)],
                s0.at[sp, :, pl.ds((ct + 1) * TILE + FIRST, 16), :],
                load_sem.at[sp],
            ).start()
    pal_load = pltpu.make_async_copy(palette, pal, load_sem.at[5])
    f_load = pltpu.make_async_copy(F, fv, load_sem.at[2])
    k_load = pltpu.make_async_copy(K, kv, load_sem.at[3])
    e_load = pltpu.make_async_copy(E, ev, load_sem.at[4])
    f_load.start()
    k_load.start()
    e_load.start()
    pal_load.start()

    with mark("w_barrier"):
        pl.semaphore_wait(barrier, sum(jnp.where(has[flag], 1, 0) for flag in ("lo", "hi", "zlo")) + jnp.where(collects, DEPTHS - 1, 0))

    @pl.when(has["zlo"])
    def _():
        signal(ready, d, zdown)

    @pl.when(collects)
    def _():
        def tell(i, carry):
            signal(everyone, 2 * ((chip + i) & (CHIPS - 1)) + core, z)
            return carry

        lax.fori_loop(1, CHIPS, tell, 0)

    zero = jnp.zeros((8, 128), jnp.float32)
    for sp in range(2):
        for layer in range(LAYERS):
            for buf in (s0, s1):
                for t in (0, CT + 1):
                    for rb in range(2):
                        buf[sp, layer, pl.ds(t * TILE + FIRST + 8 * rb, 8), :] = zero
            for row in (FIRST - 1, FIRST + 16):
                s0[sp, layer, pl.ds(TILE + row, CT, stride=TILE), :] = zero
    for side, flag in ((0, "lo"), (1, "hi")):
        @pl.when(jnp.logical_not(has[flag]))
        def _(side=side):
            for sp in range(2):
                for rowside in range(2):
                    eg[side, rowside, sp] = zero

                def fill(i, carry):
                    h0[side, sp, :, pl.ds(i * 128, 128)] = jnp.zeros((16, 128), jnp.float32)
                    ph[side, i // HALF, sp, pl.ds((i % HALF) * 16, 16), :] = jnp.zeros((16, 128), jnp.float32)
                    return carry

                lax.fori_loop(0, CT, fill, 0)
    for side, flag in ((0, "zlo"), (1, "zhi")):
        @pl.when(jnp.logical_not(has[flag]))
        def _(side=side):
            for sp in range(2):
                for layer in range(LAYERS):
                    r0[side, sp, layer] = zero
                    r1[side, sp, layer] = zero
                for depthside in range(2):
                    dg[depthside, side, sp] = zero

    def remote(src, dst, send, recv, depth, row):
        return pltpu.make_async_remote_copy(
            src_ref=src, dst_ref=dst, send_sem=send, recv_sem=recv,
            device_id=(depth, row), device_id_type=MESH)

    def depth_copy(kind, side, sp):
        target = up if side == 0 else down
        if kind == "h":
            src = (S, C)[sp].at[LAYERS - 1 if side == 0 else 0]
            return remote(src, h0.at[side, sp], h_send.at[side], h_recv.at[side], target, z)
        if kind == "both":
            return remote(h0.at[side], h0.at[side], h_send.at[side], h_recv.at[side], target, z)
        if kind == "halves":
            return remote(ps.at[side], ph.at[side], p_send.at[side], p_recv.at[side, 0], target, z)
        if kind == "p":
            half = sp
            return remote(ps.at[side, half], ph.at[side, half], p_send.at[side], p_recv.at[side, half], target, z)
        return remote(rs0.at[:, :, LAYERS - 1 if side == 0 else 0], eg.at[side],
                      e_send.at[side], e_recv.at[side], target, z)

    def row_copy(kind, side):
        target = zup if side == 0 else zdown
        if kind == "0":
            return remote(rs0.at[side], r0.at[side], r0_send.at[side], r0_recv.at[side], d, target)
        if kind == "corner":
            return remote(eg.at[:, side], dg.at[:, side], g_send.at[side], g_recv.at[side], d, target)
        return remote(rs1.at[side], r1.at[side], r1_send.at[side], r1_recv.at[side], d, target)

    to = ("hi", "lo")
    source = ("lo", "hi")
    zto = ("zhi", "zlo")
    zsource = ("zlo", "zhi")

    def each(flag, copies, what):
        @pl.when(has[flag])
        def _():
            for copy in copies:
                getattr(copy, what)()

    with mark("w_load"):
        for sp in range(2):
            whole = s0.at[sp, :, pl.ds(0, CT * 16), :]
            pltpu.make_async_copy(whole, whole, load_sem.at[sp]).wait()
    for side in range(2):
        row = TILE + FIRST + (15 if side == 0 else 0)
        for sp in range(2):
            for layer in range(LAYERS):
                rs0[side, sp, layer] = s0[sp, layer, pl.ds(row, CT, stride=TILE), :]
    for side in range(2):
        each(to[side], [depth_copy("edge", side, 0)] + [depth_copy("h", side, sp) for sp in range(2)], "start")
    each("zlo", [row_copy("0", 1)], "start")

    with mark("w_loadfk"):
        f_load.wait()
        k_load.wait()

    lane = lax.broadcasted_iota(jnp.int32, (8, 128), 1)

    def in_groups(step):
        def group(g, carry):
            for q in range(GROUP):
                step(g * GROUP + q, carry)
            return carry

        lax.fori_loop(0, CT // GROUP, group, 0)

    def start_of(ct, rb):
        return pl.multiple_of((ct + 1) * TILE + FIRST + 8 * rb, 8)

    def centre(buf, sp, layer, ct, rb):
        return buf[sp, layer, pl.ds(start_of(ct, rb), 8), :]

    def around(buf, sp, layer, ct, rb):
        here = centre(buf, sp, layer, ct, rb)
        left = centre(buf, sp, layer, ct - 1, rb)
        right = centre(buf, sp, layer, ct + 1, rb)
        total = pltpu.roll(jnp.where(lane == 127, left, here), 1, 1)
        total += pltpu.roll(jnp.where(lane == 0, right, here), 127, 1)
        base = start_of(ct, rb)
        total += buf[sp, layer, pl.ds(base - 1, 8), :]
        total += buf[sp, layer, pl.ds(base + 1, 8), :]
        return here, total

    def native(ref, layer, ct, rb):
        return ref[layer, pl.ds(8 * rb, 8), pl.ds(pl.multiple_of(ct * 128, 128), 128)]

    def react(s, c, around_s, around_c, layer, ct, rb):
        feed = native(fv, layer, ct, rb)
        kill = native(kv, layer, ct, rb)
        feed = feed + feed
        reaction = s * c * c
        reaction = reaction + reaction
        new_s = COEF[0] * around_s + (feed + s * (0.04 - feed)) - reaction
        new_c = COEF[1] * around_c + c * (0.52 - feed - (kill + kill)) + reaction
        return new_s, new_c

    def first(layers):
        def body(ct, carry):
            for layer in layers:
                for rb in range(2):
                    values = []
                    for sp in range(2):
                        here, total = around(s0, sp, layer, ct, rb)
                        if layer > 0:
                            total += centre(s0, sp, layer - 1, ct, rb)
                        if layer < LAYERS - 1:
                            total += centre(s0, sp, layer + 1, ct, rb)
                        values.append((here, total))
                    result = react(values[0][0], values[1][0], values[0][1], values[1][1], layer, ct, rb)
                    for sp in range(2):
                        s1[sp, layer, pl.ds(start_of(ct, rb), 8), :] = result[sp]
                        for side, edge, target in ((0, LAYERS - 1, up), (1, 0, down)):
                            if layer == edge:
                                place = (ct - (target >> 3) + (Y - 2)) & (Y - 1)
                                rows = pl.multiple_of((place & (HALF - 1)) * 16 + 8 * rb, 8)
                                ps[side, place >> 2, sp, pl.ds(rows, 8), :] = result[sp]
            return carry

        in_groups(body)

    with mark("first03"):
        first((0, LAYERS - 1))
    for side in range(2):
        each(to[side], [depth_copy("p", side, half) for half in range(2)], "start")
    with mark("first12"):
        first(range(1, LAYERS - 1))
    for side in range(2):
        row = TILE + FIRST + (15 if side == 0 else 0)
        for sp in range(2):
            for layer in range(LAYERS):
                rs1[side, sp, layer] = s1[sp, layer, pl.ds(row, CT, stride=TILE), :]
    each("zlo", [row_copy("1", 1)], "start")
    with mark("w_readyz"):
        @pl.when(has["zhi"])
        def _():
            pl.semaphore_wait(ready, 1)
            for kind in ("0", "1"):
                row_copy(kind, 0).start()

    with mark("w_edge"):
        for side in range(2):
            each(source[side], [depth_copy("edge", side, 0)], "wait_recv")
    for side in range(2):
        each(zto[side], [row_copy("corner", side)], "start")

    with mark("w_row0"):
        for side in range(2):
            each(zsource[side], [row_copy("0", side)], "wait_recv")

    scale = {flag: jnp.where(has[flag], 1.0, 0.0).astype(jnp.float32) for flag in has}
    for side in range(2):
        row = TILE + FIRST + (0 if side == 0 else 15)
        for sp in range(2):
            for layer in range(LAYERS):
                where = pl.ds(row, CT, stride=TILE)
                s1[sp, layer, where, :] = s1[sp, layer, where, :] + COEF[sp] * r0[side, sp, layer]
    with mark("w_row1"):
        for side in range(2):
            each(zsource[side], [row_copy("1", side)], "wait_recv")
    for side in range(2):
        edge = TILE + FIRST + (0 if side == 0 else 15)
        outside = TILE + FIRST + (-1 if side == 0 else 16)
        for sp in range(2):
            factor = COEF[sp] * scale[zsource[side]]
            for layer in range(LAYERS):
                s1[sp, layer, pl.ds(outside, CT, stride=TILE), :] = (
                    r1[side, sp, layer] + factor * s0[sp, layer, pl.ds(edge, CT, stride=TILE), :])

    with mark("w_h"):
        for side in range(2):
            each(source[side], [depth_copy("both", side, 0)], "wait_recv")

    def add_layers(ct, carry):
        for side, layer in ((0, 0), (1, LAYERS - 1)):
            for sp in range(2):
                for rb in range(2):
                    where = pl.ds(start_of(ct, rb), 8)
                    halo = h0[side, sp, pl.ds(8 * rb, 8), pl.ds(pl.multiple_of(ct * 128, 128), 128)]
                    s1[sp, layer, where, :] = s1[sp, layer, where, :] + COEF[sp] * halo
        return carry

    with mark("addlayers"):
        in_groups(add_layers)

    e_load.wait()
    pal_load.wait()
    weights = []
    for k in range(3):
        a, b = -8.0 * pal[k, 0], -8.0 * pal[k, 1]
        weights.append((a, b, -pal[k, 2] - 0.65 * a - 0.25 * b))

    def columns_of(ct):
        return pl.ds(pl.multiple_of(ct * 128, 128), 128)

    def second(layer, ct, rb):
        values = []
        for sp in range(2):
            here, total = around(s1, sp, layer, ct, rb)
            if layer > 0:
                total += centre(s1, sp, layer - 1, ct, rb)
            else:
                total += (COEF[sp] * scale["lo"]) * centre(s0, sp, 0, ct, rb)
            if layer < LAYERS - 1:
                total += centre(s1, sp, layer + 1, ct, rb)
            else:
                total += (COEF[sp] * scale["hi"]) * centre(s0, sp, LAYERS - 1, ct, rb)
            values.append((here, total))
        return react(values[0][0], values[1][0], values[0][1], values[1][1], layer, ct, rb)

    def shade(s, c, layer, ct, rb):
        new[0, layer, pl.ds(8 * rb, 8), columns_of(ct)] = s
        new[1, layer, pl.ds(8 * rb, 8), columns_of(ct)] = c
        passing = jnp.exp(-native(ev, layer, ct, rb) * (0.25 + 4.0 * c * c))
        opacity = 1.0 - passing
        colors = [opacity / (1.0 + jnp.exp(a * s + b * c + e)) for a, b, e in weights]
        return colors, passing

    def middle(ct, carry):
        for rb in range(2):
            rows = pl.ds(pl.multiple_of(ct * 16 + 8 * rb, 8), 8)
            near, light = shade(*second(1, ct, rb), 1, ct, rb)
            far, light_far = shade(*second(2, ct, rb), 2, ct, rb)
            for k in range(3):
                mid[k, rows, :] = near[k] + light * far[k]
            mid[3, rows, :] = light * light_far
        return carry

    with mark("middle"):
        in_groups(middle)

    def open_ends(ct, carry):
        for layer in (0, LAYERS - 1):
            for rb in range(2):
                for sp, value in enumerate(second(layer, ct, rb)):
                    new[sp, layer, pl.ds(8 * rb, 8), columns_of(ct)] = value
        return carry

    with mark("open_ends"):
        in_groups(open_ends)

    with mark("w_diag"):
        for side in range(2):
            each(zsource[side], [row_copy("corner", side)], "wait_recv")
    corner = {}
    for side in range(2):
        for rowside in range(2):
            for sp in range(2):
                corner[side, rowside, sp] = pltpu.roll(dg[side, rowside, sp], (Y - 2 - y) & (Y - 1), 0) * (2.0 * COEF[sp])

    def add_corners(half):
        for (side, rowside, sp), rows in corner.items():
            where = pl.ds(15 * rowside, HALF, stride=16)
            ph[side, half, sp, where, :] = ph[side, half, sp, where, :] + rows[half * HALF:half * HALF + HALF]

    partner = d + 1 - 2 * core

    def core_copy(g):
        some = pl.ds(g * HALF * X, HALF * X)
        return remote(t0.at[1 - core, some], cr.at[some], c_send.at[g], c_recv.at[g], partner, z)

    def ends(g):
        with mark(f"w_p{g}"):
            for side in range(2):
                each(source[side], [depth_copy("p", side, g)], "wait_recv")
        add_corners(g)
        for q in range(HALF):
            place = g * HALF + q
            ct = (y + place + 2) & (Y - 1)
            for rb in range(2):
                parts = []
                for side, layer in ((0, 0), (1, LAYERS - 1)):
                    values = [new[sp, layer, pl.ds(8 * rb, 8), columns_of(ct)]
                              + COEF[sp] * ph[side, g, sp, pl.ds(q * 16 + 8 * rb, 8), :] for sp in range(2)]
                    parts.append(shade(*values, layer, ct, rb))
                (near, light), (far, light_far) = parts
                rows = pl.ds(pl.multiple_of(ct * 16 + 8 * rb, 8), 8)
                light_mid = light * mid[3, rows, :]
                for k in range(3):
                    flat[place * 8 + 2 * k + rb] = near[k] + light * mid[k, rows, :] + light_mid * far[k]
                flat[place * 8 + 6 + rb] = light_mid * light_far
        for place in range(g * HALF, g * HALF + HALF):
            for j, tile in enumerate(regroup([flat[place * 8 + i] for i in range(8)], lane)):
                t0[j % 2, place * X + j // 2] = tile
        core_copy(g).start()
        for away, across in DIRECT:
            place = (away - 2) % Y
            if place // HALF == g:
                yy, xx = (y + away) & (Y - 1), (x + across) & (X - 1)
                for c in range(2):
                    remote(t0.at[c, place * X + xx], xr.at[CHIPS * (1 + core) + chip], x_send, x_recv, at(yy, xx, c), z).start()

    with mark("w_everyone"):
        @pl.when(jnp.logical_not(collects))
        def _():
            pl.semaphore_wait(everyone, 1)

    for g in range(2):
        with mark(f"ends{g}"):
            ends(g)

    def chip_copy(place, away, across):
        xx = (x + across) & (X - 1)
        return remote(x0.at[place * X + xx], xr.at[chip], x_send, x_recv, at((y + away) & (Y - 1), xx, core), z)

    def joined(near, far):
        return jnp.where(lane < 96, near, 0.0) + expand(near, lane) * far

    def merge(g):
        core_copy(g).wait_recv()
        for i in range(g * HALF * X, (g + 1) * HALF * X):
            mine, other = t0[core, i], cr[i]
            x0[i] = joined(jnp.where(core == 0, mine, other), jnp.where(core == 0, other, mine))
        for away in ((4, 3, 5, 2), (6, 1, 7, 0))[g]:
            for across in (2, 1, 3, 0):
                if (away or across) and (away, across) not in DIRECT:
                    chip_copy((away - 2) % Y, away, across).start()

    for g in range(2):
        with mark(f"merge{g}"):
            merge(g)
    for side in range(2):
        each(to[side], [depth_copy(kind, side, 0) for kind in ("edge", "both", "halves")], "wait_send")
        each(zto[side], [row_copy(kind, side) for kind in ("0", "1", "corner")], "wait_send")
    for g in range(2):
        core_copy(g).wait_send()
    xr[chip] = x0[(Y - 2) * X + x]
    arrived = xr.at[pl.ds(0, TILES)]
    with mark("w_xy"):
        pltpu.make_async_copy(arrived, arrived, x_recv).wait()
    both = []
    for away, across in DIRECT:
        i = ((y - away) & (Y - 1)) * X + ((x - across) & (X - 1))
        both.append((i, joined(xr[CHIPS + i], xr[2 * CHIPS + i])))
    for i, tile in both:
        xr[i] = tile

    pltpu.make_async_copy(arrived, arrived, x_send).wait()


def finish(new, xr, out_s, out_c, out_image, img, out_sem):
    copies = [pltpu.make_async_copy(new.at[0], out_s, out_sem.at[0]),
              pltpu.make_async_copy(new.at[1], out_c, out_sem.at[1])]
    for copy in copies:
        copy.start()
    lane = lax.broadcasted_iota(jnp.int32, (8, 128), 1)

    def compose(g, carry):
        total, light = carry
        for i in range(HALF * X):
            tile = xr[g * HALF * X + i]
            total += light * jnp.where(lane < 96, tile, 0.0)
            light *= expand(tile, lane)
        return total, light

    total, light = lax.fori_loop(0, 2, compose, (jnp.zeros((8, 128), jnp.float32), jnp.ones((8, 128), jnp.float32)))
    tile = jnp.where(lane < 96, total, 1.0 - light)
    for g in range(8):
        part = tile if g == 0 else pltpu.roll(tile, 128 - 16 * g, 1)
        img[g // 2, pl.ds(8 * (g % 2), 8), :] = part[:, :16]
    copies.append(pltpu.make_async_copy(img, out_image, out_sem.at[2]))
    copies[2].start()
    for copy in copies:
        copy.wait()


def body(substrate, catalyst, feed_rate, kill_rate, extinction, palette):
    field = jax.ShapeDtypeStruct(substrate.shape, jnp.float32)
    any_ref = pl.BlockSpec(memory_space=pl.ANY)
    f32 = jnp.float32
    dma = pltpu.SemaphoreType.DMA
    new, parts = pl.pallas_call(
        kernel,
        out_shape=(pltpu.VMEM((2,) + field.shape, f32), pltpu.VMEM((3 * CHIPS, 8, 128), f32)),
        in_specs=[any_ref] * 6,
        out_specs=(pl.BlockSpec(memory_space=pltpu.VMEM),) * 2,
        scratch_shapes=[
            pltpu.VMEM((2, LAYERS, (CT + 2) * TILE, 128), f32),
            pltpu.VMEM((2, LAYERS, (CT + 2) * TILE, 128), f32),
            pltpu.VMEM((LAYERS, 16, CT * 128), f32),
            pltpu.VMEM((LAYERS, 16, CT * 128), f32),
            pltpu.VMEM((LAYERS, 16, CT * 128), f32),
            pltpu.VMEM((2, 2, 16, CT * 128), f32),
            pltpu.VMEM((2, 2, 2, HALF * 16, 128), f32),
            pltpu.VMEM((2, 2, 2, HALF * 16, 128), f32),
            pltpu.VMEM((2, 2, LAYERS, CT, 128), f32),
            pltpu.VMEM((2, 2, LAYERS, CT, 128), f32),
            pltpu.VMEM((2, 2, LAYERS, CT, 128), f32),
            pltpu.VMEM((2, 2, LAYERS, CT, 128), f32),
            pltpu.VMEM((2, 2, 2, CT, 128), f32),
            pltpu.VMEM((2, 2, 2, CT, 128), f32),
            pltpu.VMEM((4, CT * 16, 128), f32),
            pltpu.VMEM((CT * 8, 8, 128), f32),
            pltpu.VMEM((2, CHIPS, 8, 128), f32),
            pltpu.VMEM((CHIPS, 8, 128), f32),
            pltpu.VMEM((CHIPS, 8, 128), f32),
            pltpu.SMEM((3, 3), f32),
            dma((6,)),
            dma((2,)), dma((2,)), dma((2,)), dma((2, 2)),
            dma((2,)), dma((2,)), dma((2,)), dma((2,)),
            dma((2,)), dma((2,)), dma((2,)), dma((2,)),
            dma((2,)), dma((2,)), dma, dma,
            pltpu.SemaphoreType.REGULAR, pltpu.SemaphoreType.REGULAR,
        ],
        compiler_params=pltpu.CompilerParams(collective_id=0, has_side_effects=True),
    )(palette, substrate, catalyst, feed_rate, kill_rate, extinction)
    return pl.pallas_call(
        finish,
        out_shape=(field, field, jax.ShapeDtypeStruct((4, 16, 16), f32)),
        in_specs=[pl.BlockSpec(memory_space=pltpu.VMEM)] * 2,
        out_specs=(any_ref,) * 3,
        scratch_shapes=[pltpu.VMEM((4, 16, 16), f32), dma((3,))],
    )(*(pltpu.with_memory_space_constraint(part, pltpu.VMEM) for part in (new, parts)))


def solution(mesh):
    split = P("depth", "rows", None)
    return jax.shard_map(
        body,
        mesh=mesh,
        in_specs=(split,) * 5 + (P(),),
        out_specs=(split, split, P(None, "rows", "depth")),
        check_vma=False,
    )
```

```python
import contextlib

import jax
import jax.numpy as jnp
from jax import lax
from jax.experimental import pallas as pl
from jax.experimental.pallas import tpu as pltpu
from jax.sharding import PartitionSpec as P

mark = contextlib.nullcontext
MESH = pl.DeviceIdType.MESH
X, Y = 4, 8
CHIPS = X * Y
DEPTHS = 2 * CHIPS
ZS = 8
CT = 8
LAYERS = 4
TILE = 32
COEF = (0.16, 0.08)
FIRST = 8
GROUP = 4
HALF = CT // 2
COLLECTORS = (9, (Y // 2) * X + X // 2)
DIRECT = ((4, 2), (4, 1), (4, 3), (3, 2), (5, 2), (6, 2))
TILES = CHIPS - 1 + len(DIRECT)


def expand(tile, lane):
    light = jnp.where(lane >= 96, tile, 0.0)
    return light + pltpu.roll(light, 32, 1) + (pltpu.roll(light, 64, 1) + pltpu.roll(light, 96, 1))


def joined(near, far, lane):
    return jnp.where(lane < 96, near, 0.0) + expand(near, lane) * far


def regroup(tiles, lane):
    tiles = list(tiles)
    for bit in (1, 2, 4):
        low_half = (lane & (16 * bit)) == 0
        for g in range(8):
            if g & bit:
                continue
            low, high = tiles[g], tiles[g | bit]
            tiles[g] = jnp.where(low_half, low, pltpu.roll(high, 16 * bit, 1))
            tiles[g | bit] = jnp.where(low_half, pltpu.roll(low, 128 - 16 * bit, 1), high)
    return tiles


def kernel(palette, S, C, F, K, E, new, xr,
           s0, s1, fv, kv, ev, h0, ph, ps, r0, r1, rs0, rs1, eg, dg, mid, flat, t0, cr, x0, pal,
           load_sem, h_send, h_recv, p_send, p_recv, r0_send, r0_recv, r1_send, r1_recv,
           e_send, e_recv, g_send, g_recv, s_send, s_recv, c_send, c_recv, x_send, x_recv, everyone, ready):
    d = lax.axis_index("depth")
    z = lax.axis_index("rows")
    core = d & 1
    chip = d >> 1
    x = chip & (X - 1)
    y = chip >> 2

    def at(yy, xx, cc):
        return (yy * X + xx) * 2 + cc

    has = {"lo": d > 0, "hi": d < DEPTHS - 1, "zlo": z > 0, "zhi": z < ZS - 1}
    up, down = jnp.minimum(d + 1, DEPTHS - 1), jnp.maximum(d - 1, 0)
    zup, zdown = jnp.minimum(z + 1, ZS - 1), jnp.maximum(z - 1, 0)

    barrier = pltpu.get_barrier_semaphore()

    def signal(sem, depth, row):
        pl.semaphore_signal(sem, inc=1, device_id=(depth, row), device_id_type=MESH)

    for flag, depth, row in (("lo", down, z), ("hi", up, z), ("zhi", d, zup)):
        @pl.when(has[flag])
        def _(depth=depth, row=row):
            signal(barrier, depth, row)

    above, below = has["zlo"], has["zhi"]
    for flag, depth in (("lo", down), ("hi", up)):
        @pl.when(below & has[flag])
        def _(depth=depth):
            signal(barrier, depth, zup)
    has["above_lo"], has["above_hi"] = above & has["lo"], above & has["hi"]
    has["below_lo"], has["below_hi"] = below & has["lo"], below & has["hi"]

    collector = jnp.where(z == 0, COLLECTORS[0], COLLECTORS[1])
    collects = chip == collector
    for c in range(2):
        @pl.when(d != 2 * collector + c)
        def _(c=c):
            signal(barrier, 2 * collector + c, z)

    for ct in range(CT):
        for sp, src in ((0, S), (1, C)):
            pltpu.make_async_copy(
                src.at[:, :, pl.ds(ct * 128, 128)],
                s0.at[sp, :, pl.ds((ct + 1) * TILE + FIRST, 16), :],
                load_sem.at[sp],
            ).start()
    pal_load = pltpu.make_async_copy(palette, pal, load_sem.at[5])
    f_load = pltpu.make_async_copy(F, fv, load_sem.at[2])
    k_load = pltpu.make_async_copy(K, kv, load_sem.at[3])
    e_load = pltpu.make_async_copy(E, ev, load_sem.at[4])
    f_load.start()
    k_load.start()
    e_load.start()
    pal_load.start()

    with mark("w_barrier"):
        pl.semaphore_wait(barrier, sum(jnp.where(has[flag], 1, 0) for flag in ("lo", "hi", "zlo", "above_lo", "above_hi")) + jnp.where(collects, DEPTHS - 1, 0))

    @pl.when(has["zlo"])
    def _():
        signal(ready, d, zdown)

    @pl.when(collects)
    def _():
        def tell(i, carry):
            signal(everyone, 2 * ((chip + i) & (CHIPS - 1)) + core, z)
            return carry

        lax.fori_loop(1, CHIPS, tell, 0)

    zero = jnp.zeros((8, 128), jnp.float32)
    for sp in range(2):
        for layer in range(LAYERS):
            for buf in (s0, s1):
                for t in (0, CT + 1):
                    for rb in range(2):
                        buf[sp, layer, pl.ds(t * TILE + FIRST + 8 * rb, 8), :] = zero
            for row in (FIRST - 1, FIRST + 16):
                s0[sp, layer, pl.ds(TILE + row, CT, stride=TILE), :] = zero
    clear = jnp.where(lax.broadcasted_iota(jnp.int32, (8, 128), 1) < 96, 0.0, 1.0)
    for away in range(Y):
        for across in range(X):
            if (away, across) not in DIRECT:
                xr[CHIPS + ((y - away) & (Y - 1)) * X + ((x - across) & (X - 1))] = clear
    for side, flag in ((0, "lo"), (1, "hi")):
        @pl.when(jnp.logical_not(has[flag]))
        def _(side=side):
            for sp in range(2):
                eg[side, 0, sp] = zero
                dg[side, 1, sp] = zero

                def fill(i, carry):
                    h0[side, sp, :, pl.ds(i * 128, 128)] = jnp.zeros((16, 128), jnp.float32)
                    ph[side, i // HALF, sp, pl.ds((i % HALF) * 16, 16), :] = jnp.zeros((16, 128), jnp.float32)
                    return carry

                lax.fori_loop(0, CT, fill, 0)
    for side, flag in ((0, "zlo"), (1, "zhi")):
        @pl.when(jnp.logical_not(has[flag]))
        def _(side=side):
            for sp in range(2):
                for layer in range(LAYERS):
                    r0[side, sp, layer] = zero
                    r1[side, sp, layer] = zero
                for depthside in range(2):
                    dg[depthside, side, sp] = zero

    def remote(src, dst, send, recv, depth, row):
        return pltpu.make_async_remote_copy(
            src_ref=src, dst_ref=dst, send_sem=send, recv_sem=recv,
            device_id=(depth, row), device_id_type=MESH)

    def depth_copy(kind, side, sp):
        target = up if side == 0 else down
        if kind == "h":
            src = (S, C)[sp].at[LAYERS - 1 if side == 0 else 0]
            return remote(src, h0.at[side, sp], h_send.at[side], h_recv.at[side], target, z)
        if kind == "both":
            return remote(h0.at[side], h0.at[side], h_send.at[side], h_recv.at[side], target, z)
        if kind == "halves":
            return remote(ps.at[side], ph.at[side], p_send.at[side], p_recv.at[side, 0], target, z)
        if kind == "p":
            half = sp
            return remote(ps.at[side, half], ph.at[side, half], p_send.at[side], p_recv.at[side, half], target, z)
        if kind == "straight":
            return remote(rs0.at[1, :, LAYERS - 1 if side == 0 else 0], dg.at[side, 1],
                          s_send.at[side], s_recv.at[side], target, zdown)
        return remote(rs0.at[0:1, :, LAYERS - 1 if side == 0 else 0], eg.at[side],
                      e_send.at[side], e_recv.at[side], target, z)

    def row_copy(kind, side):
        target = zup if side == 0 else zdown
        if kind == "0":
            return remote(rs0.at[side], r0.at[side], r0_send.at[side], r0_recv.at[side], d, target)
        if kind == "corner":
            return remote(eg.at[:, 0], dg.at[:, 0], g_send, g_recv, d, target)
        return remote(rs1.at[side], r1.at[side], r1_send.at[side], r1_recv.at[side], d, target)

    to = ("hi", "lo")
    source = ("lo", "hi")
    zto = ("zhi", "zlo")
    zsource = ("zlo", "zhi")

    def each(flag, copies, what):
        @pl.when(has[flag])
        def _():
            for copy in copies:
                getattr(copy, what)()

    with mark("w_load"):
        for sp in range(2):
            whole = s0.at[sp, :, pl.ds(0, CT * 16), :]
            pltpu.make_async_copy(whole, whole, load_sem.at[sp]).wait()
    for side in range(2):
        row = TILE + FIRST + (15 if side == 0 else 0)
        for sp in range(2):
            for layer in range(LAYERS):
                rs0[side, sp, layer] = s0[sp, layer, pl.ds(row, CT, stride=TILE), :]
    for side in range(2):
        each("above_" + to[side], [depth_copy("straight", side, 0)], "start")
    for side in range(2):
        each(to[side], [depth_copy("edge", side, 0)] + [depth_copy("h", side, sp) for sp in range(2)], "start")
    each("zlo", [row_copy("0", 1)], "start")

    with mark("w_loadfk"):
        f_load.wait()
        k_load.wait()

    lane = lax.broadcasted_iota(jnp.int32, (8, 128), 1)

    def in_groups(step):
        def group(g, carry):
            for q in range(GROUP):
                step(g * GROUP + q, carry)
            return carry

        lax.fori_loop(0, CT // GROUP, group, 0)

    def start_of(ct, rb):
        return pl.multiple_of((ct + 1) * TILE + FIRST + 8 * rb, 8)

    def centre(buf, sp, layer, ct, rb):
        return buf[sp, layer, pl.ds(start_of(ct, rb), 8), :]

    def around(buf, sp, layer, ct, rb):
        here = centre(buf, sp, layer, ct, rb)
        left = centre(buf, sp, layer, ct - 1, rb)
        right = centre(buf, sp, layer, ct + 1, rb)
        total = pltpu.roll(jnp.where(lane == 127, left, here), 1, 1)
        total += pltpu.roll(jnp.where(lane == 0, right, here), 127, 1)
        base = start_of(ct, rb)
        total += buf[sp, layer, pl.ds(base - 1, 8), :]
        total += buf[sp, layer, pl.ds(base + 1, 8), :]
        return here, total

    def native(ref, layer, ct, rb):
        return ref[layer, pl.ds(8 * rb, 8), pl.ds(pl.multiple_of(ct * 128, 128), 128)]

    def react(s, c, around_s, around_c, layer, ct, rb):
        feed = native(fv, layer, ct, rb)
        kill = native(kv, layer, ct, rb)
        feed = feed + feed
        reaction = s * c * c
        reaction = reaction + reaction
        new_s = COEF[0] * around_s + (feed + s * (0.04 - feed)) - reaction
        new_c = COEF[1] * around_c + c * (0.52 - feed - (kill + kill)) + reaction
        return new_s, new_c

    def first(layers):
        def body(ct, carry):
            for layer in layers:
                for rb in range(2):
                    values = []
                    for sp in range(2):
                        here, total = around(s0, sp, layer, ct, rb)
                        if layer > 0:
                            total += centre(s0, sp, layer - 1, ct, rb)
                        if layer < LAYERS - 1:
                            total += centre(s0, sp, layer + 1, ct, rb)
                        values.append((here, total))
                    result = react(values[0][0], values[1][0], values[0][1], values[1][1], layer, ct, rb)
                    for sp in range(2):
                        s1[sp, layer, pl.ds(start_of(ct, rb), 8), :] = result[sp]
                        for side, edge, target in ((0, LAYERS - 1, up), (1, 0, down)):
                            if layer == edge:
                                place = (ct - (target >> 3) + (Y - 2)) & (Y - 1)
                                rows = pl.multiple_of((place & (HALF - 1)) * 16 + 8 * rb, 8)
                                ps[side, place >> 2, sp, pl.ds(rows, 8), :] = result[sp]
            return carry

        in_groups(body)

    with mark("first03"):
        first((0, LAYERS - 1))
    for side in range(2):
        each(to[side], [depth_copy("p", side, half) for half in range(2)], "start")
    with mark("first12"):
        first(range(1, LAYERS - 1))
    for side in range(2):
        row = TILE + FIRST + (15 if side == 0 else 0)
        for sp in range(2):
            for layer in range(LAYERS):
                rs1[side, sp, layer] = s1[sp, layer, pl.ds(row, CT, stride=TILE), :]
    each("zlo", [row_copy("1", 1)], "start")
    with mark("w_readyz"):
        @pl.when(has["zhi"])
        def _():
            pl.semaphore_wait(ready, 1)
            for kind in ("0", "1"):
                row_copy(kind, 0).start()

    with mark("w_edge"):
        for side in range(2):
            each(source[side], [depth_copy("edge", side, 0)], "wait_recv")
    each("zhi", [row_copy("corner", 0)], "start")

    with mark("w_row0"):
        for side in range(2):
            each(zsource[side], [row_copy("0", side)], "wait_recv")

    scale = {flag: jnp.where(has[flag], 1.0, 0.0).astype(jnp.float32) for flag in source + zsource}
    for side in range(2):
        row = TILE + FIRST + (0 if side == 0 else 15)
        for sp in range(2):
            for layer in range(LAYERS):
                where = pl.ds(row, CT, stride=TILE)
                s1[sp, layer, where, :] = s1[sp, layer, where, :] + COEF[sp] * r0[side, sp, layer]
    with mark("w_row1"):
        for side in range(2):
            each(zsource[side], [row_copy("1", side)], "wait_recv")
    for side in range(2):
        edge = TILE + FIRST + (0 if side == 0 else 15)
        outside = TILE + FIRST + (-1 if side == 0 else 16)
        for sp in range(2):
            factor = COEF[sp] * scale[zsource[side]]
            for layer in range(LAYERS):
                s1[sp, layer, pl.ds(outside, CT, stride=TILE), :] = (
                    r1[side, sp, layer] + factor * s0[sp, layer, pl.ds(edge, CT, stride=TILE), :])

    with mark("w_h"):
        for side in range(2):
            each(source[side], [depth_copy("both", side, 0)], "wait_recv")

    def add_layers(ct, carry):
        for side, layer in ((0, 0), (1, LAYERS - 1)):
            for sp in range(2):
                for rb in range(2):
                    where = pl.ds(start_of(ct, rb), 8)
                    halo = h0[side, sp, pl.ds(8 * rb, 8), pl.ds(pl.multiple_of(ct * 128, 128), 128)]
                    s1[sp, layer, where, :] = s1[sp, layer, where, :] + COEF[sp] * halo
        return carry

    with mark("addlayers"):
        in_groups(add_layers)

    e_load.wait()
    pal_load.wait()
    weights = []
    for k in range(3):
        a, b = -8.0 * pal[k, 0], -8.0 * pal[k, 1]
        weights.append((a, b, -pal[k, 2] - 0.65 * a - 0.25 * b))

    def columns_of(ct):
        return pl.ds(pl.multiple_of(ct * 128, 128), 128)

    def second(layer, ct, rb):
        values = []
        for sp in range(2):
            here, total = around(s1, sp, layer, ct, rb)
            if layer > 0:
                total += centre(s1, sp, layer - 1, ct, rb)
            else:
                total += (COEF[sp] * scale["lo"]) * centre(s0, sp, 0, ct, rb)
            if layer < LAYERS - 1:
                total += centre(s1, sp, layer + 1, ct, rb)
            else:
                total += (COEF[sp] * scale["hi"]) * centre(s0, sp, LAYERS - 1, ct, rb)
            values.append((here, total))
        return react(values[0][0], values[1][0], values[0][1], values[1][1], layer, ct, rb)

    def shade(s, c, layer, ct, rb):
        new[0, layer, pl.ds(8 * rb, 8), columns_of(ct)] = s
        new[1, layer, pl.ds(8 * rb, 8), columns_of(ct)] = c
        passing = jnp.exp(-native(ev, layer, ct, rb) * (0.25 + 4.0 * c * c))
        opacity = 1.0 - passing
        colors = [opacity / (1.0 + jnp.exp(a * s + b * c + e)) for a, b, e in weights]
        return colors, passing

    def middle(ct, carry):
        for rb in range(2):
            rows = pl.ds(pl.multiple_of(ct * 16 + 8 * rb, 8), 8)
            near, light = shade(*second(1, ct, rb), 1, ct, rb)
            far, light_far = shade(*second(2, ct, rb), 2, ct, rb)
            for k in range(3):
                mid[k, rows, :] = near[k] + light * far[k]
            mid[3, rows, :] = light * light_far
        return carry

    with mark("middle"):
        in_groups(middle)

    def open_ends(ct, carry):
        for layer in (0, LAYERS - 1):
            for rb in range(2):
                for sp, value in enumerate(second(layer, ct, rb)):
                    new[sp, layer, pl.ds(8 * rb, 8), columns_of(ct)] = value
        return carry

    with mark("open_ends"):
        in_groups(open_ends)

    with mark("w_diag"):
        for side in range(2):
            each("below_" + source[side], [depth_copy("straight", side, 0)], "wait_recv")
        each("zlo", [row_copy("corner", 0)], "wait_recv")
    corner = {}
    for side in range(2):
        for rowside in range(2):
            for sp in range(2):
                corner[side, rowside, sp] = pltpu.roll(dg[side, rowside, sp], (Y - 2 - y) & (Y - 1), 0) * (2.0 * COEF[sp])

    def add_corners(half):
        for (side, rowside, sp), rows in corner.items():
            where = pl.ds(15 * rowside, HALF, stride=16)
            ph[side, half, sp, where, :] = ph[side, half, sp, where, :] + rows[half * HALF:half * HALF + HALF]

    partner = d + 1 - 2 * core

    def core_copy(g):
        some = pl.ds(g * HALF * X, HALF * X)
        return remote(t0.at[1 - core, some], cr.at[some], c_send.at[g], c_recv.at[g], partner, z)

    def ends(g):
        with mark(f"w_p{g}"):
            for side in range(2):
                each(source[side], [depth_copy("p", side, g)], "wait_recv")
        add_corners(g)
        for q in range(HALF):
            place = g * HALF + q
            ct = (y + place + 2) & (Y - 1)
            for rb in range(2):
                parts = []
                for side, layer in ((0, 0), (1, LAYERS - 1)):
                    values = [new[sp, layer, pl.ds(8 * rb, 8), columns_of(ct)]
                              + COEF[sp] * ph[side, g, sp, pl.ds(q * 16 + 8 * rb, 8), :] for sp in range(2)]
                    parts.append(shade(*values, layer, ct, rb))
                (near, light), (far, light_far) = parts
                rows = pl.ds(pl.multiple_of(ct * 16 + 8 * rb, 8), 8)
                light_mid = light * mid[3, rows, :]
                for k in range(3):
                    flat[place * 8 + 2 * k + rb] = near[k] + light * mid[k, rows, :] + light_mid * far[k]
                flat[place * 8 + 6 + rb] = light_mid * light_far
        for place in range(g * HALF, g * HALF + HALF):
            for j, tile in enumerate(regroup([flat[place * 8 + i] for i in range(8)], lane)):
                t0[j % 2, place * X + j // 2] = tile
        core_copy(g).start()
        for away, across in DIRECT:
            place = (away - 2) % Y
            if place // HALF == g:
                yy, xx = (y + away) & (Y - 1), (x + across) & (X - 1)
                for c in range(2):
                    remote(t0.at[c, place * X + xx], xr.at[CHIPS * core + chip], x_send, x_recv, at(yy, xx, c), z).start()

    with mark("w_everyone"):
        @pl.when(jnp.logical_not(collects))
        def _():
            pl.semaphore_wait(everyone, 1)

    for g in range(2):
        with mark(f"ends{g}"):
            ends(g)

    def chip_copy(place, away, across):
        xx = (x + across) & (X - 1)
        return remote(x0.at[place * X + xx], xr.at[chip], x_send, x_recv, at((y + away) & (Y - 1), xx, core), z)

    def merge(g):
        core_copy(g).wait_recv()
        for i in range(g * HALF * X, (g + 1) * HALF * X):
            mine, other = t0[core, i], cr[i]
            x0[i] = joined(jnp.where(core == 0, mine, other), jnp.where(core == 0, other, mine), lane)
        for away in ((4, 3, 5, 2), (6, 1, 7, 0))[g]:
            for across in (2, 1, 3, 0):
                if (away or across) and (away, across) not in DIRECT:
                    chip_copy((away - 2) % Y, away, across).start()

    for g in range(2):
        with mark(f"merge{g}"):
            merge(g)
    for side in range(2):
        each(to[side], [depth_copy(kind, side, 0) for kind in ("edge", "both", "halves")], "wait_send")
        each("above_" + to[side], [depth_copy("straight", side, 0)], "wait_send")
        each(zto[side], [row_copy(kind, side) for kind in ("0", "1")], "wait_send")
    each("zhi", [row_copy("corner", 0)], "wait_send")
    for g in range(2):
        core_copy(g).wait_send()
    xr[chip] = x0[(Y - 2) * X + x]
    arrived = xr.at[pl.ds(0, TILES)]
    with mark("w_xy"):
        pltpu.make_async_copy(arrived, arrived, x_recv).wait()
    pltpu.make_async_copy(arrived, arrived, x_send).wait()


def finish(new, xr, out_s, out_c, out_image, img, out_sem):
    copies = [pltpu.make_async_copy(new.at[0], out_s, out_sem.at[0]),
              pltpu.make_async_copy(new.at[1], out_c, out_sem.at[1])]
    for copy in copies:
        copy.start()
    last = pltpu.make_async_copy(img, out_image, out_sem.at[2])

    def compose(once, carry):
        lane = lax.broadcasted_iota(jnp.int32, (8, 128), 1)
        pieces = []
        for first in range(0, CHIPS, HALF):
            total, light = None, None
            for i in range(first, first + HALF):
                for c in range(2):
                    tile = xr[c * CHIPS + i]
                    color = jnp.where(lane < 96, tile, 0.0)
                    passing = expand(tile, lane)
                    total = color if total is None else total + light * color
                    light = passing if light is None else light * passing
            pieces.append((total, light))
        while len(pieces) > 1:
            pieces = [(near + light * far, light * light_far)
                      for (near, light), (far, light_far) in zip(pieces[::2], pieces[1::2])]
        total, light = pieces[0]
        tile = jnp.where(lane < 96, total, 1.0 - light)
        for g in range(8):
            part = tile if g == 0 else pltpu.roll(tile, 128 - 16 * g, 1)
            img[g // 2, pl.ds(8 * (g % 2), 8), :] = part[:, :16]
        last.start()
        return carry

    lax.fori_loop(0, 1 + (lax.axis_index("depth") >> 6), compose, 0)
    for copy in copies + [last]:
        copy.wait()


def body(substrate, catalyst, feed_rate, kill_rate, extinction, palette):
    field = jax.ShapeDtypeStruct(substrate.shape, jnp.float32)
    any_ref = pl.BlockSpec(memory_space=pl.ANY)
    f32 = jnp.float32
    dma = pltpu.SemaphoreType.DMA
    new, parts = pl.pallas_call(
        kernel,
        out_shape=(pltpu.VMEM((2,) + field.shape, f32), pltpu.VMEM((2 * CHIPS, 8, 128), f32)),
        in_specs=[any_ref] * 6,
        out_specs=(pl.BlockSpec(memory_space=pltpu.VMEM),) * 2,
        scratch_shapes=[
            pltpu.VMEM((2, LAYERS, (CT + 2) * TILE, 128), f32),
            pltpu.VMEM((2, LAYERS, (CT + 2) * TILE, 128), f32),
            pltpu.VMEM((LAYERS, 16, CT * 128), f32),
            pltpu.VMEM((LAYERS, 16, CT * 128), f32),
            pltpu.VMEM((LAYERS, 16, CT * 128), f32),
            pltpu.VMEM((2, 2, 16, CT * 128), f32),
            pltpu.VMEM((2, 2, 2, HALF * 16, 128), f32),
            pltpu.VMEM((2, 2, 2, HALF * 16, 128), f32),
            pltpu.VMEM((2, 2, LAYERS, CT, 128), f32),
            pltpu.VMEM((2, 2, LAYERS, CT, 128), f32),
            pltpu.VMEM((2, 2, LAYERS, CT, 128), f32),
            pltpu.VMEM((2, 2, LAYERS, CT, 128), f32),
            pltpu.VMEM((2, 1, 2, CT, 128), f32),
            pltpu.VMEM((2, 2, 2, CT, 128), f32),
            pltpu.VMEM((4, CT * 16, 128), f32),
            pltpu.VMEM((CT * 8, 8, 128), f32),
            pltpu.VMEM((2, CHIPS, 8, 128), f32),
            pltpu.VMEM((CHIPS, 8, 128), f32),
            pltpu.VMEM((CHIPS, 8, 128), f32),
            pltpu.SMEM((3, 3), f32),
            dma((6,)),
            dma((2,)), dma((2,)), dma((2,)), dma((2, 2)),
            dma((2,)), dma((2,)), dma((2,)), dma((2,)),
            dma((2,)), dma((2,)), dma, dma, dma((2,)), dma((2,)),
            dma((2,)), dma((2,)), dma, dma,
            pltpu.SemaphoreType.REGULAR, pltpu.SemaphoreType.REGULAR,
        ],
        compiler_params=pltpu.CompilerParams(collective_id=0, has_side_effects=True),
    )(palette, substrate, catalyst, feed_rate, kill_rate, extinction)
    return pl.pallas_call(
        finish,
        out_shape=(field, field, jax.ShapeDtypeStruct((4, 16, 16), f32)),
        in_specs=[pl.BlockSpec(memory_space=pltpu.VMEM)] * 2,
        out_specs=(any_ref,) * 3,
        scratch_shapes=[pltpu.VMEM((4, 16, 16), f32), dma((3,))],
    )(*(pltpu.with_memory_space_constraint(part, pltpu.VMEM) for part in (new, parts)))


def solution(mesh):
    split = P("depth", "rows", None)
    return jax.shard_map(
        body,
        mesh=mesh,
        in_specs=(split,) * 5 + (P(),),
        out_specs=(split, split, P(None, "rows", "depth")),
        check_vma=False,
    )
```

```python
import contextlib

import jax
import jax.numpy as jnp
from jax import lax
from jax.experimental import pallas as pl
from jax.experimental.pallas import tpu as pltpu
from jax.sharding import PartitionSpec as P

mark = contextlib.nullcontext
MESH = pl.DeviceIdType.MESH
X, Y = 4, 8
CHIPS = X * Y
DEPTHS = 2 * CHIPS
ZS = 8
CT = 8
LAYERS = 4
TILE = 32
COEF = (0.16, 0.08)
FIRST = 8
GROUP = 4
HALF = CT // 2
COLLECTORS = (10, (Y // 2) * X + X // 2)
DIRECT = ((4, 2), (4, 1), (4, 3), (3, 2), (5, 2))
TILES = CHIPS - 1 + len(DIRECT)


def expand(tile, lane):
    light = jnp.where(lane >= 96, tile, 0.0)
    return light + pltpu.roll(light, 32, 1) + (pltpu.roll(light, 64, 1) + pltpu.roll(light, 96, 1))


def joined(near, far, lane):
    return jnp.where(lane < 96, near, 0.0) + expand(near, lane) * far


def regroup(tiles, lane):
    tiles = list(tiles)
    for bit in (1, 2, 4):
        low_half = (lane & (16 * bit)) == 0
        for g in range(8):
            if g & bit:
                continue
            low, high = tiles[g], tiles[g | bit]
            tiles[g] = jnp.where(low_half, low, pltpu.roll(high, 16 * bit, 1))
            tiles[g | bit] = jnp.where(low_half, pltpu.roll(low, 128 - 16 * bit, 1), high)
    return tiles


def kernel(palette, S, C, F, K, E, new, xr,
           s0, s1, fv, kv, ev, h0, ph, ps, r0, r1, rs0, rs1, eg, dg, mid, flat, t0, cr, x0, pal,
           load_sem, sent, h_recv, p_recv, r0_recv, r1_recv,
           e_recv, g_recv, s_recv, c_recv, x_send, x_recv, everyone, ready):
    d = lax.axis_index("depth")
    z = lax.axis_index("rows")
    core = d & 1
    chip = d >> 1
    x = chip & (X - 1)
    y = chip >> 2

    def at(yy, xx, cc):
        return (yy * X + xx) * 2 + cc

    has = {"lo": d > 0, "hi": d < DEPTHS - 1, "zlo": z > 0, "zhi": z < ZS - 1}
    up, down = jnp.minimum(d + 1, DEPTHS - 1), jnp.maximum(d - 1, 0)
    zup, zdown = jnp.minimum(z + 1, ZS - 1), jnp.maximum(z - 1, 0)

    barrier = pltpu.get_barrier_semaphore()

    def signal(sem, depth, row):
        pl.semaphore_signal(sem, inc=1, device_id=(depth, row), device_id_type=MESH)

    for flag, depth, row in (("lo", down, z), ("hi", up, z), ("zhi", d, zup)):
        @pl.when(has[flag])
        def _(depth=depth, row=row):
            signal(barrier, depth, row)

    above, below = has["zlo"], has["zhi"]
    for flag, depth in (("lo", down), ("hi", up)):
        @pl.when(below & has[flag])
        def _(depth=depth):
            signal(barrier, depth, zup)
    has["above_lo"], has["above_hi"] = above & has["lo"], above & has["hi"]
    has["below_lo"], has["below_hi"] = below & has["lo"], below & has["hi"]

    collector = jnp.where(z == 0, COLLECTORS[0], COLLECTORS[1])
    collects = chip == collector
    for c in range(2):
        @pl.when(d != 2 * collector + c)
        def _(c=c):
            signal(barrier, 2 * collector + c, z)

    for ct in range(CT):
        for sp, src in ((0, S), (1, C)):
            pltpu.make_async_copy(
                src.at[:, :, pl.ds(ct * 128, 128)],
                s0.at[sp, :, pl.ds((ct + 1) * TILE + FIRST, 16), :],
                load_sem.at[sp],
            ).start()
    pal_load = pltpu.make_async_copy(palette, pal, load_sem.at[5])
    f_load = pltpu.make_async_copy(F, fv, load_sem.at[2])
    k_load = pltpu.make_async_copy(K, kv, load_sem.at[3])
    e_load = pltpu.make_async_copy(E, ev, load_sem.at[4])
    f_load.start()
    k_load.start()
    e_load.start()
    pal_load.start()

    with mark("w_barrier"):
        pl.semaphore_wait(barrier, sum(jnp.where(has[flag], 1, 0) for flag in ("lo", "hi", "zlo", "above_lo", "above_hi")) + jnp.where(collects, DEPTHS - 1, 0))

    @pl.when(has["zlo"])
    def _():
        signal(ready, d, zdown)

    def tell():
        def one(i, carry):
            signal(everyone, 2 * ((chip + i) & (CHIPS - 1)) + core, z)
            return carry

        lax.fori_loop(1, CHIPS, one, 0)

    @pl.when(collects & (z == 0))
    def _():
        tell()

    zero = jnp.zeros((8, 128), jnp.float32)
    for sp in range(2):
        for layer in range(LAYERS):
            for buf in (s0, s1):
                for t in (0, CT + 1):
                    for rb in range(2):
                        buf[sp, layer, pl.ds(t * TILE + FIRST + 8 * rb, 8), :] = zero
            for row in (FIRST - 1, FIRST + 16):
                s0[sp, layer, pl.ds(TILE + row, CT, stride=TILE), :] = zero
    clear = jnp.where(lax.broadcasted_iota(jnp.int32, (8, 128), 1) < 96, 0.0, 1.0)
    for away in range(Y):
        for across in range(X):
            if (away, across) not in DIRECT:
                xr[CHIPS + ((y - away) & (Y - 1)) * X + ((x - across) & (X - 1))] = clear
    for side, flag in ((0, "lo"), (1, "hi")):
        @pl.when(jnp.logical_not(has[flag]))
        def _(side=side):
            for sp in range(2):
                eg[side, 0, sp] = zero
                dg[side, 1, sp] = zero

                def fill(i, carry):
                    h0[side, sp, :, pl.ds(i * 128, 128)] = jnp.zeros((16, 128), jnp.float32)
                    ph[side, i // HALF, sp, pl.ds((i % HALF) * 16, 16), :] = jnp.zeros((16, 128), jnp.float32)
                    return carry

                lax.fori_loop(0, CT, fill, 0)
    for side, flag in ((0, "zlo"), (1, "zhi")):
        @pl.when(jnp.logical_not(has[flag]))
        def _(side=side):
            for sp in range(2):
                for layer in range(LAYERS):
                    r0[side, sp, layer] = zero
                    r1[side, sp, layer] = zero
                for depthside in range(2):
                    dg[depthside, side, sp] = zero

    def remote(src, dst, send, recv, depth, row):
        return pltpu.make_async_remote_copy(
            src_ref=src, dst_ref=dst, send_sem=send, recv_sem=recv,
            device_id=(depth, row), device_id_type=MESH)

    def depth_copy(kind, side, sp):
        target = up if side == 0 else down
        if kind == "h":
            src = (S, C)[sp].at[LAYERS - 1 if side == 0 else 0]
            return remote(src, h0.at[side, sp], sent, h_recv.at[side], target, z)
        if kind == "both":
            return remote(h0.at[side], h0.at[side], sent, h_recv.at[side], target, z)
        if kind == "halves":
            return remote(ps.at[side], ph.at[side], sent, p_recv.at[side, 0], target, z)
        if kind == "p":
            half = sp
            return remote(ps.at[side, half], ph.at[side, half], sent, p_recv.at[side, half], target, z)
        if kind == "straight":
            return remote(rs0.at[1, :, LAYERS - 1 if side == 0 else 0], dg.at[side, 1],
                          sent, s_recv.at[side], target, zdown)
        return remote(rs0.at[0:1, :, LAYERS - 1 if side == 0 else 0], eg.at[side],
                      sent, e_recv.at[side], target, z)

    def row_copy(kind, side):
        target = zup if side == 0 else zdown
        if kind == "0":
            return remote(rs0.at[side], r0.at[side], sent, r0_recv.at[side], d, target)
        if kind == "corner":
            return remote(eg.at[:, 0], dg.at[:, 0], sent, g_recv, d, target)
        return remote(rs1.at[side], r1.at[side], sent, r1_recv.at[side], d, target)

    to = ("hi", "lo")
    source = ("lo", "hi")
    zto = ("zhi", "zlo")
    zsource = ("zlo", "zhi")

    def each(flag, copies, what):
        @pl.when(has[flag])
        def _():
            for copy in copies:
                getattr(copy, what)()

    with mark("w_load"):
        for sp in range(2):
            whole = s0.at[sp, :, pl.ds(0, CT * 16), :]
            pltpu.make_async_copy(whole, whole, load_sem.at[sp]).wait()
    for side in range(2):
        row = TILE + FIRST + (15 if side == 0 else 0)
        for sp in range(2):
            for layer in range(LAYERS):
                rs0[side, sp, layer] = s0[sp, layer, pl.ds(row, CT, stride=TILE), :]
    for side in range(2):
        each("above_" + to[side], [depth_copy("straight", side, 0)], "start")
    for side in range(2):
        each(to[side], [depth_copy("edge", side, 0)] + [depth_copy("h", side, sp) for sp in range(2)], "start")
    each("zlo", [row_copy("0", 1)], "start")

    @pl.when(collects & (z > 0))
    def _():
        tell()

    with mark("w_loadfk"):
        f_load.wait()
        k_load.wait()

    lane = lax.broadcasted_iota(jnp.int32, (8, 128), 1)

    def in_groups(step):
        def group(g, carry):
            for q in range(GROUP):
                step(g * GROUP + q, carry)
            return carry

        lax.fori_loop(0, CT // GROUP, group, 0)

    def start_of(ct, rb):
        return pl.multiple_of((ct + 1) * TILE + FIRST + 8 * rb, 8)

    def centre(buf, sp, layer, ct, rb):
        return buf[sp, layer, pl.ds(start_of(ct, rb), 8), :]

    def around(buf, sp, layer, ct, rb):
        here = centre(buf, sp, layer, ct, rb)
        left = centre(buf, sp, layer, ct - 1, rb)
        right = centre(buf, sp, layer, ct + 1, rb)
        total = pltpu.roll(jnp.where(lane == 127, left, here), 1, 1)
        total += pltpu.roll(jnp.where(lane == 0, right, here), 127, 1)
        base = start_of(ct, rb)
        total += buf[sp, layer, pl.ds(base - 1, 8), :]
        total += buf[sp, layer, pl.ds(base + 1, 8), :]
        return here, total

    def native(ref, layer, ct, rb):
        return ref[layer, pl.ds(8 * rb, 8), pl.ds(pl.multiple_of(ct * 128, 128), 128)]

    def react(s, c, around_s, around_c, layer, ct, rb):
        feed = native(fv, layer, ct, rb)
        kill = native(kv, layer, ct, rb)
        feed = feed + feed
        reaction = s * c * c
        reaction = reaction + reaction
        new_s = COEF[0] * around_s + (feed + s * (0.04 - feed)) - reaction
        new_c = COEF[1] * around_c + c * (0.52 - feed - (kill + kill)) + reaction
        return new_s, new_c

    def first(layers):
        def body(ct, carry):
            for layer in layers:
                for rb in range(2):
                    values = []
                    for sp in range(2):
                        here, total = around(s0, sp, layer, ct, rb)
                        if layer > 0:
                            total += centre(s0, sp, layer - 1, ct, rb)
                        if layer < LAYERS - 1:
                            total += centre(s0, sp, layer + 1, ct, rb)
                        values.append((here, total))
                    result = react(values[0][0], values[1][0], values[0][1], values[1][1], layer, ct, rb)
                    for sp in range(2):
                        s1[sp, layer, pl.ds(start_of(ct, rb), 8), :] = result[sp]
                        for side, edge, target in ((0, LAYERS - 1, up), (1, 0, down)):
                            if layer == edge:
                                place = (ct - (target >> 3) + (Y - 2)) & (Y - 1)
                                rows = pl.multiple_of((place & (HALF - 1)) * 16 + 8 * rb, 8)
                                ps[side, place >> 2, sp, pl.ds(rows, 8), :] = result[sp]
            return carry

        in_groups(body)

    with mark("first03"):
        first((0, LAYERS - 1))
    for side in range(2):
        each(to[side], [depth_copy("p", side, half) for half in range(2)], "start")
    with mark("first12"):
        first(range(1, LAYERS - 1))
    for side in range(2):
        row = TILE + FIRST + (15 if side == 0 else 0)
        for sp in range(2):
            for layer in range(LAYERS):
                rs1[side, sp, layer] = s1[sp, layer, pl.ds(row, CT, stride=TILE), :]
    each("zlo", [row_copy("1", 1)], "start")
    with mark("w_readyz"):
        @pl.when(has["zhi"])
        def _():
            pl.semaphore_wait(ready, 1)
            for kind in ("0", "1"):
                row_copy(kind, 0).start()

    with mark("w_edge"):
        for side in range(2):
            each(source[side], [depth_copy("edge", side, 0)], "wait_recv")
    each("zhi", [row_copy("corner", 0)], "start")

    with mark("w_row0"):
        for side in range(2):
            each(zsource[side], [row_copy("0", side)], "wait_recv")

    scale = {flag: jnp.where(has[flag], 1.0, 0.0).astype(jnp.float32) for flag in source + zsource}
    for side in range(2):
        row = TILE + FIRST + (0 if side == 0 else 15)
        for sp in range(2):
            for layer in range(LAYERS):
                where = pl.ds(row, CT, stride=TILE)
                s1[sp, layer, where, :] = s1[sp, layer, where, :] + COEF[sp] * r0[side, sp, layer]
    with mark("w_row1"):
        for side in range(2):
            each(zsource[side], [row_copy("1", side)], "wait_recv")
    for side in range(2):
        edge = TILE + FIRST + (0 if side == 0 else 15)
        outside = TILE + FIRST + (-1 if side == 0 else 16)
        for sp in range(2):
            factor = COEF[sp] * scale[zsource[side]]
            for layer in range(LAYERS):
                s1[sp, layer, pl.ds(outside, CT, stride=TILE), :] = (
                    r1[side, sp, layer] + factor * s0[sp, layer, pl.ds(edge, CT, stride=TILE), :])

    with mark("w_h"):
        for side in range(2):
            each(source[side], [depth_copy("both", side, 0)], "wait_recv")

    def add_layers(ct, carry):
        for side, layer in ((0, 0), (1, LAYERS - 1)):
            for sp in range(2):
                for rb in range(2):
                    where = pl.ds(start_of(ct, rb), 8)
                    halo = h0[side, sp, pl.ds(8 * rb, 8), pl.ds(pl.multiple_of(ct * 128, 128), 128)]
                    s1[sp, layer, where, :] = s1[sp, layer, where, :] + COEF[sp] * halo
        return carry

    with mark("addlayers"):
        in_groups(add_layers)

    e_load.wait()
    pal_load.wait()
    weights = []
    for k in range(3):
        a, b = -8.0 * pal[k, 0], -8.0 * pal[k, 1]
        weights.append((a, b, -pal[k, 2] - 0.65 * a - 0.25 * b))

    def columns_of(ct):
        return pl.ds(pl.multiple_of(ct * 128, 128), 128)

    def second(layer, ct, rb):
        values = []
        for sp in range(2):
            here, total = around(s1, sp, layer, ct, rb)
            if layer > 0:
                total += centre(s1, sp, layer - 1, ct, rb)
            else:
                total += (COEF[sp] * scale["lo"]) * centre(s0, sp, 0, ct, rb)
            if layer < LAYERS - 1:
                total += centre(s1, sp, layer + 1, ct, rb)
            else:
                total += (COEF[sp] * scale["hi"]) * centre(s0, sp, LAYERS - 1, ct, rb)
            values.append((here, total))
        return react(values[0][0], values[1][0], values[0][1], values[1][1], layer, ct, rb)

    def shade(s, c, layer, ct, rb):
        new[0, layer, pl.ds(8 * rb, 8), columns_of(ct)] = s
        new[1, layer, pl.ds(8 * rb, 8), columns_of(ct)] = c
        passing = jnp.exp(-native(ev, layer, ct, rb) * (0.25 + 4.0 * c * c))
        opacity = 1.0 - passing
        colors = [opacity / (1.0 + jnp.exp(a * s + b * c + e)) for a, b, e in weights]
        return colors, passing

    def middle(ct, carry):
        for rb in range(2):
            rows = pl.ds(pl.multiple_of(ct * 16 + 8 * rb, 8), 8)
            near, light = shade(*second(1, ct, rb), 1, ct, rb)
            far, light_far = shade(*second(2, ct, rb), 2, ct, rb)
            for k in range(3):
                mid[k, rows, :] = near[k] + light * far[k]
            mid[3, rows, :] = light * light_far
        return carry

    with mark("middle"):
        in_groups(middle)

    def open_ends(ct, carry):
        for layer in (0, LAYERS - 1):
            for rb in range(2):
                for sp, value in enumerate(second(layer, ct, rb)):
                    new[sp, layer, pl.ds(8 * rb, 8), columns_of(ct)] = value
        return carry

    with mark("open_ends"):
        in_groups(open_ends)

    with mark("w_diag"):
        for side in range(2):
            each("below_" + source[side], [depth_copy("straight", side, 0)], "wait_recv")
        each("zlo", [row_copy("corner", 0)], "wait_recv")
    corner = {}
    for side in range(2):
        for rowside in range(2):
            for sp in range(2):
                corner[side, rowside, sp] = pltpu.roll(dg[side, rowside, sp], (Y - 2 - y) & (Y - 1), 0) * (2.0 * COEF[sp])

    def add_corners(half):
        for (side, rowside, sp), rows in corner.items():
            where = pl.ds(15 * rowside, HALF, stride=16)
            ph[side, half, sp, where, :] = ph[side, half, sp, where, :] + rows[half * HALF:half * HALF + HALF]

    partner = d + 1 - 2 * core

    def core_copy(g):
        some = pl.ds(g * HALF * X, HALF * X)
        return remote(t0.at[1 - core, some], cr.at[some], sent, c_recv.at[g], partner, z)

    def ends(g):
        with mark(f"w_p{g}"):
            for side in range(2):
                each(source[side], [depth_copy("p", side, g)], "wait_recv")
        add_corners(g)
        for q in range(HALF):
            place = g * HALF + q
            ct = (y + place + 2) & (Y - 1)
            for rb in range(2):
                parts = []
                for side, layer in ((0, 0), (1, LAYERS - 1)):
                    values = [new[sp, layer, pl.ds(8 * rb, 8), columns_of(ct)]
                              + COEF[sp] * ph[side, g, sp, pl.ds(q * 16 + 8 * rb, 8), :] for sp in range(2)]
                    parts.append(shade(*values, layer, ct, rb))
                (near, light), (far, light_far) = parts
                rows = pl.ds(pl.multiple_of(ct * 16 + 8 * rb, 8), 8)
                light_mid = light * mid[3, rows, :]
                for k in range(3):
                    flat[place * 8 + 2 * k + rb] = near[k] + light * mid[k, rows, :] + light_mid * far[k]
                flat[place * 8 + 6 + rb] = light_mid * light_far
        for place in range(g * HALF, g * HALF + HALF):
            for j, tile in enumerate(regroup([flat[place * 8 + i] for i in range(8)], lane)):
                t0[j % 2, place * X + j // 2] = tile
        core_copy(g).start()
        for away, across in DIRECT:
            place = (away - 2) % Y
            if place // HALF == g:
                yy, xx = (y + away) & (Y - 1), (x + across) & (X - 1)
                for c in range(2):
                    remote(t0.at[c, place * X + xx], xr.at[CHIPS * core + chip], x_send, x_recv, at(yy, xx, c), z).start()

    with mark("w_everyone"):
        @pl.when(jnp.logical_not(collects))
        def _():
            pl.semaphore_wait(everyone, 1)

    for g in range(2):
        with mark(f"ends{g}"):
            ends(g)

    def chip_copy(place, away, across):
        xx = (x + across) & (X - 1)
        return remote(x0.at[place * X + xx], xr.at[chip], x_send, x_recv, at((y + away) & (Y - 1), xx, core), z)

    def merge(g):
        core_copy(g).wait_recv()
        for i in range(g * HALF * X, (g + 1) * HALF * X):
            mine, other = t0[core, i], cr[i]
            x0[i] = joined(jnp.where(core == 0, mine, other), jnp.where(core == 0, other, mine), lane)
        for away in ((4, 3, 5, 2), (6, 1, 7, 0))[g]:
            for across in (2, 1, 3, 0):
                if (away or across) and (away, across) not in DIRECT:
                    chip_copy((away - 2) % Y, away, across).start()

    for g in range(2):
        with mark(f"merge{g}"):
            merge(g)
    for side in range(2):
        each(to[side], [depth_copy(kind, side, 0) for kind in ("edge", "both", "halves")], "wait_send")
        each("above_" + to[side], [depth_copy("straight", side, 0)], "wait_send")
        each(zto[side], [row_copy(kind, side) for kind in ("0", "1")], "wait_send")
    each("zhi", [row_copy("corner", 0)], "wait_send")
    for g in range(2):
        core_copy(g).wait_send()
    xr[chip] = x0[(Y - 2) * X + x]
    arrived = xr.at[pl.ds(0, TILES)]
    with mark("w_xy"):
        pltpu.make_async_copy(arrived, arrived, x_recv).wait()
    pltpu.make_async_copy(arrived, arrived, x_send).wait()


def finish(new, xr, out_s, out_c, out_image, img, out_sem):
    copies = [pltpu.make_async_copy(new.at[0], out_s, out_sem.at[0]),
              pltpu.make_async_copy(new.at[1], out_c, out_sem.at[1])]
    for copy in copies:
        copy.start()
    last = pltpu.make_async_copy(img, out_image, out_sem.at[2])

    def compose(once, carry):
        lane = lax.broadcasted_iota(jnp.int32, (8, 128), 1)
        pieces = []
        for first in range(0, CHIPS, HALF):
            total, light = None, None
            for i in range(first, first + HALF):
                for c in range(2):
                    tile = xr[c * CHIPS + i]
                    color = jnp.where(lane < 96, tile, 0.0)
                    passing = expand(tile, lane)
                    total = color if total is None else total + light * color
                    light = passing if light is None else light * passing
            pieces.append((total, light))
        while len(pieces) > 1:
            pieces = [(near + light * far, light * light_far)
                      for (near, light), (far, light_far) in zip(pieces[::2], pieces[1::2])]
        total, light = pieces[0]
        tile = jnp.where(lane < 96, total, 1.0 - light)
        for g in range(8):
            part = tile if g == 0 else pltpu.roll(tile, 128 - 16 * g, 1)
            img[g // 2, pl.ds(8 * (g % 2), 8), :] = part[:, :16]
        last.start()
        return carry

    lax.fori_loop(0, 1 + (lax.axis_index("depth") >> 6), compose, 0)
    for copy in copies + [last]:
        copy.wait()


def body(substrate, catalyst, feed_rate, kill_rate, extinction, palette):
    field = jax.ShapeDtypeStruct(substrate.shape, jnp.float32)
    any_ref = pl.BlockSpec(memory_space=pl.ANY)
    f32 = jnp.float32
    dma = pltpu.SemaphoreType.DMA
    new, parts = pl.pallas_call(
        kernel,
        out_shape=(pltpu.VMEM((2,) + field.shape, f32), pltpu.VMEM((2 * CHIPS, 8, 128), f32)),
        in_specs=[any_ref] * 6,
        out_specs=(pl.BlockSpec(memory_space=pltpu.VMEM),) * 2,
        scratch_shapes=[
            pltpu.VMEM((2, LAYERS, (CT + 2) * TILE, 128), f32),
            pltpu.VMEM((2, LAYERS, (CT + 2) * TILE, 128), f32),
            pltpu.VMEM((LAYERS, 16, CT * 128), f32),
            pltpu.VMEM((LAYERS, 16, CT * 128), f32),
            pltpu.VMEM((LAYERS, 16, CT * 128), f32),
            pltpu.VMEM((2, 2, 16, CT * 128), f32),
            pltpu.VMEM((2, 2, 2, HALF * 16, 128), f32),
            pltpu.VMEM((2, 2, 2, HALF * 16, 128), f32),
            pltpu.VMEM((2, 2, LAYERS, CT, 128), f32),
            pltpu.VMEM((2, 2, LAYERS, CT, 128), f32),
            pltpu.VMEM((2, 2, LAYERS, CT, 128), f32),
            pltpu.VMEM((2, 2, LAYERS, CT, 128), f32),
            pltpu.VMEM((2, 1, 2, CT, 128), f32),
            pltpu.VMEM((2, 2, 2, CT, 128), f32),
            pltpu.VMEM((4, CT * 16, 128), f32),
            pltpu.VMEM((CT * 8, 8, 128), f32),
            pltpu.VMEM((2, CHIPS, 8, 128), f32),
            pltpu.VMEM((CHIPS, 8, 128), f32),
            pltpu.VMEM((CHIPS, 8, 128), f32),
            pltpu.SMEM((3, 3), f32),
            dma((6,)),
            dma, dma((2,)), dma((2, 2)),
            dma((2,)), dma((2,)),
            dma((2,)), dma, dma((2,)),
            dma((2,)), dma, dma,
            pltpu.SemaphoreType.REGULAR, pltpu.SemaphoreType.REGULAR,
        ],
        compiler_params=pltpu.CompilerParams(collective_id=0, has_side_effects=True),
    )(palette, substrate, catalyst, feed_rate, kill_rate, extinction)
    return pl.pallas_call(
        finish,
        out_shape=(field, field, jax.ShapeDtypeStruct((4, 16, 16), f32)),
        in_specs=[pl.BlockSpec(memory_space=pltpu.VMEM)] * 2,
        out_specs=(any_ref,) * 3,
        scratch_shapes=[pltpu.VMEM((4, 16, 16), f32), dma((3,))],
    )(*(pltpu.with_memory_space_constraint(part, pltpu.VMEM) for part in (new, parts)))


def solution(mesh):
    split = P("depth", "rows", None)
    return jax.shard_map(
        body,
        mesh=mesh,
        in_specs=(split,) * 5 + (P(),),
        out_specs=(split, split, P(None, "rows", "depth")),
        check_vma=False,
    )
```

```python
import contextlib

import jax
import jax.numpy as jnp
from jax import lax
from jax.experimental import pallas as pl
from jax.experimental.pallas import tpu as pltpu
from jax.sharding import PartitionSpec as P

mark = contextlib.nullcontext
MESH = pl.DeviceIdType.MESH
X, Y = 4, 8
CHIPS = X * Y
DEPTHS = 2 * CHIPS
ZS = 8
CT = 8
LAYERS = 4
TILE = 32
COEF = (0.16, 0.08)
FIRST = 8
GROUP = 4
HALF = CT // 2
COLLECTORS = (10, (Y // 2) * X + X // 2)
DIRECT = ((4, 2), (4, 1), (4, 3), (3, 2), (5, 2))
SEAM = 4
TILES = CHIPS - 1 + len(DIRECT)


def expand(tile, lane):
    light = jnp.where(lane >= 96, tile, 0.0)
    return light + pltpu.roll(light, 32, 1) + (pltpu.roll(light, 64, 1) + pltpu.roll(light, 96, 1))


def joined(near, far, lane):
    return jnp.where(lane < 96, near, 0.0) + expand(near, lane) * far


def regroup(tiles, lane):
    tiles = list(tiles)
    for bit in (1, 2, 4):
        low_half = (lane & (16 * bit)) == 0
        for g in range(8):
            if g & bit:
                continue
            low, high = tiles[g], tiles[g | bit]
            tiles[g] = jnp.where(low_half, low, pltpu.roll(high, 16 * bit, 1))
            tiles[g | bit] = jnp.where(low_half, pltpu.roll(low, 128 - 16 * bit, 1), high)
    return tiles


def kernel(palette, S, C, F, K, E, new, xr,
           s0, s1, fv, kv, ev, h0, ph, ps, r0, r1, rs0, rs1, eg, dg, mid, flat, t0, cr, x0, pal,
           load_sem, sent, h_recv, p_recv, r0_recv, r1_recv,
           e_recv, g_recv, s_recv, c_recv, x_send, x_recv, everyone, ready):
    d = lax.axis_index("depth")
    z = lax.axis_index("rows")
    core = d & 1
    chip = d >> 1
    x = chip & (X - 1)
    y = chip >> 2

    def at(yy, xx, cc):
        return (yy * X + xx) * 2 + cc

    has = {"lo": d > 0, "hi": d < DEPTHS - 1, "zlo": z > 0, "zhi": z < ZS - 1}
    up, down = jnp.minimum(d + 1, DEPTHS - 1), jnp.maximum(d - 1, 0)
    zup, zdown = jnp.minimum(z + 1, ZS - 1), jnp.maximum(z - 1, 0)

    barrier = pltpu.get_barrier_semaphore()

    def signal(sem, depth, row):
        pl.semaphore_signal(sem, inc=1, device_id=(depth, row), device_id_type=MESH)

    for flag, depth, row in (("lo", down, z), ("hi", up, z), ("zhi", d, zup)):
        @pl.when(has[flag])
        def _(depth=depth, row=row):
            signal(barrier, depth, row)

    above, below = has["zlo"], has["zhi"]
    for flag, depth in (("lo", down), ("hi", up)):
        @pl.when(below & has[flag])
        def _(depth=depth):
            signal(barrier, depth, zup)
    has["above_lo"], has["above_hi"] = above & has["lo"], above & has["hi"]
    has["below_lo"], has["below_hi"] = below & has["lo"], below & has["hi"]

    collector = jnp.where(z == 0, COLLECTORS[0], COLLECTORS[1])
    collects = chip == collector
    for c in range(2):
        @pl.when(d != 2 * collector + c)
        def _(c=c):
            signal(barrier, 2 * collector + c, z)

    for ct in range(CT):
        for sp, src in ((0, S), (1, C)):
            pltpu.make_async_copy(
                src.at[:, :, pl.ds(ct * 128, 128)],
                s0.at[sp, :, pl.ds((ct + 1) * TILE + FIRST, 16), :],
                load_sem.at[sp],
            ).start()
    pal_load = pltpu.make_async_copy(palette, pal, load_sem.at[5])
    f_load = pltpu.make_async_copy(F, fv, load_sem.at[2])
    k_load = pltpu.make_async_copy(K, kv, load_sem.at[3])
    e_load = pltpu.make_async_copy(E, ev, load_sem.at[4])
    f_load.start()
    k_load.start()
    e_load.start()
    pal_load.start()

    zero = jnp.zeros((8, 128), jnp.float32)
    for sp in range(2):
        for layer in range(LAYERS):
            for buf in (s0, s1):
                for t in (0, CT + 1):
                    for rb in range(2):
                        buf[sp, layer, pl.ds(t * TILE + FIRST + 8 * rb, 8), :] = zero
            for row in (FIRST - 1, FIRST + 16):
                s0[sp, layer, pl.ds(TILE + row, CT, stride=TILE), :] = zero
    lane = lax.broadcasted_iota(jnp.int32, (8, 128), 1)

    def in_groups(step):
        def group(g, carry):
            for q in range(GROUP):
                step(g * GROUP + q, carry)
            return carry

        lax.fori_loop(0, CT // GROUP, group, 0)

    def start_of(ct, rb):
        return pl.multiple_of((ct + 1) * TILE + FIRST + 8 * rb, 8)

    def centre(buf, sp, layer, ct, rb):
        return buf[sp, layer, pl.ds(start_of(ct, rb), 8), :]

    def around(buf, sp, layer, ct, rb):
        here = centre(buf, sp, layer, ct, rb)
        left = centre(buf, sp, layer, ct - 1, rb)
        right = centre(buf, sp, layer, ct + 1, rb)
        total = pltpu.roll(jnp.where(lane == 127, left, here), 1, 1)
        total += pltpu.roll(jnp.where(lane == 0, right, here), 127, 1)
        base = start_of(ct, rb)
        total += buf[sp, layer, pl.ds(base - 1, 8), :]
        total += buf[sp, layer, pl.ds(base + 1, 8), :]
        return here, total

    def native(ref, layer, ct, rb):
        return ref[layer, pl.ds(8 * rb, 8), pl.ds(pl.multiple_of(ct * 128, 128), 128)]

    def react(s, c, around_s, around_c, layer, ct, rb):
        feed = native(fv, layer, ct, rb)
        kill = native(kv, layer, ct, rb)
        feed = feed + feed
        reaction = s * c * c
        reaction = reaction + reaction
        new_s = COEF[0] * around_s + (feed + s * (0.04 - feed)) - reaction
        new_c = COEF[1] * around_c + c * (0.52 - feed - (kill + kill)) + reaction
        return new_s, new_c

    def first(layers):
        def body(ct, carry):
            for layer in layers:
                for rb in range(2):
                    values = []
                    for sp in range(2):
                        here, total = around(s0, sp, layer, ct, rb)
                        if layer > 0:
                            total += centre(s0, sp, layer - 1, ct, rb)
                        if layer < LAYERS - 1:
                            total += centre(s0, sp, layer + 1, ct, rb)
                        values.append((here, total))
                    result = react(values[0][0], values[1][0], values[0][1], values[1][1], layer, ct, rb)
                    for sp in range(2):
                        s1[sp, layer, pl.ds(start_of(ct, rb), 8), :] = result[sp]
                        for side, edge, target in ((0, LAYERS - 1, up), (1, 0, down)):
                            if layer == edge:
                                place = (ct - (target >> 3) + (Y - 2)) & (Y - 1)
                                rows = pl.multiple_of((place & (HALF - 1)) * 16 + 8 * rb, 8)
                                ps[side, place >> 2, sp, pl.ds(rows, 8), :] = result[sp]
            return carry

        in_groups(body)

    early = (z == SEAM) & (collects | ((x == 0) & (core == 0) & (y > 0)) | ((x == X - 1) & (core == 1) & (y < Y // 2)))
    later = jnp.logical_not(early)

    def fields_loaded():
        with mark("w_load"):
            for sp in range(2):
                whole = s0.at[sp, :, pl.ds(0, CT * 16), :]
                pltpu.make_async_copy(whole, whole, load_sem.at[sp]).wait()

    def rates_loaded():
        with mark("w_loadfk"):
            f_load.wait()
            k_load.wait()


    @pl.when(early)
    def _():
        fields_loaded()
        rates_loaded()
        first((0, LAYERS - 1))
        first(range(1, LAYERS - 1))

    with mark("w_barrier"):
        pl.semaphore_wait(barrier, sum(jnp.where(has[flag], 1, 0) for flag in ("lo", "hi", "zlo", "above_lo", "above_hi")) + jnp.where(collects, DEPTHS - 1, 0))

    @pl.when(has["zlo"])
    def _():
        signal(ready, d, zdown)

    def tell():
        def one(i, carry):
            signal(everyone, 2 * ((chip + i) & (CHIPS - 1)) + core, z)
            return carry

        lax.fori_loop(1, CHIPS, one, 0)

    @pl.when(collects & (z == 0))
    def _():
        tell()

    clear = jnp.where(lax.broadcasted_iota(jnp.int32, (8, 128), 1) < 96, 0.0, 1.0)
    for away in range(Y):
        for across in range(X):
            if (away, across) not in DIRECT:
                xr[CHIPS + ((y - away) & (Y - 1)) * X + ((x - across) & (X - 1))] = clear
    for side, flag in ((0, "lo"), (1, "hi")):
        @pl.when(jnp.logical_not(has[flag]))
        def _(side=side):
            for sp in range(2):
                eg[side, 0, sp] = zero
                dg[side, 1, sp] = zero

                def fill(i, carry):
                    h0[side, sp, :, pl.ds(i * 128, 128)] = jnp.zeros((16, 128), jnp.float32)
                    ph[side, i // HALF, sp, pl.ds((i % HALF) * 16, 16), :] = jnp.zeros((16, 128), jnp.float32)
                    return carry

                lax.fori_loop(0, CT, fill, 0)
    for side, flag in ((0, "zlo"), (1, "zhi")):
        @pl.when(jnp.logical_not(has[flag]))
        def _(side=side):
            for sp in range(2):
                for layer in range(LAYERS):
                    r0[side, sp, layer] = zero
                    r1[side, sp, layer] = zero
                for depthside in range(2):
                    dg[depthside, side, sp] = zero

    def remote(src, dst, send, recv, depth, row):
        return pltpu.make_async_remote_copy(
            src_ref=src, dst_ref=dst, send_sem=send, recv_sem=recv,
            device_id=(depth, row), device_id_type=MESH)

    def depth_copy(kind, side, sp):
        target = up if side == 0 else down
        if kind == "h":
            src = (S, C)[sp].at[LAYERS - 1 if side == 0 else 0]
            return remote(src, h0.at[side, sp], sent, h_recv.at[side], target, z)
        if kind == "both":
            return remote(h0.at[side], h0.at[side], sent, h_recv.at[side], target, z)
        if kind == "halves":
            return remote(ps.at[side], ph.at[side], sent, p_recv.at[side, 0], target, z)
        if kind == "p":
            half = sp
            return remote(ps.at[side, half], ph.at[side, half], sent, p_recv.at[side, half], target, z)
        if kind == "straight":
            return remote(rs0.at[1, :, LAYERS - 1 if side == 0 else 0], dg.at[side, 1],
                          sent, s_recv.at[side], target, zdown)
        return remote(rs0.at[0:1, :, LAYERS - 1 if side == 0 else 0], eg.at[side],
                      sent, e_recv.at[side], target, z)

    def row_copy(kind, side):
        target = zup if side == 0 else zdown
        if kind == "0":
            return remote(rs0.at[side], r0.at[side], sent, r0_recv.at[side], d, target)
        if kind == "corner":
            return remote(eg.at[:, 0], dg.at[:, 0], sent, g_recv, d, target)
        return remote(rs1.at[side], r1.at[side], sent, r1_recv.at[side], d, target)

    to = ("hi", "lo")
    source = ("lo", "hi")
    zto = ("zhi", "zlo")
    zsource = ("zlo", "zhi")

    def each(flag, copies, what):
        @pl.when(has[flag])
        def _():
            for copy in copies:
                getattr(copy, what)()

    pl.when(later)(fields_loaded)
    for side in range(2):
        row = TILE + FIRST + (15 if side == 0 else 0)
        for sp in range(2):
            for layer in range(LAYERS):
                rs0[side, sp, layer] = s0[sp, layer, pl.ds(row, CT, stride=TILE), :]
    for side in range(2):
        each("above_" + to[side], [depth_copy("straight", side, 0)], "start")
    for side in range(2):
        each(to[side], [depth_copy("edge", side, 0)] + [depth_copy("h", side, sp) for sp in range(2)], "start")
    each("zlo", [row_copy("0", 1)], "start")

    @pl.when(collects & (z > 0))
    def _():
        tell()

    @pl.when(later)
    def _():
        rates_loaded()
        first((0, LAYERS - 1))

    for side in range(2):
        each(to[side], [depth_copy("p", side, half) for half in range(2)], "start")
    @pl.when(later)
    def _():
        first(range(1, LAYERS - 1))

    for side in range(2):
        row = TILE + FIRST + (15 if side == 0 else 0)
        for sp in range(2):
            for layer in range(LAYERS):
                rs1[side, sp, layer] = s1[sp, layer, pl.ds(row, CT, stride=TILE), :]
    each("zlo", [row_copy("1", 1)], "start")
    with mark("w_readyz"):
        @pl.when(has["zhi"])
        def _():
            pl.semaphore_wait(ready, 1)
            for kind in ("0", "1"):
                row_copy(kind, 0).start()

    with mark("w_edge"):
        for side in range(2):
            each(source[side], [depth_copy("edge", side, 0)], "wait_recv")
    each("zhi", [row_copy("corner", 0)], "start")

    with mark("w_row0"):
        for side in range(2):
            each(zsource[side], [row_copy("0", side)], "wait_recv")

    scale = {flag: jnp.where(has[flag], 1.0, 0.0).astype(jnp.float32) for flag in source + zsource}
    for side in range(2):
        row = TILE + FIRST + (0 if side == 0 else 15)
        for sp in range(2):
            for layer in range(LAYERS):
                where = pl.ds(row, CT, stride=TILE)
                s1[sp, layer, where, :] = s1[sp, layer, where, :] + COEF[sp] * r0[side, sp, layer]
    with mark("w_row1"):
        for side in range(2):
            each(zsource[side], [row_copy("1", side)], "wait_recv")
    for side in range(2):
        edge = TILE + FIRST + (0 if side == 0 else 15)
        outside = TILE + FIRST + (-1 if side == 0 else 16)
        for sp in range(2):
            factor = COEF[sp] * scale[zsource[side]]
            for layer in range(LAYERS):
                s1[sp, layer, pl.ds(outside, CT, stride=TILE), :] = (
                    r1[side, sp, layer] + factor * s0[sp, layer, pl.ds(edge, CT, stride=TILE), :])

    with mark("w_h"):
        for side in range(2):
            each(source[side], [depth_copy("both", side, 0)], "wait_recv")

    def add_layers(ct, carry):
        for side, layer in ((0, 0), (1, LAYERS - 1)):
            for sp in range(2):
                for rb in range(2):
                    where = pl.ds(start_of(ct, rb), 8)
                    halo = h0[side, sp, pl.ds(8 * rb, 8), pl.ds(pl.multiple_of(ct * 128, 128), 128)]
                    s1[sp, layer, where, :] = s1[sp, layer, where, :] + COEF[sp] * halo
        return carry

    with mark("addlayers"):
        in_groups(add_layers)

    e_load.wait()
    pal_load.wait()
    weights = []
    for k in range(3):
        a, b = -8.0 * pal[k, 0], -8.0 * pal[k, 1]
        weights.append((a, b, -pal[k, 2] - 0.65 * a - 0.25 * b))

    def columns_of(ct):
        return pl.ds(pl.multiple_of(ct * 128, 128), 128)

    def second(layer, ct, rb):
        values = []
        for sp in range(2):
            here, total = around(s1, sp, layer, ct, rb)
            if layer > 0:
                total += centre(s1, sp, layer - 1, ct, rb)
            else:
                total += (COEF[sp] * scale["lo"]) * centre(s0, sp, 0, ct, rb)
            if layer < LAYERS - 1:
                total += centre(s1, sp, layer + 1, ct, rb)
            else:
                total += (COEF[sp] * scale["hi"]) * centre(s0, sp, LAYERS - 1, ct, rb)
            values.append((here, total))
        return react(values[0][0], values[1][0], values[0][1], values[1][1], layer, ct, rb)

    def shade(s, c, layer, ct, rb):
        new[0, layer, pl.ds(8 * rb, 8), columns_of(ct)] = s
        new[1, layer, pl.ds(8 * rb, 8), columns_of(ct)] = c
        passing = jnp.exp(-native(ev, layer, ct, rb) * (0.25 + 4.0 * c * c))
        opacity = 1.0 - passing
        colors = [opacity / (1.0 + jnp.exp(a * s + b * c + e)) for a, b, e in weights]
        return colors, passing

    def middle(ct, carry):
        for rb in range(2):
            rows = pl.ds(pl.multiple_of(ct * 16 + 8 * rb, 8), 8)
            near, light = shade(*second(1, ct, rb), 1, ct, rb)
            far, light_far = shade(*second(2, ct, rb), 2, ct, rb)
            for k in range(3):
                mid[k, rows, :] = near[k] + light * far[k]
            mid[3, rows, :] = light * light_far
        return carry

    with mark("middle"):
        in_groups(middle)

    def open_ends(ct, carry):
        for layer in (0, LAYERS - 1):
            for rb in range(2):
                for sp, value in enumerate(second(layer, ct, rb)):
                    new[sp, layer, pl.ds(8 * rb, 8), columns_of(ct)] = value
        return carry

    with mark("open_ends"):
        in_groups(open_ends)

    with mark("w_diag"):
        for side in range(2):
            each("below_" + source[side], [depth_copy("straight", side, 0)], "wait_recv")
        each("zlo", [row_copy("corner", 0)], "wait_recv")
    corner = {}
    for side in range(2):
        for rowside in range(2):
            for sp in range(2):
                corner[side, rowside, sp] = pltpu.roll(dg[side, rowside, sp], (Y - 2 - y) & (Y - 1), 0) * (2.0 * COEF[sp])

    def add_corners(half):
        for (side, rowside, sp), rows in corner.items():
            where = pl.ds(15 * rowside, HALF, stride=16)
            ph[side, half, sp, where, :] = ph[side, half, sp, where, :] + rows[half * HALF:half * HALF + HALF]

    partner = d + 1 - 2 * core

    def core_copy(g):
        some = pl.ds(g * HALF * X, HALF * X)
        return remote(t0.at[1 - core, some], cr.at[some], sent, c_recv.at[g], partner, z)

    def ends(g):
        with mark(f"w_p{g}"):
            for side in range(2):
                each(source[side], [depth_copy("p", side, g)], "wait_recv")
        add_corners(g)
        for q in range(HALF):
            place = g * HALF + q
            ct = (y + place + 2) & (Y - 1)
            for rb in range(2):
                parts = []
                for side, layer in ((0, 0), (1, LAYERS - 1)):
                    values = [new[sp, layer, pl.ds(8 * rb, 8), columns_of(ct)]
                              + COEF[sp] * ph[side, g, sp, pl.ds(q * 16 + 8 * rb, 8), :] for sp in range(2)]
                    parts.append(shade(*values, layer, ct, rb))
                (near, light), (far, light_far) = parts
                rows = pl.ds(pl.multiple_of(ct * 16 + 8 * rb, 8), 8)
                light_mid = light * mid[3, rows, :]
                for k in range(3):
                    flat[place * 8 + 2 * k + rb] = near[k] + light * mid[k, rows, :] + light_mid * far[k]
                flat[place * 8 + 6 + rb] = light_mid * light_far
        for place in range(g * HALF, g * HALF + HALF):
            for j, tile in enumerate(regroup([flat[place * 8 + i] for i in range(8)], lane)):
                t0[j % 2, place * X + j // 2] = tile
        core_copy(g).start()
        for away, across in DIRECT:
            place = (away - 2) % Y
            if place // HALF == g:
                yy, xx = (y + away) & (Y - 1), (x + across) & (X - 1)
                for c in range(2):
                    remote(t0.at[c, place * X + xx], xr.at[CHIPS * core + chip], x_send, x_recv, at(yy, xx, c), z).start()

    with mark("w_everyone"):
        @pl.when(jnp.logical_not(collects))
        def _():
            pl.semaphore_wait(everyone, 1)

    for g in range(2):
        with mark(f"ends{g}"):
            ends(g)

    def chip_copy(place, away, across):
        xx = (x + across) & (X - 1)
        return remote(x0.at[place * X + xx], xr.at[chip], x_send, x_recv, at((y + away) & (Y - 1), xx, core), z)

    def merge(g):
        core_copy(g).wait_recv()
        for i in range(g * HALF * X, (g + 1) * HALF * X):
            mine, other = t0[core, i], cr[i]
            x0[i] = joined(jnp.where(core == 0, mine, other), jnp.where(core == 0, other, mine), lane)
        for away in ((4, 3, 5, 2), (6, 1, 7, 0))[g]:
            for across in (2, 1, 3, 0):
                if (away or across) and (away, across) not in DIRECT:
                    chip_copy((away - 2) % Y, away, across).start()

    for g in range(2):
        with mark(f"merge{g}"):
            merge(g)
    for side in range(2):
        each(to[side], [depth_copy(kind, side, 0) for kind in ("edge", "both", "halves")], "wait_send")
        each("above_" + to[side], [depth_copy("straight", side, 0)], "wait_send")
        each(zto[side], [row_copy(kind, side) for kind in ("0", "1")], "wait_send")
    each("zhi", [row_copy("corner", 0)], "wait_send")
    for g in range(2):
        core_copy(g).wait_send()
    xr[chip] = x0[(Y - 2) * X + x]
    arrived = xr.at[pl.ds(0, TILES)]
    with mark("w_xy"):
        pltpu.make_async_copy(arrived, arrived, x_recv).wait()
    pltpu.make_async_copy(arrived, arrived, x_send).wait()


def finish(new, xr, out_s, out_c, out_image, img, out_sem):
    copies = [pltpu.make_async_copy(new.at[0], out_s, out_sem.at[0]),
              pltpu.make_async_copy(new.at[1], out_c, out_sem.at[1])]
    for copy in copies:
        copy.start()
    last = pltpu.make_async_copy(img, out_image, out_sem.at[2])

    def compose(once, carry):
        lane = lax.broadcasted_iota(jnp.int32, (8, 128), 1)
        pieces = []
        for first in range(0, CHIPS, HALF):
            total, light = None, None
            for i in range(first, first + HALF):
                for c in range(2):
                    tile = xr[c * CHIPS + i]
                    color = jnp.where(lane < 96, tile, 0.0)
                    passing = expand(tile, lane)
                    total = color if total is None else total + light * color
                    light = passing if light is None else light * passing
            pieces.append((total, light))
        while len(pieces) > 1:
            pieces = [(near + light * far, light * light_far)
                      for (near, light), (far, light_far) in zip(pieces[::2], pieces[1::2])]
        total, light = pieces[0]
        tile = jnp.where(lane < 96, total, 1.0 - light)
        for g in range(8):
            part = tile if g == 0 else pltpu.roll(tile, 128 - 16 * g, 1)
            img[g // 2, pl.ds(8 * (g % 2), 8), :] = part[:, :16]
        last.start()
        return carry

    lax.fori_loop(0, 1 + (lax.axis_index("depth") >> 6), compose, 0)
    for copy in copies + [last]:
        copy.wait()


def body(substrate, catalyst, feed_rate, kill_rate, extinction, palette):
    field = jax.ShapeDtypeStruct(substrate.shape, jnp.float32)
    any_ref = pl.BlockSpec(memory_space=pl.ANY)
    f32 = jnp.float32
    dma = pltpu.SemaphoreType.DMA
    new, parts = pl.pallas_call(
        kernel,
        out_shape=(pltpu.VMEM((2,) + field.shape, f32), pltpu.VMEM((2 * CHIPS, 8, 128), f32)),
        in_specs=[any_ref] * 6,
        out_specs=(pl.BlockSpec(memory_space=pltpu.VMEM),) * 2,
        scratch_shapes=[
            pltpu.VMEM((2, LAYERS, (CT + 2) * TILE, 128), f32),
            pltpu.VMEM((2, LAYERS, (CT + 2) * TILE, 128), f32),
            pltpu.VMEM((LAYERS, 16, CT * 128), f32),
            pltpu.VMEM((LAYERS, 16, CT * 128), f32),
            pltpu.VMEM((LAYERS, 16, CT * 128), f32),
            pltpu.VMEM((2, 2, 16, CT * 128), f32),
            pltpu.VMEM((2, 2, 2, HALF * 16, 128), f32),
            pltpu.VMEM((2, 2, 2, HALF * 16, 128), f32),
            pltpu.VMEM((2, 2, LAYERS, CT, 128), f32),
            pltpu.VMEM((2, 2, LAYERS, CT, 128), f32),
            pltpu.VMEM((2, 2, LAYERS, CT, 128), f32),
            pltpu.VMEM((2, 2, LAYERS, CT, 128), f32),
            pltpu.VMEM((2, 1, 2, CT, 128), f32),
            pltpu.VMEM((2, 2, 2, CT, 128), f32),
            pltpu.VMEM((4, CT * 16, 128), f32),
            pltpu.VMEM((CT * 8, 8, 128), f32),
            pltpu.VMEM((2, CHIPS, 8, 128), f32),
            pltpu.VMEM((CHIPS, 8, 128), f32),
            pltpu.VMEM((CHIPS, 8, 128), f32),
            pltpu.SMEM((3, 3), f32),
            dma((6,)),
            dma, dma((2,)), dma((2, 2)),
            dma((2,)), dma((2,)),
            dma((2,)), dma, dma((2,)),
            dma((2,)), dma, dma,
            pltpu.SemaphoreType.REGULAR, pltpu.SemaphoreType.REGULAR,
        ],
        compiler_params=pltpu.CompilerParams(collective_id=0, has_side_effects=True),
    )(palette, substrate, catalyst, feed_rate, kill_rate, extinction)
    return pl.pallas_call(
        finish,
        out_shape=(field, field, jax.ShapeDtypeStruct((4, 16, 16), f32)),
        in_specs=[pl.BlockSpec(memory_space=pltpu.VMEM)] * 2,
        out_specs=(any_ref,) * 3,
        scratch_shapes=[pltpu.VMEM((4, 16, 16), f32), dma((3,))],
    )(*(pltpu.with_memory_space_constraint(part, pltpu.VMEM) for part in (new, parts)))


def solution(mesh):
    split = P("depth", "rows", None)
    return jax.shard_map(
        body,
        mesh=mesh,
        in_specs=(split,) * 5 + (P(),),
        out_specs=(split, split, P(None, "rows", "depth")),
        check_vma=False,
    )
```

```python
import contextlib

import jax
import jax.numpy as jnp
from jax import lax
from jax.experimental import pallas as pl
from jax.experimental.pallas import tpu as pltpu
from jax.sharding import PartitionSpec as P

mark = contextlib.nullcontext
MESH = pl.DeviceIdType.MESH
X, Y = 4, 8
CHIPS = X * Y
DEPTHS = 2 * CHIPS
ZS = 8
CT = 8
LAYERS = 4
TILE = 32
COEF = (0.16, 0.08)
FIRST = 8
GROUP = 4
HALF = CT // 2
COLLECTORS = (10, (Y // 2) * X + X // 2)
DIRECT = ((4, 2), (4, 1), (4, 3), (3, 2), (5, 2))
TILES = CHIPS - 1 + len(DIRECT)


def expand(tile, lane):
    light = jnp.where(lane >= 96, tile, 0.0)
    return light + pltpu.roll(light, 32, 1) + (pltpu.roll(light, 64, 1) + pltpu.roll(light, 96, 1))


def joined(near, far, lane):
    return jnp.where(lane < 96, near, 0.0) + expand(near, lane) * far


def regroup(tiles, lane):
    tiles = list(tiles)
    for bit in (1, 2, 4):
        low_half = (lane & (16 * bit)) == 0
        for g in range(8):
            if g & bit:
                continue
            low, high = tiles[g], tiles[g | bit]
            tiles[g] = jnp.where(low_half, low, pltpu.roll(high, 16 * bit, 1))
            tiles[g | bit] = jnp.where(low_half, pltpu.roll(low, 128 - 16 * bit, 1), high)
    return tiles


def kernel(palette, S, C, F, K, E, new, xr,
           s0, s1, fv, kv, ev, h0, ph, ps, r0, r1, rs0, rs1, eg, dg, mid, flat, t0, cr, x0, pal,
           load_sem, sent, h_recv, p_recv, r0_recv, r1_recv,
           e_recv, g_recv, s_recv, c_recv, x_recv, everyone, ready):
    d = lax.axis_index("depth")
    z = lax.axis_index("rows")
    core = d & 1
    chip = d >> 1
    x = chip & (X - 1)
    y = chip >> 2

    def at(yy, xx, cc):
        return (yy * X + xx) * 2 + cc

    has = {"lo": d > 0, "hi": d < DEPTHS - 1, "zlo": z > 0, "zhi": z < ZS - 1}
    up, down = jnp.minimum(d + 1, DEPTHS - 1), jnp.maximum(d - 1, 0)
    zup, zdown = jnp.minimum(z + 1, ZS - 1), jnp.maximum(z - 1, 0)

    barrier = pltpu.get_barrier_semaphore()

    def signal(sem, depth, row):
        pl.semaphore_signal(sem, inc=1, device_id=(depth, row), device_id_type=MESH)

    for flag, depth, row in (("lo", down, z), ("hi", up, z), ("zhi", d, zup)):
        @pl.when(has[flag])
        def _(depth=depth, row=row):
            signal(barrier, depth, row)

    above, below = has["zlo"], has["zhi"]
    for flag, depth in (("lo", down), ("hi", up)):
        @pl.when(below & has[flag])
        def _(depth=depth):
            signal(barrier, depth, zup)
    has["above_lo"], has["above_hi"] = above & has["lo"], above & has["hi"]
    has["below_lo"], has["below_hi"] = below & has["lo"], below & has["hi"]

    collector = jnp.where(z == 0, COLLECTORS[0], COLLECTORS[1])
    collects = chip == collector
    for c in range(2):
        @pl.when(d != 2 * collector + c)
        def _(c=c):
            signal(barrier, 2 * collector + c, z)

    for ct in range(CT):
        for sp, src in ((0, S), (1, C)):
            pltpu.make_async_copy(
                src.at[:, :, pl.ds(ct * 128, 128)],
                s0.at[sp, :, pl.ds((ct + 1) * TILE + FIRST, 16), :],
                load_sem.at[0],
            ).start()
    pal_load = pltpu.make_async_copy(palette, pal, load_sem.at[1])
    f_load = pltpu.make_async_copy(F, fv, load_sem.at[2])
    k_load = pltpu.make_async_copy(K, kv, load_sem.at[3])
    e_load = pltpu.make_async_copy(E, ev, load_sem.at[4])
    f_load.start()
    k_load.start()
    e_load.start()
    pal_load.start()

    zero = jnp.zeros((8, 128), jnp.float32)
    for sp in range(2):
        for layer in range(LAYERS):
            for buf in (s0, s1):
                for t in (0, CT + 1):
                    for rb in range(2):
                        buf[sp, layer, pl.ds(t * TILE + FIRST + 8 * rb, 8), :] = zero
            for row in (FIRST - 1, FIRST + 16):
                s0[sp, layer, pl.ds(TILE + row, CT, stride=TILE), :] = zero
    lane = lax.broadcasted_iota(jnp.int32, (8, 128), 1)

    def in_groups(step):
        def group(g, carry):
            for q in range(GROUP):
                step(g * GROUP + q, carry)
            return carry

        lax.fori_loop(0, CT // GROUP, group, 0)

    def start_of(ct, rb):
        return pl.multiple_of((ct + 1) * TILE + FIRST + 8 * rb, 8)

    def centre(buf, sp, layer, ct, rb):
        return buf[sp, layer, pl.ds(start_of(ct, rb), 8), :]

    def around(buf, sp, layer, ct, rb):
        here = centre(buf, sp, layer, ct, rb)
        left = centre(buf, sp, layer, ct - 1, rb)
        right = centre(buf, sp, layer, ct + 1, rb)
        total = pltpu.roll(jnp.where(lane == 127, left, here), 1, 1)
        total += pltpu.roll(jnp.where(lane == 0, right, here), 127, 1)
        base = start_of(ct, rb)
        total += buf[sp, layer, pl.ds(base - 1, 8), :]
        total += buf[sp, layer, pl.ds(base + 1, 8), :]
        return here, total

    def native(ref, layer, ct, rb):
        return ref[layer, pl.ds(8 * rb, 8), pl.ds(pl.multiple_of(ct * 128, 128), 128)]

    def react(s, c, around_s, around_c, layer, ct, rb):
        feed = native(fv, layer, ct, rb)
        kill = native(kv, layer, ct, rb)
        feed = feed + feed
        reaction = s * c * c
        reaction = reaction + reaction
        new_s = COEF[0] * around_s + (feed + s * (0.04 - feed)) - reaction
        new_c = COEF[1] * around_c + c * (0.52 - feed - (kill + kill)) + reaction
        return new_s, new_c

    def first(layers):
        def body(ct, carry):
            for layer in layers:
                for rb in range(2):
                    values = []
                    for sp in range(2):
                        here, total = around(s0, sp, layer, ct, rb)
                        if layer > 0:
                            total += centre(s0, sp, layer - 1, ct, rb)
                        if layer < LAYERS - 1:
                            total += centre(s0, sp, layer + 1, ct, rb)
                        values.append((here, total))
                    result = react(values[0][0], values[1][0], values[0][1], values[1][1], layer, ct, rb)
                    for sp in range(2):
                        s1[sp, layer, pl.ds(start_of(ct, rb), 8), :] = result[sp]
                        for side, edge, target in ((0, LAYERS - 1, up), (1, 0, down)):
                            if layer == edge:
                                place = (ct - (target >> 3) + (Y - 2)) & (Y - 1)
                                rows = pl.multiple_of((place & (HALF - 1)) * 16 + 8 * rb, 8)
                                ps[side, place >> 2, sp, pl.ds(rows, 8), :] = result[sp]
            return carry

        in_groups(body)

    early = (z > 0) & (collects | ((x == 0) & (core == 0) & (y > 0)) | ((x == X - 1) & (core == 1) & (y < Y // 2)))
    later = jnp.logical_not(early)

    def fields_loaded():
        with mark("w_load"):
            whole = s0.at[:, :, pl.ds(0, CT * 16), :]
            pltpu.make_async_copy(whole, whole, load_sem.at[0]).wait()

    def rates_loaded():
        with mark("w_loadfk"):
            f_load.wait()
            k_load.wait()


    @pl.when(early)
    def _():
        fields_loaded()
        rates_loaded()
        first((0, LAYERS - 1))
        first(range(1, LAYERS - 1))

    with mark("w_barrier"):
        pl.semaphore_wait(barrier, sum(jnp.where(has[flag], 1, 0) for flag in ("lo", "hi", "zlo", "above_lo", "above_hi")) + jnp.where(collects, DEPTHS - 1, 0))

    @pl.when(has["zlo"])
    def _():
        signal(ready, d, zdown)

    def tell():
        def one(i, carry):
            signal(everyone, 2 * ((chip + i) & (CHIPS - 1)) + core, z)
            return carry

        lax.fori_loop(1, CHIPS, one, 0)

    @pl.when(collects & (z == 0))
    def _():
        tell()

    clear = jnp.where(lax.broadcasted_iota(jnp.int32, (8, 128), 1) < 96, 0.0, 1.0)
    for away in range(Y):
        for across in range(X):
            if (away, across) not in DIRECT:
                xr[CHIPS + ((y - away) & (Y - 1)) * X + ((x - across) & (X - 1))] = clear
    for side, flag in ((0, "lo"), (1, "hi")):
        @pl.when(jnp.logical_not(has[flag]))
        def _(side=side):
            for sp in range(2):
                eg[side, 0, sp] = zero
                dg[side, 1, sp] = zero

                def fill(i, carry):
                    h0[side, sp, :, pl.ds(i * 128, 128)] = jnp.zeros((16, 128), jnp.float32)
                    ph[side, i // HALF, sp, pl.ds((i % HALF) * 16, 16), :] = jnp.zeros((16, 128), jnp.float32)
                    return carry

                lax.fori_loop(0, CT, fill, 0)
    for side, flag in ((0, "zlo"), (1, "zhi")):
        @pl.when(jnp.logical_not(has[flag]))
        def _(side=side):
            for sp in range(2):
                for layer in range(LAYERS):
                    r0[side, sp, layer] = zero
                    r1[side, sp, layer] = zero
                for depthside in range(2):
                    dg[depthside, side, sp] = zero

    def remote(src, dst, send, recv, depth, row):
        return pltpu.make_async_remote_copy(
            src_ref=src, dst_ref=dst, send_sem=send, recv_sem=recv,
            device_id=(depth, row), device_id_type=MESH)

    def depth_copy(kind, side, sp):
        target = up if side == 0 else down
        if kind == "h":
            src = (S, C)[sp].at[LAYERS - 1 if side == 0 else 0]
            return remote(src, h0.at[side, sp], sent, h_recv.at[side], target, z)
        if kind == "both":
            return remote(h0.at[side], h0.at[side], sent, h_recv.at[side], target, z)
        if kind == "halves":
            return remote(ps.at[side], ph.at[side], sent, p_recv.at[side, 0], target, z)
        if kind == "p":
            half = sp
            return remote(ps.at[side, half], ph.at[side, half], sent, p_recv.at[side, half], target, z)
        if kind == "straight":
            return remote(rs0.at[1, :, LAYERS - 1 if side == 0 else 0], dg.at[side, 1],
                          sent, s_recv.at[side], target, zdown)
        return remote(rs0.at[0:1, :, LAYERS - 1 if side == 0 else 0], eg.at[side],
                      sent, e_recv.at[side], target, z)

    def row_copy(kind, side):
        target = zup if side == 0 else zdown
        if kind == "0":
            return remote(rs0.at[side], r0.at[side], sent, r0_recv.at[side], d, target)
        if kind == "corner":
            return remote(eg.at[:, 0], dg.at[:, 0], sent, g_recv, d, target)
        return remote(rs1.at[side], r1.at[side], sent, r1_recv.at[side], d, target)

    to = ("hi", "lo")
    source = ("lo", "hi")
    zto = ("zhi", "zlo")
    zsource = ("zlo", "zhi")

    def each(flag, copies, what):
        @pl.when(has[flag])
        def _():
            for copy in copies:
                getattr(copy, what)()

    pl.when(later)(fields_loaded)
    for side in range(2):
        row = TILE + FIRST + (15 if side == 0 else 0)
        for sp in range(2):
            for layer in range(LAYERS):
                rs0[side, sp, layer] = s0[sp, layer, pl.ds(row, CT, stride=TILE), :]
    for side in range(2):
        each("above_" + to[side], [depth_copy("straight", side, 0)], "start")
    for side in range(2):
        each(to[side], [depth_copy("edge", side, 0)] + [depth_copy("h", side, sp) for sp in range(2)], "start")
    each("zlo", [row_copy("0", 1)], "start")

    @pl.when(collects & (z > 0))
    def _():
        tell()

    @pl.when(later)
    def _():
        rates_loaded()
        first((0, LAYERS - 1))

    for side in range(2):
        each(to[side], [depth_copy("p", side, half) for half in range(2)], "start")
    @pl.when(later)
    def _():
        first(range(1, LAYERS - 1))

    for side in range(2):
        row = TILE + FIRST + (15 if side == 0 else 0)
        for sp in range(2):
            for layer in range(LAYERS):
                rs1[side, sp, layer] = s1[sp, layer, pl.ds(row, CT, stride=TILE), :]
    each("zlo", [row_copy("1", 1)], "start")
    with mark("w_readyz"):
        @pl.when(has["zhi"])
        def _():
            pl.semaphore_wait(ready, 1)
            for kind in ("0", "1"):
                row_copy(kind, 0).start()

    with mark("w_edge"):
        for side in range(2):
            each(source[side], [depth_copy("edge", side, 0)], "wait_recv")
    each("zhi", [row_copy("corner", 0)], "start")

    with mark("w_row0"):
        for side in range(2):
            each(zsource[side], [row_copy("0", side)], "wait_recv")

    scale = {flag: jnp.where(has[flag], 1.0, 0.0).astype(jnp.float32) for flag in source + zsource}
    for side in range(2):
        row = TILE + FIRST + (0 if side == 0 else 15)
        for sp in range(2):
            for layer in range(LAYERS):
                where = pl.ds(row, CT, stride=TILE)
                s1[sp, layer, where, :] = s1[sp, layer, where, :] + COEF[sp] * r0[side, sp, layer]
    with mark("w_row1"):
        for side in range(2):
            each(zsource[side], [row_copy("1", side)], "wait_recv")
    for side in range(2):
        edge = TILE + FIRST + (0 if side == 0 else 15)
        outside = TILE + FIRST + (-1 if side == 0 else 16)
        for sp in range(2):
            factor = COEF[sp] * scale[zsource[side]]
            for layer in range(LAYERS):
                s1[sp, layer, pl.ds(outside, CT, stride=TILE), :] = (
                    r1[side, sp, layer] + factor * s0[sp, layer, pl.ds(edge, CT, stride=TILE), :])

    with mark("w_h"):
        for side in range(2):
            each(source[side], [depth_copy("both", side, 0)], "wait_recv")

    def add_layers(ct, carry):
        for side, layer in ((0, 0), (1, LAYERS - 1)):
            for sp in range(2):
                for rb in range(2):
                    where = pl.ds(start_of(ct, rb), 8)
                    halo = h0[side, sp, pl.ds(8 * rb, 8), pl.ds(pl.multiple_of(ct * 128, 128), 128)]
                    s1[sp, layer, where, :] = s1[sp, layer, where, :] + COEF[sp] * halo
        return carry

    with mark("addlayers"):
        in_groups(add_layers)

    e_load.wait()
    pal_load.wait()
    weights = []
    for k in range(3):
        a, b = -8.0 * pal[k, 0], -8.0 * pal[k, 1]
        weights.append((a, b, -pal[k, 2] - 0.65 * a - 0.25 * b))

    def columns_of(ct):
        return pl.ds(pl.multiple_of(ct * 128, 128), 128)

    def second(layer, ct, rb):
        values = []
        for sp in range(2):
            here, total = around(s1, sp, layer, ct, rb)
            if layer > 0:
                total += centre(s1, sp, layer - 1, ct, rb)
            else:
                total += (COEF[sp] * scale["lo"]) * centre(s0, sp, 0, ct, rb)
            if layer < LAYERS - 1:
                total += centre(s1, sp, layer + 1, ct, rb)
            else:
                total += (COEF[sp] * scale["hi"]) * centre(s0, sp, LAYERS - 1, ct, rb)
            values.append((here, total))
        return react(values[0][0], values[1][0], values[0][1], values[1][1], layer, ct, rb)

    def shade(s, c, layer, ct, rb):
        new[0, layer, pl.ds(8 * rb, 8), columns_of(ct)] = s
        new[1, layer, pl.ds(8 * rb, 8), columns_of(ct)] = c
        passing = jnp.exp(-native(ev, layer, ct, rb) * (0.25 + 4.0 * c * c))
        opacity = 1.0 - passing
        colors = [opacity / (1.0 + jnp.exp(a * s + b * c + e)) for a, b, e in weights]
        return colors, passing

    def middle(ct, carry):
        for rb in range(2):
            rows = pl.ds(pl.multiple_of(ct * 16 + 8 * rb, 8), 8)
            near, light = shade(*second(1, ct, rb), 1, ct, rb)
            far, light_far = shade(*second(2, ct, rb), 2, ct, rb)
            for k in range(3):
                mid[k, rows, :] = near[k] + light * far[k]
            mid[3, rows, :] = light * light_far
        return carry

    with mark("middle"):
        in_groups(middle)

    def open_ends(ct, carry):
        for layer in (0, LAYERS - 1):
            for rb in range(2):
                for sp, value in enumerate(second(layer, ct, rb)):
                    new[sp, layer, pl.ds(8 * rb, 8), columns_of(ct)] = value
        return carry

    with mark("open_ends"):
        in_groups(open_ends)

    with mark("w_diag"):
        for side in range(2):
            each("below_" + source[side], [depth_copy("straight", side, 0)], "wait_recv")
        each("zlo", [row_copy("corner", 0)], "wait_recv")
    corner = {}
    for side in range(2):
        for rowside in range(2):
            for sp in range(2):
                corner[side, rowside, sp] = pltpu.roll(dg[side, rowside, sp], (Y - 2 - y) & (Y - 1), 0) * (2.0 * COEF[sp])

    def add_corners(half):
        for (side, rowside, sp), rows in corner.items():
            where = pl.ds(15 * rowside, HALF, stride=16)
            ph[side, half, sp, where, :] = ph[side, half, sp, where, :] + rows[half * HALF:half * HALF + HALF]

    partner = d + 1 - 2 * core

    def core_copy(g):
        some = pl.ds(g * HALF * X, HALF * X)
        return remote(t0.at[1 - core, some], cr.at[some], sent, c_recv.at[g], partner, z)

    def ends(g):
        with mark(f"w_p{g}"):
            for side in range(2):
                each(source[side], [depth_copy("p", side, g)], "wait_recv")
        add_corners(g)
        for q in range(HALF):
            place = g * HALF + q
            ct = (y + place + 2) & (Y - 1)
            for rb in range(2):
                parts = []
                for side, layer in ((0, 0), (1, LAYERS - 1)):
                    values = [new[sp, layer, pl.ds(8 * rb, 8), columns_of(ct)]
                              + COEF[sp] * ph[side, g, sp, pl.ds(q * 16 + 8 * rb, 8), :] for sp in range(2)]
                    parts.append(shade(*values, layer, ct, rb))
                (near, light), (far, light_far) = parts
                rows = pl.ds(pl.multiple_of(ct * 16 + 8 * rb, 8), 8)
                light_mid = light * mid[3, rows, :]
                for k in range(3):
                    flat[place * 8 + 2 * k + rb] = near[k] + light * mid[k, rows, :] + light_mid * far[k]
                flat[place * 8 + 6 + rb] = light_mid * light_far
        for place in range(g * HALF, g * HALF + HALF):
            for j, tile in enumerate(regroup([flat[place * 8 + i] for i in range(8)], lane)):
                t0[j % 2, place * X + j // 2] = tile
        core_copy(g).start()
        for away, across in DIRECT:
            place = (away - 2) % Y
            if place // HALF == g:
                yy, xx = (y + away) & (Y - 1), (x + across) & (X - 1)
                for c in range(2):
                    remote(t0.at[c, place * X + xx], xr.at[CHIPS * core + chip], sent, x_recv, at(yy, xx, c), z).start()

    with mark("w_everyone"):
        @pl.when(jnp.logical_not(collects))
        def _():
            pl.semaphore_wait(everyone, 1)

    for g in range(2):
        with mark(f"ends{g}"):
            ends(g)

    def chip_copy(place, away, across):
        xx = (x + across) & (X - 1)
        return remote(x0.at[place * X + xx], xr.at[chip], sent, x_recv, at((y + away) & (Y - 1), xx, core), z)

    def merge(g):
        core_copy(g).wait_recv()
        for i in range(g * HALF * X, (g + 1) * HALF * X):
            mine, other = t0[core, i], cr[i]
            x0[i] = joined(jnp.where(core == 0, mine, other), jnp.where(core == 0, other, mine), lane)
        for away in ((4, 3, 5, 2), (6, 1, 7, 0))[g]:
            for across in (2, 1, 3, 0):
                if (away or across) and (away, across) not in DIRECT:
                    chip_copy((away - 2) % Y, away, across).start()

    for g in range(2):
        with mark(f"merge{g}"):
            merge(g)
    for side in range(2):
        each(to[side], [depth_copy(kind, side, 0) for kind in ("edge", "both", "halves")], "wait_send")
        each("above_" + to[side], [depth_copy("straight", side, 0)], "wait_send")
        each(zto[side], [row_copy(kind, side) for kind in ("0", "1")], "wait_send")
    each("zhi", [row_copy("corner", 0)], "wait_send")
    for g in range(2):
        core_copy(g).wait_send()
    xr[chip] = x0[(Y - 2) * X + x]
    arrived = xr.at[pl.ds(0, TILES)]
    with mark("w_xy"):
        pltpu.make_async_copy(arrived, arrived, x_recv).wait()
    pltpu.make_async_copy(arrived, arrived, sent).wait()


def finish(new, xr, out_s, out_c, out_image, img, out_sem):
    copies = [pltpu.make_async_copy(new.at[0], out_s, out_sem.at[0]),
              pltpu.make_async_copy(new.at[1], out_c, out_sem.at[1])]
    for copy in copies:
        copy.start()
    last = pltpu.make_async_copy(img, out_image, out_sem.at[2])

    def compose(once, carry):
        lane = lax.broadcasted_iota(jnp.int32, (8, 128), 1)
        pieces = []
        for first in range(0, CHIPS, HALF):
            total, light = None, None
            for i in range(first, first + HALF):
                for c in range(2):
                    tile = xr[c * CHIPS + i]
                    color = jnp.where(lane < 96, tile, 0.0)
                    passing = expand(tile, lane)
                    total = color if total is None else total + light * color
                    light = passing if light is None else light * passing
            pieces.append((total, light))
        while len(pieces) > 1:
            pieces = [(near + light * far, light * light_far)
                      for (near, light), (far, light_far) in zip(pieces[::2], pieces[1::2])]
        total, light = pieces[0]
        tile = jnp.where(lane < 96, total, 1.0 - light)
        for g in range(8):
            part = tile if g == 0 else pltpu.roll(tile, 128 - 16 * g, 1)
            img[g // 2, pl.ds(8 * (g % 2), 8), :] = part[:, :16]
        last.start()
        return carry

    lax.fori_loop(0, 1 + (lax.axis_index("depth") >> 6), compose, 0)
    for copy in copies + [last]:
        copy.wait()


def body(substrate, catalyst, feed_rate, kill_rate, extinction, palette):
    field = jax.ShapeDtypeStruct(substrate.shape, jnp.float32)
    any_ref = pl.BlockSpec(memory_space=pl.ANY)
    f32 = jnp.float32
    dma = pltpu.SemaphoreType.DMA
    new, parts = pl.pallas_call(
        kernel,
        out_shape=(pltpu.VMEM((2,) + field.shape, f32), pltpu.VMEM((2 * CHIPS, 8, 128), f32)),
        in_specs=[any_ref] * 6,
        out_specs=(pl.BlockSpec(memory_space=pltpu.VMEM),) * 2,
        scratch_shapes=[
            pltpu.VMEM((2, LAYERS, (CT + 2) * TILE, 128), f32),
            pltpu.VMEM((2, LAYERS, (CT + 2) * TILE, 128), f32),
            pltpu.VMEM((LAYERS, 16, CT * 128), f32),
            pltpu.VMEM((LAYERS, 16, CT * 128), f32),
            pltpu.VMEM((LAYERS, 16, CT * 128), f32),
            pltpu.VMEM((2, 2, 16, CT * 128), f32),
            pltpu.VMEM((3, 2, 2, HALF * 16, 128), f32),
            pltpu.VMEM((2, 2, 2, HALF * 16, 128), f32),
            pltpu.VMEM((2, 2, LAYERS, CT, 128), f32),
            pltpu.VMEM((2, 2, LAYERS, CT, 128), f32),
            pltpu.VMEM((2, 2, LAYERS, CT, 128), f32),
            pltpu.VMEM((2, 2, LAYERS, CT, 128), f32),
            pltpu.VMEM((2, 1, 2, CT, 128), f32),
            pltpu.VMEM((2, 2, 2, CT, 128), f32),
            pltpu.VMEM((4, CT * 16, 128), f32),
            pltpu.VMEM((CT * 8, 8, 128), f32),
            pltpu.VMEM((2, CHIPS, 8, 128), f32),
            pltpu.VMEM((CHIPS, 8, 128), f32),
            pltpu.VMEM((CHIPS, 8, 128), f32),
            pltpu.SMEM((3, 3), f32),
            dma((5,)),
            dma, dma((2,)), dma((2, 2)),
            dma((2,)), dma((2,)),
            dma((2,)), dma, dma((2,)),
            dma((2,)), dma,
            pltpu.SemaphoreType.REGULAR, pltpu.SemaphoreType.REGULAR,
        ],
        compiler_params=pltpu.CompilerParams(collective_id=0, has_side_effects=True),
    )(palette, substrate, catalyst, feed_rate, kill_rate, extinction)
    return pl.pallas_call(
        finish,
        out_shape=(field, field, jax.ShapeDtypeStruct((4, 16, 16), f32)),
        in_specs=[pl.BlockSpec(memory_space=pltpu.VMEM)] * 2,
        out_specs=(any_ref,) * 3,
        scratch_shapes=[pltpu.VMEM((4, 16, 16), f32), dma((3,))],
    )(*(pltpu.with_memory_space_constraint(part, pltpu.VMEM) for part in (new, parts)))


def solution(mesh):
    split = P("depth", "rows", None)
    return jax.shard_map(
        body,
        mesh=mesh,
        in_specs=(split,) * 5 + (P(),),
        out_specs=(split, split, P(None, "rows", "depth")),
        check_vma=False,
    )
```
